256 devices in a mesh: lon: 32 (over z_hi, y, core), lat: 8 (over x, z_lo).
Axes of the slice: x: 4, y: 4, z: 8 (z_hi: 4, z_lo: 2; z = z_hi * 2 + z_lo), core: 2. Of those that a mesh axis runs over, the one named last changes fastest.
Arguments:
- temp: float32 [16, 1024, 4096], P(None, 'lat', 'lon'), may hold values from -6 to 6
- salt: float32 [16, 1024, 4096], P(None, 'lat', 'lon'), may hold values from -6 to 6
- uvel: float32 [16, 1024, 4096], P(None, 'lat', 'lon'), may hold values from -6 to 6
- vvel: float32 [16, 1024, 4096], P(None, 'lat', 'lon'), may hold values from -6 to 6
- depth_levels: int32 [1024, 4096], P('lat', 'lon'), may hold values from 0 to 16
Outputs:
- temp_next: float32 [16, 1024, 4096], P(None, 'lat', 'lon')
- salt_next: float32 [16, 1024, 4096], P(None, 'lat', 'lon')
- uvel_next: float32 [16, 1024, 4096], P(None, 'lat', 'lon')
- vvel_next: float32 [16, 1024, 4096], P(None, 'lat', 'lon')
The draws below stay inside these ranges and needn't reach their ends.
Inputs may be any that keep to these rules, and one draw needn't show every extreme that they name: `depth_levels`: wet levels are counted from the top.
All inputs are finite; a program needn't handle non-finite values.
Results may differ from the reference program's by a relative error of at most 0.0003.
Values sent between devices are 32-bit elements; how exact they have to be, the bound alone decides.
A program may use at most 128 MiB of HBM per device.

```python
import math
import jax
import jax.numpy as jnp
from jax import lax

K = 16
NI = 4096
NJ = 1024


def with_ends(entries, key, least, largest):
    place = [jax.random.randint(jax.random.fold_in(key, axis), (), 0, length) for axis, length in enumerate(entries.shape)]
    main_axis = entries.shape.index(max(entries.shape))
    next_to = place[:main_axis] + [(place[main_axis] + 1) % entries.shape[main_axis]] + place[main_axis + 1:]
    return entries.at[tuple(place)].set(least).at[tuple(next_to)].set(largest)


def steps_of(rng, dims, pieces, smallest, high):
    def one(axis_at, shards_of):
        draws = jax.random.uniform(jax.random.fold_in(jax.random.fold_in(rng, 6), axis_at), (shards_of,), jnp.float32, smallest / len(pieces), high / len(pieces))
        return jnp.repeat(jnp.exp(draws), dims[axis_at] // shards_of).reshape((-1,) + (1,) * (len(dims) - axis_at - 1))

    factor_of = one(*pieces[0])
    for cut in pieces[1:]:
        factor_of = factor_of * one(*cut)
    return factor_of


def normal_values(rng, extent, scale, most, cuts=(), kind=jnp.bfloat16):
    array = scale * jax.random.normal(rng, extent, jnp.float32)
    if cuts:
        array = array * steps_of(rng, extent, cuts, -0.22, 0.18)
    return jnp.clip(array, -most, most).astype(kind)


def setup_inputs(seed: int = 0) -> dict:
    keys = jax.random.split(jax.random.key(seed), 6)
    return {
        "temp": normal_values(keys[0], (K, NJ, NI), 1.0, 6.0, ((1, 8), (2, 32)), jnp.float32),
        "salt": normal_values(keys[1], (K, NJ, NI), 1.0, 6.0, ((1, 8), (2, 32)), jnp.float32),
        "uvel": normal_values(keys[2], (K, NJ, NI), 1.0, 6.0, ((1, 8), (2, 32)), jnp.float32),
        "vvel": normal_values(keys[3], (K, NJ, NI), 1.0, 6.0, ((1, 8), (2, 32)), jnp.float32),
        "depth_levels": with_ends(jax.random.randint(keys[4], (NJ, NI), 0, K + 1), jax.random.fold_in(keys[4], 1), 0, K).astype(jnp.int32),
    }


time_step = 0.2
biharmonic = 0.01


def extend_level(field, sign):
    north = sign * field[::-1, ::-1][:2]
    south = jnp.zeros((2, field.shape[1]), field.dtype)
    rows = jnp.concatenate([south, field, north], 0)
    return jnp.concatenate([rows[:, -2:], rows, rows[:, :2]], 1)


def laplace(grid):
    return (grid[..., 2:, 1:-1] + grid[..., :-2, 1:-1] + grid[..., 1:-1, 2:]
            + grid[..., 1:-1, :-2] - 4.0 * grid[..., 1:-1, 1:-1])


def advance(extended, pres, wet, coriolis):
    centre = extended[..., 2:-2, 2:-2]
    east = extended[..., 2:-2, 3:-1]
    west = extended[..., 2:-2, 1:-3]
    north = extended[..., 3:-1, 2:-2]
    south = extended[..., 1:-3, 2:-2]
    first = centre[2]
    second = centre[3]
    carried = 0.5 * (first * (east - west) + second * (north - south))
    smooth = laplace(laplace(extended))
    grad_x = 0.5 * (pres[..., 2:-2, 3:-1] - pres[..., 2:-2, 1:-3])
    grad_y = 0.5 * (pres[..., 3:-1, 2:-2] - pres[..., 1:-3, 2:-2])
    temp_new = centre[0] - time_step * carried[0] - biharmonic * smooth[0]
    salt_new = centre[1] - time_step * carried[1] - biharmonic * smooth[1]
    first_new = first + time_step * (coriolis * second - grad_x - carried[2]) - biharmonic * smooth[2]
    second_new = second + time_step * (-coriolis * first - grad_y - carried[3]) - biharmonic * smooth[3]
    return jnp.stack([temp_new, salt_new, first_new, second_new]) * wet


def reference(temp, salt, uvel, vvel, depth_levels):
    rows = jnp.arange(NJ).astype(temp.dtype)
    coriolis = (0.5 * jnp.sin(math.pi * (rows + 0.5) / NJ - 0.5 * math.pi))[:, None]
    signs = (1.0, 1.0, -1.0, -1.0)

    def level(total, inputs):
        fields, index = inputs
        wet = jnp.where(depth_levels > index, 1.0, 0.0).astype(temp.dtype)
        masked = fields * wet
        extended = jnp.stack([extend_level(masked[n], signs[n]) for n in range(4)])
        density = -0.2 * extended[0] + 0.8 * extended[1]
        total = total + density
        pres = total - 0.5 * density
        return total, advance(extended, pres, wet, coriolis)

    stacked = jnp.stack([temp, salt, uvel, vvel], 1)
    start = jnp.zeros((NJ + 4, NI + 4), temp.dtype)
    _, result = lax.scan(level, start, (stacked, jnp.arange(K, dtype=jnp.int32)))
    return result[:, 0], result[:, 1], result[:, 2], result[:, 3]
```

```python
import math

import jax
import jax.numpy as jnp
from jax import lax
from jax.experimental import pallas as pl
from jax.experimental.pallas import tpu as pltpu
from jax.sharding import PartitionSpec as P

time_step = 0.2
biharmonic = 0.01
signs = (1.0, 1.0, -1.0, -1.0)
top = 8


def step_kernel(t_ref, s_ref, u_ref, v_ref, d_ref, f_ref, rs_ref, rn_ref, cw_ref, ce_ref,
                to_ref, so_ref, uo_ref, vo_ref,
                base, vp1, vm1, vp2, vm2, accx, accy):
    k = pl.program_id(0)
    frame, width = base.shape[1], base.shape[2]
    rows = t_ref.shape[1]

    @pl.when(k == 0)
    def _():
        base[...] = jnp.zeros_like(base)
        accx[...] = jnp.zeros_like(accx)
        accy[...] = jnp.zeros_like(accy)

    wet = jnp.where(d_ref[...] > k, 1.0, 0.0).astype(jnp.float32)
    lane = lax.broadcasted_iota(jnp.int32, (frame, width), 1)
    ins = (t_ref, s_ref, u_ref, v_ref)
    for n in range(4):
        base[n, top:top + rows, :] = ins[n][0] * wet
        base[n, top - 2:top, :] = rs_ref[n, 0]
        base[n, top + rows:top + rows + 2, :] = rn_ref[n, 0]
        whole = base[n]
        ce = ce_ref[n, 0]
        cw = cw_ref[n, 0]
        e0 = jnp.broadcast_to(ce[:, 0:1], (frame, width))
        e1 = jnp.broadcast_to(ce[:, 1:2], (frame, width))
        w0 = jnp.broadcast_to(cw[:, 0:1], (frame, width))
        w1 = jnp.broadcast_to(cw[:, 1:2], (frame, width))
        vp1[n] = jnp.where(lane == width - 1, e0, pltpu.roll(whole, width - 1, 1))
        vm1[n] = jnp.where(lane == 0, w1, pltpu.roll(whole, 1, 1))
        vp2[n] = jnp.where(lane == width - 2, e0,
                           jnp.where(lane == width - 1, e1, pltpu.roll(whole, width - 2, 1)))
        vm2[n] = jnp.where(lane == 0, w0, jnp.where(lane == 1, w1, pltpu.roll(whole, 2, 1)))

    def at(ref, n, d):
        return ref[n, top + d:top + d + rows, :]

    centre = [at(base, n, 0) for n in range(4)]
    first, second = centre[2], centre[3]
    parts = []
    for n in range(4):
        east, west = at(vp1, n, 0), at(vm1, n, 0)
        north, south = at(base, n, 1), at(base, n, -1)
        carried = 0.5 * (first * (east - west) + second * (north - south))
        smooth = (
            20.0 * centre[n]
            - 8.0 * (east + west + north + south)
            + 2.0 * (at(vp1, n, 1) + at(vp1, n, -1) + at(vm1, n, 1) + at(vm1, n, -1))
            + at(base, n, 2) + at(base, n, -2) + at(vp2, n, 0) + at(vm2, n, 0)
        )
        parts.append((east, west, north, south, carried, smooth))

    def density(a, b):
        return -0.2 * a + 0.8 * b

    dx = density(parts[0][0], parts[1][0]) - density(parts[0][1], parts[1][1])
    dy = density(parts[0][2], parts[1][2]) - density(parts[0][3], parts[1][3])
    totx = accx[...] + dx
    toty = accy[...] + dy
    accx[...] = totx
    accy[...] = toty
    grad_x = 0.5 * (totx - 0.5 * dx)
    grad_y = 0.5 * (toty - 0.5 * dy)
    coriolis = f_ref[...]
    to_ref[0] = (centre[0] - time_step * parts[0][4] - biharmonic * parts[0][5]) * wet
    so_ref[0] = (centre[1] - time_step * parts[1][4] - biharmonic * parts[1][5]) * wet
    uo_ref[0] = (
        first + time_step * (coriolis * second - grad_x - parts[2][4]) - biharmonic * parts[2][5]
    ) * wet
    vo_ref[0] = (
        second + time_step * (-coriolis * first - grad_y - parts[3][4]) - biharmonic * parts[3][5]
    ) * wet


def shards(temp, salt, uvel, vvel, depth_levels):
    levels, rows_dev, cols_dev = temp.shape
    nlat = lax.axis_size("lat")
    nlon = lax.axis_size("lon")
    at_lat = lax.axis_index("lat")
    fields = (temp, salt, uvel, vvel)
    level_index = jnp.arange(levels, dtype=jnp.int32)[:, None, None]

    def masked_rows(lo, hi):
        wet = jnp.where(depth_levels[None, lo:hi, :] > level_index, 1.0, 0.0).astype(jnp.float32)
        return jnp.stack([x[:, lo:hi, :] * wet for x in fields])

    def masked_cols(lo, hi):
        wet = jnp.where(depth_levels[None, :, lo:hi] > level_index, 1.0, 0.0).astype(jnp.float32)
        return jnp.stack([x[:, :, lo:hi] * wet for x in fields])

    head = masked_rows(0, 2)
    tail = masked_rows(rows_dev - 2, rows_dev)
    south = lax.ppermute(tail, "lat", [(i, i + 1) for i in range(nlat - 1)])
    north = lax.ppermute(head, "lat", [(i + 1, i) for i in range(nlat - 1)])
    sign = jnp.array(signs, jnp.float32)[:, None, None, None]
    piece = tail[:, :, ::-1, ::-1] * sign
    last = nlat - 1
    fold = lax.ppermute(
        piece, ("lon", "lat"), [(i * nlat + last, (nlon - 1 - i) * nlat + last) for i in range(nlon)]
    )
    north = north + fold

    pad = top - 2
    frame = rows_dev + 2 * top

    def strip(lo, hi):
        zeros = jnp.zeros((4, levels, pad, hi - lo), jnp.float32)
        return jnp.concatenate(
            [zeros, south[..., lo:hi], masked_cols(lo, hi), north[..., lo:hi], zeros], axis=2
        )

    west = lax.ppermute(
        strip(cols_dev - 2, cols_dev), "lon", [(i, (i + 1) % nlon) for i in range(nlon)]
    )
    east = lax.ppermute(strip(0, 2), "lon", [((i + 1) % nlon, i) for i in range(nlon)])

    total_rows = rows_dev * nlat
    global_rows = (at_lat * rows_dev + jnp.arange(rows_dev, dtype=jnp.int32)).astype(jnp.float32)
    coriolis = (0.5 * jnp.sin(math.pi * (global_rows + 0.5) / total_rows - 0.5 * math.pi))[:, None]
    coriolis = jnp.broadcast_to(coriolis, (rows_dev, cols_dev))

    level_block = pl.BlockSpec((1, rows_dev, cols_dev), lambda k: (k, 0, 0))
    plane = pl.BlockSpec((rows_dev, cols_dev), lambda k: (0, 0))
    row_halo = pl.BlockSpec((4, 1, 2, cols_dev), lambda k: (0, k, 0, 0))
    col_halo = pl.BlockSpec((4, 1, frame, 2), lambda k: (0, k, 0, 0))
    out = pl.pallas_call(
        step_kernel,
        grid=(levels,),
        in_specs=[level_block] * 4 + [plane] * 2 + [row_halo] * 2 + [col_halo] * 2,
        out_specs=[level_block] * 4,
        out_shape=[jax.ShapeDtypeStruct(temp.shape, jnp.float32)] * 4,
        scratch_shapes=[pltpu.VMEM((4, frame, cols_dev), jnp.float32)] * 5
        + [pltpu.VMEM((rows_dev, cols_dev), jnp.float32)] * 2,
        compiler_params=pltpu.CompilerParams(dimension_semantics=("arbitrary",)),
    )(temp, salt, uvel, vvel, depth_levels, coriolis, south, north, west, east)
    return tuple(out)


def solution(mesh):
    placed = (
        P(None, "lat", "lon"),
        P(None, "lat", "lon"),
        P(None, "lat", "lon"),
        P(None, "lat", "lon"),
        P("lat", "lon"),
    )
    return jax.shard_map(
        shards,
        mesh=mesh,
        in_specs=placed,
        out_specs=(
            P(None, "lat", "lon"),
            P(None, "lat", "lon"),
            P(None, "lat", "lon"),
            P(None, "lat", "lon"),
        ),
        check_vma=False,
    )
```

```python
import functools
import math

import jax
import jax.numpy as jnp
from jax import lax
from jax.experimental import pallas as pl
from jax.experimental.pallas import tpu as pltpu
from jax.sharding import PartitionSpec as P

time_step = 0.2
biharmonic = 0.01
signs = (1.0, 1.0, -1.0, -1.0)
top = 8


def when(cond, fn):
    if cond is True:
        fn()
    else:
        pl.when(cond)(fn)


def reverse_lanes(x):
    lane = lax.broadcasted_iota(jnp.int32, x.shape, 1)
    width = x.shape[1]
    bit = 1
    while bit < width:
        x = jnp.where((lane & bit) != 0, pltpu.roll(x, bit, 1), pltpu.roll(x, width - bit, 1))
        bit *= 2
    return x


def exchange_kernel(axes, nlat, nlon, t_ref, s_ref, u_ref, v_ref, d_ref,
                    hs_o, hn_o, hw_o, he_o, cor_o,
                    top_b, bot_b, fold_b, lft_b, rgt_b, hs, hn, hw, he, cor,
                    send_sem, recv_sem, local_sem):
    a = lax.axis_index("lat")
    b = lax.axis_index("lon")
    last = nlat - 1
    levels, rows, cols = t_ref.shape
    left = (b + nlon - 1) % nlon
    right = (b + 1) % nlon
    mirror = nlon - 1 - b
    ne = (2 * nlon - 2 - b) % nlon
    nw = (nlon - b) % nlon
    fold = a == last

    def dev(la, lo):
        return tuple(la if ax == "lat" else lo for ax in axes)

    def zero_south():
        hs[...] = jnp.zeros_like(hs)
        cor[0] = jnp.zeros_like(cor[0])
        cor[1] = jnp.zeros_like(cor[1])

    when(a == 0, zero_south)

    partners = [
        (a < last, (a + 1, b)), (a > 0, (a - 1, b)), (True, (a, left)), (True, (a, right)),
        (a < last, (a + 1, right)), (a < last, (a + 1, left)),
        (a > 0, (a - 1, right)), (a > 0, (a - 1, left)),
        (fold, (last, mirror)), (fold & (ne != b), (last, ne)), (fold & (nw != b), (last, nw)),
    ]
    barrier = pltpu.get_barrier_semaphore()
    for cond, target in partners:
        when(cond, lambda target=target: pl.semaphore_signal(
            barrier, 1, device_id=dev(*target), device_id_type=pl.DeviceIdType.MESH))

    ins = (t_ref, s_ref, u_ref, v_ref)

    def body(k, carry):
        wet = jnp.where(d_ref[...] > k, 1.0, 0.0).astype(jnp.float32)
        for n, ref in enumerate(ins):
            x = ref[k] * wet
            top_b[n, k] = x[0:2]
            bot_b[n, k] = x[rows - 2:rows]
            flipped = reverse_lanes(x[rows - 8:rows])
            fold_b[n, k, 0:1] = signs[n] * flipped[7:8]
            fold_b[n, k, 1:2] = signs[n] * flipped[6:7]
            xt = jnp.transpose(x)
            lft_b[n, k] = xt[0:2]
            rgt_b[n, k] = xt[cols - 2:cols]
        return carry

    lax.fori_loop(0, levels, body, 0)

    below = (a + last) // (last + 1)
    above = (2 * last - a) // (last + 1)
    at_fold = a // last
    ne_apart = ((2 * b + 2) % nlon + nlon - 1) // nlon
    nw_apart = ((2 * b) % nlon + nlon - 1) // nlon
    peers = 2 + 3 * below + 3 * above + at_fold * (1 + ne_apart + nw_apart)
    pl.semaphore_wait(barrier, peers)

    relations = [
        (a < last, a > 0, bot_b, hs, (a + 1, b)),
        (a > 0, a < last, top_b, hn, (a - 1, b)),
        (fold, fold, fold_b, hn, (last, mirror)),
        (True, True, lft_b, he, (a, left)),
        (True, True, rgt_b, hw, (a, right)),
        (a < last, a > 0, rgt_b.at[:, :, 1:2], cor.at[0], (a + 1, right)),
        (a < last, a > 0, lft_b.at[:, :, 0:1], cor.at[1], (a + 1, left)),
        (a > 0, a < last, rgt_b.at[:, :, 1:2], cor.at[2], (a - 1, right)),
        (a > 0, a < last, lft_b.at[:, :, 0:1], cor.at[3], (a - 1, left)),
        (fold & (ne != b), fold & (ne != b), rgt_b.at[:, :, 1:2], cor.at[3], (last, ne)),
        (fold & (nw != b), fold & (nw != b), lft_b.at[:, :, 0:1], cor.at[2], (last, nw)),
    ]
    copies = []
    for idx, (send, recv, src, dst, target) in enumerate(relations):
        copy = pltpu.make_async_remote_copy(
            src_ref=src, dst_ref=dst, send_sem=send_sem.at[idx], recv_sem=recv_sem.at[idx],
            device_id=dev(*target), device_id_type=pl.DeviceIdType.MESH)
        copies.append((send, recv, copy))
        when(send, copy.start)
    own = [
        (fold & (ne == b), pltpu.make_async_copy(rgt_b.at[:, :, 1:2], cor.at[3], local_sem.at[0])),
        (fold & (nw == b), pltpu.make_async_copy(lft_b.at[:, :, 0:1], cor.at[2], local_sem.at[1])),
    ]
    for cond, copy in own:
        when(cond, copy.start)
    for send, recv, copy in copies:
        when(send, copy.wait_send)
        when(recv, copy.wait_recv)
    for cond, copy in own:
        when(cond, copy.wait)
    hs_o[...] = hs[...]
    hn_o[...] = hn[...]
    hw_o[...] = hw[...]
    he_o[...] = he[...]
    cor_o[...] = cor[...]


def step_kernel(nlat, t_ref, s_ref, u_ref, v_ref, d_ref, f_ref, hs_ref, hn_ref, hw_ref, he_ref,
                cor_ref, to_ref, so_ref, uo_ref, vo_ref,
                base, vp1, vm1, vp2, vm2, accx, accy, mt):
    k = pl.program_id(0)
    frame, width = base.shape[1], base.shape[2]
    rows = t_ref.shape[1]
    at_lat = lax.axis_index("lat")
    south = at_lat > 0
    fold = at_lat == nlat - 1

    @pl.when(k == 0)
    def _():
        base[...] = jnp.zeros_like(base)
        accx[...] = jnp.zeros_like(accx)
        accy[...] = jnp.zeros_like(accy)
        mt[...] = jnp.zeros_like(mt)

    for n in range(4):
        mt[8 * n:8 * n + 2] = he_ref[n, 0]
        mt[8 * n + 2:8 * n + 4] = hw_ref[n, 0]
        for c in range(4):
            mt[8 * n + 4 + c:8 * n + 5 + c] = cor_ref[c, n, 0]
    tt = jnp.transpose(mt[...])
    sub = lax.broadcasted_iota(jnp.int32, (top, 1), 0)
    zeros = jnp.zeros((top, 1), jnp.float32)

    wet = jnp.where(d_ref[...] > k, 1.0, 0.0).astype(jnp.float32)
    lane = lax.broadcasted_iota(jnp.int32, (frame, width), 1)
    ins = (t_ref, s_ref, u_ref, v_ref)
    for n in range(4):
        base[n, top:top + rows, :] = ins[n][0] * wet
        base[n, top - 2:top, :] = jnp.where(south, hs_ref[n, 0], 0.0)
        base[n, top + rows:top + rows + 2, :] = hn_ref[n, 0]
        whole = base[n]

        def col(r):
            return tt[:, 8 * n + r:8 * n + r + 1]

        def last_of(r):
            return tt[rows - 1:rows, 8 * n + r:8 * n + r + 1]

        def first_of(r):
            return tt[0:1, 8 * n + r:8 * n + r + 1]

        low_sw = jnp.where((sub == top - 1) & south, last_of(4), 0.0)
        low_se = jnp.where((sub == top - 1) & south, last_of(5), 0.0)
        nw_val = jnp.where(fold, signs[n] * last_of(6), first_of(6))
        ne_val = jnp.where(fold, signs[n] * last_of(7), first_of(7))
        high_nw = jnp.where(sub == 0, nw_val, 0.0)
        high_ne = jnp.where(sub == 0, ne_val, 0.0)
        e0 = jnp.broadcast_to(jnp.concatenate([low_se, col(0), high_ne], 0), (frame, width))
        e1 = jnp.broadcast_to(jnp.concatenate([zeros, col(1), zeros], 0), (frame, width))
        w0 = jnp.broadcast_to(jnp.concatenate([zeros, col(2), zeros], 0), (frame, width))
        w1 = jnp.broadcast_to(jnp.concatenate([low_sw, col(3), high_nw], 0), (frame, width))
        vp1[n] = jnp.where(lane == width - 1, e0, pltpu.roll(whole, width - 1, 1))
        vm1[n] = jnp.where(lane == 0, w1, pltpu.roll(whole, 1, 1))
        vp2[n] = jnp.where(lane == width - 2, e0,
                           jnp.where(lane == width - 1, e1, pltpu.roll(whole, width - 2, 1)))
        vm2[n] = jnp.where(lane == 0, w0, jnp.where(lane == 1, w1, pltpu.roll(whole, 2, 1)))

    def at(ref, n, d):
        return ref[n, top + d:top + d + rows, :]

    centre = [at(base, n, 0) for n in range(4)]
    first, second = centre[2], centre[3]
    parts = []
    for n in range(4):
        east, west = at(vp1, n, 0), at(vm1, n, 0)
        north, south_ = at(base, n, 1), at(base, n, -1)
        carried = 0.5 * (first * (east - west) + second * (north - south_))
        smooth = (
            20.0 * centre[n]
            - 8.0 * (east + west + north + south_)
            + 2.0 * (at(vp1, n, 1) + at(vp1, n, -1) + at(vm1, n, 1) + at(vm1, n, -1))
            + at(base, n, 2) + at(base, n, -2) + at(vp2, n, 0) + at(vm2, n, 0)
        )
        parts.append((east, west, north, south_, carried, smooth))

    def density(a, b):
        return -0.2 * a + 0.8 * b

    dx = density(parts[0][0], parts[1][0]) - density(parts[0][1], parts[1][1])
    dy = density(parts[0][2], parts[1][2]) - density(parts[0][3], parts[1][3])
    totx = accx[...] + dx
    toty = accy[...] + dy
    accx[...] = totx
    accy[...] = toty
    grad_x = 0.5 * (totx - 0.5 * dx)
    grad_y = 0.5 * (toty - 0.5 * dy)
    coriolis = f_ref[...]
    to_ref[0] = (centre[0] - time_step * parts[0][4] - biharmonic * parts[0][5]) * wet
    so_ref[0] = (centre[1] - time_step * parts[1][4] - biharmonic * parts[1][5]) * wet
    uo_ref[0] = (
        first + time_step * (coriolis * second - grad_x - parts[2][4]) - biharmonic * parts[2][5]
    ) * wet
    vo_ref[0] = (
        second + time_step * (-coriolis * first - grad_y - parts[3][4]) - biharmonic * parts[3][5]
    ) * wet


def shards(axes, temp, salt, uvel, vvel, depth_levels):
    levels, rows_dev, cols_dev = temp.shape
    nlat = lax.axis_size("lat")
    nlon = lax.axis_size("lon")
    at_lat = lax.axis_index("lat")
    f32 = jnp.float32
    vmem = pl.BlockSpec(memory_space=pltpu.VMEM)
    strip = jax.ShapeDtypeStruct((4, levels, 2, cols_dev), f32)
    corners = jax.ShapeDtypeStruct((4, 4, levels, 1, cols_dev), f32)
    hs, hn, hw, he, cor = pl.pallas_call(
        functools.partial(exchange_kernel, axes, nlat, nlon),
        out_shape=[strip] * 4 + [corners],
        in_specs=[vmem] * 5,
        out_specs=[vmem] * 5,
        scratch_shapes=[pltpu.VMEM(strip.shape, f32)] * 9
        + [pltpu.VMEM(corners.shape, f32)]
        + [pltpu.SemaphoreType.DMA((11,)), pltpu.SemaphoreType.DMA((11,)),
           pltpu.SemaphoreType.DMA((2,))],
        compiler_params=pltpu.CompilerParams(
            collective_id=0, has_side_effects=True, vmem_limit_bytes=48 * 1024 * 1024),
    )(temp, salt, uvel, vvel, depth_levels)

    total_rows = rows_dev * nlat
    global_rows = (at_lat * rows_dev + jnp.arange(rows_dev, dtype=jnp.int32)).astype(f32)
    coriolis = (0.5 * jnp.sin(math.pi * (global_rows + 0.5) / total_rows - 0.5 * math.pi))[:, None]
    coriolis = jnp.broadcast_to(coriolis, (rows_dev, cols_dev))

    frame = rows_dev + 2 * top
    level_block = pl.BlockSpec((1, rows_dev, cols_dev), lambda k: (k, 0, 0))
    plane = pl.BlockSpec((rows_dev, cols_dev), lambda k: (0, 0))
    halo = pl.BlockSpec((4, 1, 2, cols_dev), lambda k: (0, k, 0, 0))
    corner = pl.BlockSpec((4, 4, 1, 1, cols_dev), lambda k: (0, 0, k, 0, 0))
    out = pl.pallas_call(
        functools.partial(step_kernel, nlat),
        grid=(levels,),
        in_specs=[level_block] * 4 + [plane] * 2 + [halo] * 4 + [corner],
        out_specs=[level_block] * 4,
        out_shape=[jax.ShapeDtypeStruct(temp.shape, f32)] * 4,
        scratch_shapes=[pltpu.VMEM((4, frame, cols_dev), f32)] * 5
        + [pltpu.VMEM((rows_dev, cols_dev), f32)] * 2
        + [pltpu.VMEM((cols_dev, cols_dev), f32)],
        compiler_params=pltpu.CompilerParams(dimension_semantics=("arbitrary",)),
    )(temp, salt, uvel, vvel, depth_levels, coriolis, hs, hn, hw, he, cor)
    return tuple(out)


def solution(mesh):
    placed = (
        P(None, "lat", "lon"),
        P(None, "lat", "lon"),
        P(None, "lat", "lon"),
        P(None, "lat", "lon"),
        P("lat", "lon"),
    )
    return jax.shard_map(
        functools.partial(shards, tuple(mesh.axis_names)),
        mesh=mesh,
        in_specs=placed,
        out_specs=(
            P(None, "lat", "lon"),
            P(None, "lat", "lon"),
            P(None, "lat", "lon"),
            P(None, "lat", "lon"),
        ),
        check_vma=False,
    )
```

```python
import functools
import math

import jax
import jax.numpy as jnp
from jax import lax
from jax.experimental import pallas as pl
from jax.experimental.pallas import tpu as pltpu
from jax.sharding import PartitionSpec as P

time_step = 0.2
biharmonic = 0.01
signs = (1.0, 1.0, -1.0, -1.0)
top = 8


def when(cond, fn):
    if cond is True:
        fn()
    else:
        pl.when(cond)(fn)


def exchange_kernel(axes, nlat, nlon, t_hbm, s_hbm, u_hbm, v_hbm, d_hbm,
                    hs_o, hn_o, hw_o, he_o, cor_o,
                    xin, d_ref, top_b, bot_b, lft_b, rgt_b, hs, hn, hw, he, cor,
                    send_sem, recv_sem, in_sem):
    a = lax.axis_index("lat")
    b = lax.axis_index("lon")
    last = nlat - 1
    levels, rows, cols = t_hbm.shape
    left = (b + nlon - 1) % nlon
    right = (b + 1) % nlon
    loads = [pltpu.make_async_copy(src, xin.at[n], in_sem.at[n])
             for n, src in enumerate((t_hbm, s_hbm, u_hbm, v_hbm))]
    loads.append(pltpu.make_async_copy(d_hbm, d_ref, in_sem.at[4]))
    for copy in loads:
        copy.start()

    def dev(la, lo):
        return tuple(la if ax == "lat" else lo for ax in axes)

    def zero_south():
        hs[...] = jnp.zeros_like(hs)
        cor[0] = jnp.zeros_like(cor[0])
        cor[1] = jnp.zeros_like(cor[1])

    when(a == 0, zero_south)

    def zero_north():
        hn[...] = jnp.zeros_like(hn)
        cor[2] = jnp.zeros_like(cor[2])
        cor[3] = jnp.zeros_like(cor[3])

    when(a == last, zero_north)

    partners = [
        (a < last, (a + 1, b)), (a > 0, (a - 1, b)), (True, (a, left)), (True, (a, right)),
        (a < last, (a + 1, right)), (a < last, (a + 1, left)),
        (a > 0, (a - 1, right)), (a > 0, (a - 1, left)),
    ]
    barrier = pltpu.get_barrier_semaphore()
    for cond, target in partners:
        when(cond, lambda target=target: pl.semaphore_signal(
            barrier, 1, device_id=dev(*target), device_id_type=pl.DeviceIdType.MESH))

    for copy in loads:
        copy.wait()

    def body(k, carry):
        wet = jnp.where(d_ref[...] > k, 1.0, 0.0).astype(jnp.float32)
        for n in range(4):
            x = xin[n, k] * wet
            top_b[n, k] = x[0:2]
            bot_b[n, k] = x[rows - 2:rows]
            xt = jnp.transpose(x)
            lft_b[n, k] = xt[0:2]
            rgt_b[n, k] = xt[cols - 2:cols]
        return carry

    lax.fori_loop(0, levels, body, 0)

    below = (a + last) // (last + 1)
    above = (2 * last - a) // (last + 1)
    peers = 2 + 3 * below + 3 * above
    pl.semaphore_wait(barrier, peers)

    relations = [
        (a < last, a > 0, bot_b, hs, (a + 1, b)),
        (a > 0, a < last, top_b, hn, (a - 1, b)),
        (True, True, lft_b, he, (a, left)),
        (True, True, rgt_b, hw, (a, right)),
        (a < last, a > 0, rgt_b.at[:, :, 1:2], cor.at[0], (a + 1, right)),
        (a < last, a > 0, lft_b.at[:, :, 0:1], cor.at[1], (a + 1, left)),
        (a > 0, a < last, rgt_b.at[:, :, 1:2], cor.at[2], (a - 1, right)),
        (a > 0, a < last, lft_b.at[:, :, 0:1], cor.at[3], (a - 1, left)),
    ]
    copies = []
    for idx, (send, recv, src, dst, target) in enumerate(relations):
        copy = pltpu.make_async_remote_copy(
            src_ref=src, dst_ref=dst, send_sem=send_sem.at[idx], recv_sem=recv_sem.at[idx],
            device_id=dev(*target), device_id_type=pl.DeviceIdType.MESH)
        copies.append((send, recv, copy))
        when(send, copy.start)
    for send, recv, copy in copies:
        when(send, copy.wait_send)
        when(recv, copy.wait_recv)
    hs_o[...] = hs[...]
    hn_o[...] = hn[...]
    hw_o[...] = hw[...]
    he_o[...] = he[...]
    cor_o[...] = cor[...]


def step_kernel(nlat, t_ref, s_ref, u_ref, v_ref, d_ref, f_ref, hs_ref, hn_ref, hw_ref, he_ref,
                cor_ref, fr_ref, fc_ref, to_ref, so_ref, uo_ref, vo_ref,
                base, vp1, vm1, vp2, vm2, accx, accy, mt):
    k = pl.program_id(0)
    frame, width = base.shape[1], base.shape[2]
    rows = t_ref.shape[1]
    at_lat = lax.axis_index("lat")
    south = at_lat > 0
    fold = at_lat == nlat - 1

    @pl.when(k == 0)
    def _():
        base[...] = jnp.zeros_like(base)
        accx[...] = jnp.zeros_like(accx)
        accy[...] = jnp.zeros_like(accy)
        mt[...] = jnp.zeros_like(mt)

    for n in range(4):
        mt[8 * n:8 * n + 2] = he_ref[n, 0]
        mt[8 * n + 2:8 * n + 4] = hw_ref[n, 0]
        for c in range(4):
            mt[8 * n + 4 + c:8 * n + 5 + c] = cor_ref[c, n, 0]
    tt = jnp.transpose(mt[...])
    sub = lax.broadcasted_iota(jnp.int32, (top, 1), 0)
    zeros = jnp.zeros((top, 1), jnp.float32)

    wet = jnp.where(d_ref[...] > k, 1.0, 0.0).astype(jnp.float32)
    lane = lax.broadcasted_iota(jnp.int32, (frame, width), 1)
    ins = (t_ref, s_ref, u_ref, v_ref)
    for n in range(4):
        base[n, top:top + rows, :] = ins[n][0] * wet
        base[n, top - 2:top, :] = jnp.where(south, hs_ref[n, 0], 0.0)
        base[n, top + rows:top + rows + 2, :] = jnp.where(fold, fr_ref[n, 0], hn_ref[n, 0])
        whole = base[n]

        def col(r):
            return tt[:, 8 * n + r:8 * n + r + 1]

        def last_of(r):
            return tt[rows - 1:rows, 8 * n + r:8 * n + r + 1]

        def first_of(r):
            return tt[0:1, 8 * n + r:8 * n + r + 1]

        low_sw = jnp.where((sub == top - 1) & south, last_of(4), 0.0)
        low_se = jnp.where((sub == top - 1) & south, last_of(5), 0.0)
        nw_val = jnp.where(fold, fc_ref[n, 0, 0:1, 0:1], first_of(6))
        ne_val = jnp.where(fold, fc_ref[n, 0, 0:1, 1:2], first_of(7))
        high_nw = jnp.where(sub == 0, nw_val, 0.0)
        high_ne = jnp.where(sub == 0, ne_val, 0.0)
        e0 = jnp.broadcast_to(jnp.concatenate([low_se, col(0), high_ne], 0), (frame, width))
        e1 = jnp.broadcast_to(jnp.concatenate([zeros, col(1), zeros], 0), (frame, width))
        w0 = jnp.broadcast_to(jnp.concatenate([zeros, col(2), zeros], 0), (frame, width))
        w1 = jnp.broadcast_to(jnp.concatenate([low_sw, col(3), high_nw], 0), (frame, width))
        vp1[n] = jnp.where(lane == width - 1, e0, pltpu.roll(whole, width - 1, 1))
        vm1[n] = jnp.where(lane == 0, w1, pltpu.roll(whole, 1, 1))
        vp2[n] = jnp.where(lane == width - 2, e0,
                           jnp.where(lane == width - 1, e1, pltpu.roll(whole, width - 2, 1)))
        vm2[n] = jnp.where(lane == 0, w0, jnp.where(lane == 1, w1, pltpu.roll(whole, 2, 1)))

    def at(ref, n, d):
        return ref[n, top + d:top + d + rows, :]

    centre = [at(base, n, 0) for n in range(4)]
    first, second = centre[2], centre[3]
    parts = []
    for n in range(4):
        east, west = at(vp1, n, 0), at(vm1, n, 0)
        north, south_ = at(base, n, 1), at(base, n, -1)
        carried = 0.5 * (first * (east - west) + second * (north - south_))
        smooth = (
            20.0 * centre[n]
            - 8.0 * (east + west + north + south_)
            + 2.0 * (at(vp1, n, 1) + at(vp1, n, -1) + at(vm1, n, 1) + at(vm1, n, -1))
            + at(base, n, 2) + at(base, n, -2) + at(vp2, n, 0) + at(vm2, n, 0)
        )
        parts.append((east, west, north, south_, carried, smooth))

    def density(a, b):
        return -0.2 * a + 0.8 * b

    dx = density(parts[0][0], parts[1][0]) - density(parts[0][1], parts[1][1])
    dy = density(parts[0][2], parts[1][2]) - density(parts[0][3], parts[1][3])
    totx = accx[...] + dx
    toty = accy[...] + dy
    accx[...] = totx
    accy[...] = toty
    grad_x = 0.5 * (totx - 0.5 * dx)
    grad_y = 0.5 * (toty - 0.5 * dy)
    coriolis = f_ref[...]
    to_ref[0] = (centre[0] - time_step * parts[0][4] - biharmonic * parts[0][5]) * wet
    so_ref[0] = (centre[1] - time_step * parts[1][4] - biharmonic * parts[1][5]) * wet
    uo_ref[0] = (
        first + time_step * (coriolis * second - grad_x - parts[2][4]) - biharmonic * parts[2][5]
    ) * wet
    vo_ref[0] = (
        second + time_step * (-coriolis * first - grad_y - parts[3][4]) - biharmonic * parts[3][5]
    ) * wet


def shards(axes, temp, salt, uvel, vvel, depth_levels):
    levels, rows_dev, cols_dev = temp.shape
    nlat = lax.axis_size("lat")
    nlon = lax.axis_size("lon")
    at_lat = lax.axis_index("lat")
    f32 = jnp.float32
    vmem = pl.BlockSpec(memory_space=pltpu.VMEM)
    strip = jax.ShapeDtypeStruct((4, levels, 2, cols_dev), f32)
    corners = jax.ShapeDtypeStruct((4, 4, levels, 1, cols_dev), f32)
    fields = (temp, salt, uvel, vvel)
    level_index = jnp.arange(levels, dtype=jnp.int32)[:, None, None]
    wet_tail = jnp.where(depth_levels[None, rows_dev - 2:, :] > level_index, 1.0, 0.0).astype(f32)
    tail = jnp.stack([x[:, rows_dev - 2:, :] * wet_tail for x in fields])
    sign = jnp.array(signs, f32)[:, None, None, None]
    piece = tail[:, :, ::-1, ::-1] * sign
    ends = jnp.concatenate([tail[:, :, 1:, :1], tail[:, :, 1:, -1:]], axis=3) * sign
    last = nlat - 1

    def on_fold(value, target):
        pairs = [(i * nlat + last, target(i) * nlat + last) for i in range(nlon)]
        return lax.ppermute(value, ("lon", "lat"), pairs)

    fold_rows = on_fold(piece, lambda i: nlon - 1 - i)
    fold_nw = on_fold(ends[..., 0:1], lambda i: (nlon - i) % nlon)
    fold_ne = on_fold(ends[..., 1:2], lambda i: (2 * nlon - 2 - i) % nlon)
    fold_corners = jnp.concatenate([fold_nw, fold_ne], axis=3)
    hs, hn, hw, he, cor = pl.pallas_call(
        functools.partial(exchange_kernel, axes, nlat, nlon),
        out_shape=[strip] * 4 + [corners],
        in_specs=[pl.BlockSpec(memory_space=pl.ANY)] * 5,
        out_specs=[vmem] * 5,
        scratch_shapes=[pltpu.VMEM((4,) + temp.shape, f32),
                        pltpu.VMEM(depth_levels.shape, jnp.int32)]
        + [pltpu.VMEM(strip.shape, f32)] * 8
        + [pltpu.VMEM(corners.shape, f32)]
        + [pltpu.SemaphoreType.DMA((8,)), pltpu.SemaphoreType.DMA((8,)),
           pltpu.SemaphoreType.DMA((5,))],
        compiler_params=pltpu.CompilerParams(
            collective_id=0, has_side_effects=True, vmem_limit_bytes=48 * 1024 * 1024),
    )(temp, salt, uvel, vvel, depth_levels)

    total_rows = rows_dev * nlat
    global_rows = (at_lat * rows_dev + jnp.arange(rows_dev, dtype=jnp.int32)).astype(f32)
    coriolis = (0.5 * jnp.sin(math.pi * (global_rows + 0.5) / total_rows - 0.5 * math.pi))[:, None]
    coriolis = jnp.broadcast_to(coriolis, (rows_dev, cols_dev))

    frame = rows_dev + 2 * top
    level_block = pl.BlockSpec((1, rows_dev, cols_dev), lambda k: (k, 0, 0))
    plane = pl.BlockSpec((rows_dev, cols_dev), lambda k: (0, 0))
    halo = pl.BlockSpec((4, 1, 2, cols_dev), lambda k: (0, k, 0, 0))
    corner = pl.BlockSpec((4, 4, 1, 1, cols_dev), lambda k: (0, 0, k, 0, 0))
    fold_corner = pl.BlockSpec((4, 1, 1, 2), lambda k: (0, k, 0, 0))
    out = pl.pallas_call(
        functools.partial(step_kernel, nlat),
        grid=(levels,),
        in_specs=[level_block] * 4 + [plane] * 2 + [halo] * 4 + [corner, halo, fold_corner],
        out_specs=[level_block] * 4,
        out_shape=[jax.ShapeDtypeStruct(temp.shape, f32)] * 4,
        scratch_shapes=[pltpu.VMEM((4, frame, cols_dev), f32)] * 5
        + [pltpu.VMEM((rows_dev, cols_dev), f32)] * 2
        + [pltpu.VMEM((cols_dev, cols_dev), f32)],
        compiler_params=pltpu.CompilerParams(dimension_semantics=("arbitrary",)),
    )(temp, salt, uvel, vvel, depth_levels, coriolis, hs, hn, hw, he, cor, fold_rows, fold_corners)
    return tuple(out)


def solution(mesh):
    placed = (
        P(None, "lat", "lon"),
        P(None, "lat", "lon"),
        P(None, "lat", "lon"),
        P(None, "lat", "lon"),
        P("lat", "lon"),
    )
    return jax.shard_map(
        functools.partial(shards, tuple(mesh.axis_names)),
        mesh=mesh,
        in_specs=placed,
        out_specs=(
            P(None, "lat", "lon"),
            P(None, "lat", "lon"),
            P(None, "lat", "lon"),
            P(None, "lat", "lon"),
        ),
        check_vma=False,
    )
```

```python
import functools
import math

import jax
import jax.numpy as jnp
from jax import lax
from jax.experimental import pallas as pl
from jax.experimental.pallas import tpu as pltpu
from jax.sharding import PartitionSpec as P

time_step = 0.2
biharmonic = 0.01
signs = (1.0, 1.0, -1.0, -1.0)
top = 8


def when(cond, fn):
    if cond is True:
        fn()
    else:
        pl.when(cond)(fn)


def exchange_kernel(axes, nlat, nlon, t_hbm, s_hbm, u_hbm, v_hbm, d_hbm,
                    hs_o, hn_o, hw_o, he_o, cor_o,
                    xin, d_ref, top_b, bot_b, lft_b, rgt_b, hs, hn, hw, he, cor,
                    send_sem, recv_sem, in_sem):
    a = lax.axis_index("lat")
    b = lax.axis_index("lon")
    last = nlat - 1
    levels, rows, cols = t_hbm.shape
    left = (b + nlon - 1) % nlon
    right = (b + 1) % nlon
    loads = [pltpu.make_async_copy(src, xin.at[n], in_sem.at[n])
             for n, src in enumerate((t_hbm, s_hbm, u_hbm, v_hbm))]
    loads.append(pltpu.make_async_copy(d_hbm, d_ref, in_sem.at[4]))
    for copy in loads:
        copy.start()

    def dev(la, lo):
        return tuple(la if ax == "lat" else lo for ax in axes)

    def zero_south():
        hs[...] = jnp.zeros_like(hs)
        cor[0] = jnp.zeros_like(cor[0])
        cor[1] = jnp.zeros_like(cor[1])

    when(a == 0, zero_south)

    def zero_north():
        hn[...] = jnp.zeros_like(hn)
        cor[2] = jnp.zeros_like(cor[2])
        cor[3] = jnp.zeros_like(cor[3])

    when(a == last, zero_north)

    partners = [
        (a < last, (a + 1, b)), (a > 0, (a - 1, b)), (True, (a, left)), (True, (a, right)),
        (a < last, (a + 1, right)), (a < last, (a + 1, left)),
        (a > 0, (a - 1, right)), (a > 0, (a - 1, left)),
    ]
    barrier = pltpu.get_barrier_semaphore()
    for cond, target in partners:
        when(cond, lambda target=target: pl.semaphore_signal(
            barrier, 1, device_id=dev(*target), device_id_type=pl.DeviceIdType.MESH))

    for copy in loads:
        copy.wait()

    def body(k, carry):
        wet = jnp.where(d_ref[...] > k, 1.0, 0.0).astype(jnp.float32)
        for n in range(4):
            x = xin[n, k] * wet
            top_b[n, k] = x[0:2]
            bot_b[n, k] = x[rows - 2:rows]
            xt = jnp.transpose(x)
            lft_b[n, k] = xt[0:2]
            rgt_b[n, k] = xt[cols - 2:cols]
        return carry

    lax.fori_loop(0, levels, body, 0)

    below = (a + last) // (last + 1)
    above = (2 * last - a) // (last + 1)
    peers = 2 + 3 * below + 3 * above
    pl.semaphore_wait(barrier, peers)

    relations = [
        (a < last, a > 0, bot_b, hs, (a + 1, b)),
        (a > 0, a < last, top_b, hn, (a - 1, b)),
        (True, True, lft_b, he, (a, left)),
        (True, True, rgt_b, hw, (a, right)),
        (a < last, a > 0, rgt_b.at[:, :, 1:2], cor.at[0], (a + 1, right)),
        (a < last, a > 0, lft_b.at[:, :, 0:1], cor.at[1], (a + 1, left)),
        (a > 0, a < last, rgt_b.at[:, :, 1:2], cor.at[2], (a - 1, right)),
        (a > 0, a < last, lft_b.at[:, :, 0:1], cor.at[3], (a - 1, left)),
    ]
    copies = []
    for idx, (send, recv, src, dst, target) in enumerate(relations):
        copy = pltpu.make_async_remote_copy(
            src_ref=src, dst_ref=dst, send_sem=send_sem.at[idx], recv_sem=recv_sem.at[idx],
            device_id=dev(*target), device_id_type=pl.DeviceIdType.MESH)
        copies.append((send, recv, copy))
        when(send, copy.start)
    for send, recv, copy in copies:
        when(send, copy.wait_send)
        when(recv, copy.wait_recv)
    hs_o[...] = hs[...]
    hn_o[...] = hn[...]
    hw_o[...] = hw[...]
    he_o[...] = he[...]
    cor_o[...] = cor[...]


def step_kernel(nlat, t_ref, s_ref, u_ref, v_ref, d_ref, f_ref, hs_ref, hn_ref, hw_ref, he_ref,
                cor_ref, fr_ref, fc_ref, to_ref, so_ref, uo_ref, vo_ref,
                base, vp1, vm1, vp2, vm2, accx, accy, mt):
    k = pl.program_id(0)
    frame, width = base.shape[1], base.shape[2]
    rows = t_ref.shape[1]
    at_lat = lax.axis_index("lat")
    south = at_lat > 0
    fold = at_lat == nlat - 1

    @pl.when(k == 0)
    def _():
        base[...] = jnp.zeros_like(base)
        accx[...] = jnp.zeros_like(accx)
        accy[...] = jnp.zeros_like(accy)
        mt[...] = jnp.zeros_like(mt)

    for n in range(4):
        mt[8 * n:8 * n + 2] = he_ref[n, k]
        mt[8 * n + 2:8 * n + 4] = hw_ref[n, k]
        for c in range(4):
            mt[8 * n + 4 + c:8 * n + 5 + c] = cor_ref[c, n, k]
    tt = jnp.transpose(mt[...])
    sub = lax.broadcasted_iota(jnp.int32, (top, 1), 0)
    zeros = jnp.zeros((top, 1), jnp.float32)

    wet = jnp.where(d_ref[...] > k, 1.0, 0.0).astype(jnp.float32)
    lane = lax.broadcasted_iota(jnp.int32, (frame, width), 1)
    ins = (t_ref, s_ref, u_ref, v_ref)
    for n in range(4):
        base[n, top:top + rows, :] = ins[n][0] * wet
        base[n, top - 2:top, :] = jnp.where(south, hs_ref[n, k], 0.0)
        base[n, top + rows:top + rows + 2, :] = jnp.where(fold, fr_ref[n, k], hn_ref[n, k])
        whole = base[n]

        def col(r):
            return tt[:, 8 * n + r:8 * n + r + 1]

        def last_of(r):
            return tt[rows - 1:rows, 8 * n + r:8 * n + r + 1]

        def first_of(r):
            return tt[0:1, 8 * n + r:8 * n + r + 1]

        low_sw = jnp.where((sub == top - 1) & south, last_of(4), 0.0)
        low_se = jnp.where((sub == top - 1) & south, last_of(5), 0.0)
        fold_pair = fc_ref[n, k]
        nw_val = jnp.where(fold, fold_pair[:, 0:1], first_of(6))
        ne_val = jnp.where(fold, fold_pair[:, 1:2], first_of(7))
        high_nw = jnp.where(sub == 0, nw_val, 0.0)
        high_ne = jnp.where(sub == 0, ne_val, 0.0)
        e0 = jnp.broadcast_to(jnp.concatenate([low_se, col(0), high_ne], 0), (frame, width))
        e1 = jnp.broadcast_to(jnp.concatenate([zeros, col(1), zeros], 0), (frame, width))
        w0 = jnp.broadcast_to(jnp.concatenate([zeros, col(2), zeros], 0), (frame, width))
        w1 = jnp.broadcast_to(jnp.concatenate([low_sw, col(3), high_nw], 0), (frame, width))
        vp1[n] = jnp.where(lane == width - 1, e0, pltpu.roll(whole, width - 1, 1))
        vm1[n] = jnp.where(lane == 0, w1, pltpu.roll(whole, 1, 1))
        vp2[n] = jnp.where(lane == width - 2, e0,
                           jnp.where(lane == width - 1, e1, pltpu.roll(whole, width - 2, 1)))
        vm2[n] = jnp.where(lane == 0, w0, jnp.where(lane == 1, w1, pltpu.roll(whole, 2, 1)))

    def at(ref, n, d):
        return ref[n, top + d:top + d + rows, :]

    centre = [at(base, n, 0) for n in range(4)]
    first, second = centre[2], centre[3]
    parts = []
    for n in range(4):
        east, west = at(vp1, n, 0), at(vm1, n, 0)
        north, south_ = at(base, n, 1), at(base, n, -1)
        carried = 0.5 * (first * (east - west) + second * (north - south_))
        smooth = (
            20.0 * centre[n]
            - 8.0 * (east + west + north + south_)
            + 2.0 * (at(vp1, n, 1) + at(vp1, n, -1) + at(vm1, n, 1) + at(vm1, n, -1))
            + at(base, n, 2) + at(base, n, -2) + at(vp2, n, 0) + at(vm2, n, 0)
        )
        parts.append((east, west, north, south_, carried, smooth))

    def density(a, b):
        return -0.2 * a + 0.8 * b

    dx = density(parts[0][0], parts[1][0]) - density(parts[0][1], parts[1][1])
    dy = density(parts[0][2], parts[1][2]) - density(parts[0][3], parts[1][3])
    totx = accx[...] + dx
    toty = accy[...] + dy
    accx[...] = totx
    accy[...] = toty
    grad_x = 0.5 * (totx - 0.5 * dx)
    grad_y = 0.5 * (toty - 0.5 * dy)
    coriolis = f_ref[...]
    to_ref[0] = (centre[0] - time_step * parts[0][4] - biharmonic * parts[0][5]) * wet
    so_ref[0] = (centre[1] - time_step * parts[1][4] - biharmonic * parts[1][5]) * wet
    uo_ref[0] = (
        first + time_step * (coriolis * second - grad_x - parts[2][4]) - biharmonic * parts[2][5]
    ) * wet
    vo_ref[0] = (
        second + time_step * (-coriolis * first - grad_y - parts[3][4]) - biharmonic * parts[3][5]
    ) * wet


def shards(axes, temp, salt, uvel, vvel, depth_levels):
    levels, rows_dev, cols_dev = temp.shape
    nlat = lax.axis_size("lat")
    nlon = lax.axis_size("lon")
    at_lat = lax.axis_index("lat")
    f32 = jnp.float32
    vmem = pl.BlockSpec(memory_space=pltpu.VMEM)
    strip = jax.ShapeDtypeStruct((4, levels, 2, cols_dev), f32)
    corners = jax.ShapeDtypeStruct((4, 4, levels, 1, cols_dev), f32)
    fields = (temp, salt, uvel, vvel)
    level_index = jnp.arange(levels, dtype=jnp.int32)[:, None, None]
    wet_tail = jnp.where(depth_levels[None, rows_dev - 2:, :] > level_index, 1.0, 0.0).astype(f32)
    tail = jnp.stack([x[:, rows_dev - 2:, :] * wet_tail for x in fields])
    sign = jnp.array(signs, f32)[:, None, None, None]
    piece = tail[:, :, ::-1, ::-1] * sign
    ends = jnp.concatenate([tail[:, :, 1:, :1], tail[:, :, 1:, -1:]], axis=3) * sign
    last = nlat - 1

    def on_fold(value, target):
        pairs = [(i * nlat + last, target(i) * nlat + last) for i in range(nlon)]
        return lax.ppermute(value, ("lon", "lat"), pairs)

    fold_rows = on_fold(piece, lambda i: nlon - 1 - i)
    fold_nw = on_fold(ends[..., 0:1], lambda i: (nlon - i) % nlon)
    fold_ne = on_fold(ends[..., 1:2], lambda i: (2 * nlon - 2 - i) % nlon)
    fold_corners = jnp.concatenate([fold_nw, fold_ne], axis=3)
    hs, hn, hw, he, cor = pl.pallas_call(
        functools.partial(exchange_kernel, axes, nlat, nlon),
        out_shape=[strip] * 4 + [corners],
        in_specs=[pl.BlockSpec(memory_space=pl.ANY)] * 5,
        out_specs=[vmem] * 5,
        scratch_shapes=[pltpu.VMEM((4,) + temp.shape, f32),
                        pltpu.VMEM(depth_levels.shape, jnp.int32)]
        + [pltpu.VMEM(strip.shape, f32)] * 8
        + [pltpu.VMEM(corners.shape, f32)]
        + [pltpu.SemaphoreType.DMA((8,)), pltpu.SemaphoreType.DMA((8,)),
           pltpu.SemaphoreType.DMA((5,))],
        compiler_params=pltpu.CompilerParams(collective_id=0, has_side_effects=True),
    )(temp, salt, uvel, vvel, depth_levels)

    total_rows = rows_dev * nlat
    global_rows = (at_lat * rows_dev + jnp.arange(rows_dev, dtype=jnp.int32)).astype(f32)
    coriolis = (0.5 * jnp.sin(math.pi * (global_rows + 0.5) / total_rows - 0.5 * math.pi))[:, None]
    coriolis = jnp.broadcast_to(coriolis, (rows_dev, cols_dev))

    frame = rows_dev + 2 * top
    level_block = pl.BlockSpec((1, rows_dev, cols_dev), lambda k: (k, 0, 0))
    plane = pl.BlockSpec((rows_dev, cols_dev), lambda k: (0, 0))
    out = pl.pallas_call(
        functools.partial(step_kernel, nlat),
        grid=(levels,),
        in_specs=[level_block] * 4 + [plane] * 2 + [vmem] * 7,
        out_specs=[level_block] * 4,
        out_shape=[jax.ShapeDtypeStruct(temp.shape, f32)] * 4,
        scratch_shapes=[pltpu.VMEM((4, frame, cols_dev), f32)] * 5
        + [pltpu.VMEM((rows_dev, cols_dev), f32)] * 2
        + [pltpu.VMEM((cols_dev, cols_dev), f32)],
        compiler_params=pltpu.CompilerParams(dimension_semantics=("arbitrary",)),
    )(temp, salt, uvel, vvel, depth_levels, coriolis, hs, hn, hw, he, cor, fold_rows, fold_corners)
    return tuple(out)


def solution(mesh):
    placed = (
        P(None, "lat", "lon"),
        P(None, "lat", "lon"),
        P(None, "lat", "lon"),
        P(None, "lat", "lon"),
        P("lat", "lon"),
    )
    return jax.shard_map(
        functools.partial(shards, tuple(mesh.axis_names)),
        mesh=mesh,
        in_specs=placed,
        out_specs=(
            P(None, "lat", "lon"),
            P(None, "lat", "lon"),
            P(None, "lat", "lon"),
            P(None, "lat", "lon"),
        ),
        check_vma=False,
    )
```

```python
import functools
import math

import jax
import jax.numpy as jnp
from jax import lax
from jax.experimental import pallas as pl
from jax.experimental.pallas import tpu as pltpu
from jax.sharding import PartitionSpec as P

time_step = 0.2
biharmonic = 0.01
signs = (1.0, 1.0, -1.0, -1.0)
top = 8


def when(cond, fn):
    if cond is True:
        fn()
    else:
        pl.when(cond)(fn)


def exchange_kernel(axes, nlat, nlon, t_hbm, s_hbm, u_hbm, v_hbm, d_hbm,
                    hs_o, hn_o, hw_o, he_o, cor_o,
                    xin, d_ref, top_b, bot_b, lft_b, rgt_b, hs, hn, hw, he, cor,
                    send_sem, recv_sem, in_sem):
    a = lax.axis_index("lat")
    b = lax.axis_index("lon")
    last = nlat - 1
    levels, rows, cols = t_hbm.shape
    left = (b + nlon - 1) % nlon
    right = (b + 1) % nlon
    loads = [pltpu.make_async_copy(src, xin.at[n], in_sem.at[n])
             for n, src in enumerate((t_hbm, s_hbm, u_hbm, v_hbm))]
    loads.append(pltpu.make_async_copy(d_hbm, d_ref, in_sem.at[4]))
    for copy in loads:
        copy.start()

    def dev(la, lo):
        return tuple(la if ax == "lat" else lo for ax in axes)

    def zero_south():
        hs[...] = jnp.zeros_like(hs)
        cor[0] = jnp.zeros_like(cor[0])
        cor[1] = jnp.zeros_like(cor[1])

    when(a == 0, zero_south)

    def zero_north():
        hn[...] = jnp.zeros_like(hn)
        cor[2] = jnp.zeros_like(cor[2])
        cor[3] = jnp.zeros_like(cor[3])

    when(a == last, zero_north)

    partners = [
        (a < last, (a + 1, b)), (a > 0, (a - 1, b)), (True, (a, left)), (True, (a, right)),
        (a < last, (a + 1, right)), (a < last, (a + 1, left)),
        (a > 0, (a - 1, right)), (a > 0, (a - 1, left)),
    ]
    barrier = pltpu.get_barrier_semaphore()
    for cond, target in partners:
        when(cond, lambda target=target: pl.semaphore_signal(
            barrier, 1, device_id=dev(*target), device_id_type=pl.DeviceIdType.MESH))

    for copy in loads:
        copy.wait()

    def body(k, carry):
        wet = jnp.where(d_ref[...] > k, 1.0, 0.0).astype(jnp.float32)
        for n in range(4):
            x = xin[n, k] * wet
            top_b[n, k] = x[0:2]
            bot_b[n, k] = x[rows - 2:rows]
            xt = jnp.transpose(x)
            lft_b[n, k] = xt[0:2]
            rgt_b[n, k] = xt[cols - 2:cols]
        return carry

    lax.fori_loop(0, levels, body, 0)

    below = (a + last) // (last + 1)
    above = (2 * last - a) // (last + 1)
    peers = 2 + 3 * below + 3 * above
    pl.semaphore_wait(barrier, peers)

    relations = [
        (a < last, a > 0, bot_b, hs, (a + 1, b)),
        (a > 0, a < last, top_b, hn, (a - 1, b)),
        (True, True, lft_b, he, (a, left)),
        (True, True, rgt_b, hw, (a, right)),
        (a < last, a > 0, rgt_b.at[:, :, 1:2], cor.at[0], (a + 1, right)),
        (a < last, a > 0, lft_b.at[:, :, 0:1], cor.at[1], (a + 1, left)),
        (a > 0, a < last, rgt_b.at[:, :, 1:2], cor.at[2], (a - 1, right)),
        (a > 0, a < last, lft_b.at[:, :, 0:1], cor.at[3], (a - 1, left)),
    ]
    copies = []
    for idx, (send, recv, src, dst, target) in enumerate(relations):
        copy = pltpu.make_async_remote_copy(
            src_ref=src, dst_ref=dst, send_sem=send_sem.at[idx], recv_sem=recv_sem.at[idx],
            device_id=dev(*target), device_id_type=pl.DeviceIdType.MESH)
        copies.append((send, recv, copy))
        when(send, copy.start)
    for send, recv, copy in copies:
        when(send, copy.wait_send)
        when(recv, copy.wait_recv)
    hs_o[...] = hs[...]
    hn_o[...] = hn[...]
    hw_o[...] = hw[...]
    he_o[...] = he[...]
    cor_o[...] = cor[...]


def step_kernel(nlat, t_ref, s_ref, u_ref, v_ref, d_ref, f_ref, hs_ref, hn_ref, hw_ref, he_ref,
                cor_ref, fr_ref, fc_ref, to_ref, so_ref, uo_ref, vo_ref,
                base, vp1, vm1, vp2, vm2, accx, accy, mt, tf):
    k = pl.program_id(0)
    frame, width = base.shape[1], base.shape[2]
    rows = t_ref.shape[1]
    at_lat = lax.axis_index("lat")
    south = at_lat > 0
    fold = at_lat == nlat - 1

    @pl.when(k == 0)
    def _():
        base[...] = jnp.zeros_like(base)
        accx[...] = jnp.zeros_like(accx)
        accy[...] = jnp.zeros_like(accy)
        mt[...] = jnp.zeros_like(mt)
        tf[...] = jnp.zeros_like(tf)

    wet = jnp.where(d_ref[...] > k, 1.0, 0.0).astype(jnp.float32)
    lane = lax.broadcasted_iota(jnp.int32, (frame, width), 1)
    line_lane = lax.broadcasted_iota(jnp.int32, (1, width), 1)
    ins = (t_ref, s_ref, u_ref, v_ref)
    for n in range(4):
        base[n, top:top + rows, :] = ins[n][0] * wet
        base[n, top - 2:top, :] = jnp.where(south, hs_ref[n, k], 0.0)
        base[n, top + rows:top + rows + 2, :] = jnp.where(fold, fr_ref[n, k], hn_ref[n, k])
        mt[0:2] = he_ref[n, k]
        mt[width - 2:width] = hw_ref[n, k]
        tf[top:top + rows] = jnp.transpose(mt[...])
        sw_line = cor_ref[0, n, k]
        se_line = pltpu.roll(cor_ref[1, n, k], 1, 1)
        nw_line = pltpu.roll(cor_ref[2, n, k], width - 1, 1)
        ne_line = cor_ref[3, n, k]
        low = jnp.where(line_lane == width - 1, sw_line, jnp.where(line_lane == 0, se_line, 0.0))
        high = jnp.where(line_lane == width - 1, nw_line, jnp.where(line_lane == 0, ne_line, 0.0))
        tf[top - 1:top] = jnp.where(south, low, 0.0)
        tf[top + rows:top + rows + 1] = jnp.where(fold, fc_ref[n, k], high)
        whole = base[n]
        edge = tf[...]
        vp1[n] = pltpu.roll(jnp.where(lane == 0, edge, whole), width - 1, 1)
        vm1[n] = pltpu.roll(jnp.where(lane == width - 1, edge, whole), 1, 1)
        vp2[n] = pltpu.roll(jnp.where(lane < 2, edge, whole), width - 2, 1)
        vm2[n] = pltpu.roll(jnp.where(lane >= width - 2, edge, whole), 2, 1)

    def at(ref, n, d):
        return ref[n, top + d:top + d + rows, :]

    centre = [at(base, n, 0) for n in range(4)]
    first, second = centre[2], centre[3]
    parts = []
    for n in range(4):
        east, west = at(vp1, n, 0), at(vm1, n, 0)
        north, south_ = at(base, n, 1), at(base, n, -1)
        carried = 0.5 * (first * (east - west) + second * (north - south_))
        smooth = (
            20.0 * centre[n]
            - 8.0 * (east + west + north + south_)
            + 2.0 * (at(vp1, n, 1) + at(vp1, n, -1) + at(vm1, n, 1) + at(vm1, n, -1))
            + at(base, n, 2) + at(base, n, -2) + at(vp2, n, 0) + at(vm2, n, 0)
        )
        parts.append((east, west, north, south_, carried, smooth))

    def density(a, b):
        return -0.2 * a + 0.8 * b

    dx = density(parts[0][0], parts[1][0]) - density(parts[0][1], parts[1][1])
    dy = density(parts[0][2], parts[1][2]) - density(parts[0][3], parts[1][3])
    totx = accx[...] + dx
    toty = accy[...] + dy
    accx[...] = totx
    accy[...] = toty
    grad_x = 0.5 * (totx - 0.5 * dx)
    grad_y = 0.5 * (toty - 0.5 * dy)
    coriolis = f_ref[...]
    to_ref[0] = (centre[0] - time_step * parts[0][4] - biharmonic * parts[0][5]) * wet
    so_ref[0] = (centre[1] - time_step * parts[1][4] - biharmonic * parts[1][5]) * wet
    uo_ref[0] = (
        first + time_step * (coriolis * second - grad_x - parts[2][4]) - biharmonic * parts[2][5]
    ) * wet
    vo_ref[0] = (
        second + time_step * (-coriolis * first - grad_y - parts[3][4]) - biharmonic * parts[3][5]
    ) * wet


def shards(axes, temp, salt, uvel, vvel, depth_levels):
    levels, rows_dev, cols_dev = temp.shape
    nlat = lax.axis_size("lat")
    nlon = lax.axis_size("lon")
    at_lat = lax.axis_index("lat")
    f32 = jnp.float32
    vmem = pl.BlockSpec(memory_space=pltpu.VMEM)
    strip = jax.ShapeDtypeStruct((4, levels, 2, cols_dev), f32)
    corners = jax.ShapeDtypeStruct((4, 4, levels, 1, cols_dev), f32)
    fields = (temp, salt, uvel, vvel)
    level_index = jnp.arange(levels, dtype=jnp.int32)[:, None, None]
    wet_tail = jnp.where(depth_levels[None, rows_dev - 2:, :] > level_index, 1.0, 0.0).astype(f32)
    tail = jnp.stack([x[:, rows_dev - 2:, :] * wet_tail for x in fields])
    sign = jnp.array(signs, f32)[:, None, None, None]
    piece = tail[:, :, ::-1, ::-1] * sign
    ends = jnp.concatenate([tail[:, :, 1:, :1], tail[:, :, 1:, -1:]], axis=3) * sign
    last = nlat - 1

    def on_fold(value, target):
        pairs = [(i * nlat + last, target(i) * nlat + last) for i in range(nlon)]
        return lax.ppermute(value, ("lon", "lat"), pairs)

    fold_rows = on_fold(piece, lambda i: nlon - 1 - i)
    fold_nw = on_fold(ends[..., 0:1], lambda i: (nlon - i) % nlon)
    fold_ne = on_fold(ends[..., 1:2], lambda i: (2 * nlon - 2 - i) % nlon)
    fold_corners = jnp.concatenate(
        [fold_ne, jnp.zeros((4, levels, 1, cols_dev - 2), f32), fold_nw], axis=3)
    hs, hn, hw, he, cor = pl.pallas_call(
        functools.partial(exchange_kernel, axes, nlat, nlon),
        out_shape=[strip] * 4 + [corners],
        in_specs=[pl.BlockSpec(memory_space=pl.ANY)] * 5,
        out_specs=[vmem] * 5,
        scratch_shapes=[pltpu.VMEM((4,) + temp.shape, f32),
                        pltpu.VMEM(depth_levels.shape, jnp.int32)]
        + [pltpu.VMEM(strip.shape, f32)] * 8
        + [pltpu.VMEM(corners.shape, f32)]
        + [pltpu.SemaphoreType.DMA((8,)), pltpu.SemaphoreType.DMA((8,)),
           pltpu.SemaphoreType.DMA((5,))],
        compiler_params=pltpu.CompilerParams(collective_id=0, has_side_effects=True),
    )(temp, salt, uvel, vvel, depth_levels)

    total_rows = rows_dev * nlat
    global_rows = (at_lat * rows_dev + jnp.arange(rows_dev, dtype=jnp.int32)).astype(f32)
    coriolis = (0.5 * jnp.sin(math.pi * (global_rows + 0.5) / total_rows - 0.5 * math.pi))[:, None]
    coriolis = jnp.broadcast_to(coriolis, (rows_dev, cols_dev))

    frame = rows_dev + 2 * top
    level_block = pl.BlockSpec((1, rows_dev, cols_dev), lambda k: (k, 0, 0))
    plane = pl.BlockSpec((rows_dev, cols_dev), lambda k: (0, 0))
    out = pl.pallas_call(
        functools.partial(step_kernel, nlat),
        grid=(levels,),
        in_specs=[level_block] * 4 + [plane] * 2 + [vmem] * 7,
        out_specs=[level_block] * 4,
        out_shape=[jax.ShapeDtypeStruct(temp.shape, f32)] * 4,
        scratch_shapes=[pltpu.VMEM((4, frame, cols_dev), f32)] * 5
        + [pltpu.VMEM((rows_dev, cols_dev), f32)] * 2
        + [pltpu.VMEM((cols_dev, cols_dev), f32), pltpu.VMEM((frame, cols_dev), f32)],
        compiler_params=pltpu.CompilerParams(dimension_semantics=("arbitrary",)),
    )(temp, salt, uvel, vvel, depth_levels, coriolis, hs, hn, hw, he, cor, fold_rows, fold_corners)
    return tuple(out)


def solution(mesh):
    placed = (
        P(None, "lat", "lon"),
        P(None, "lat", "lon"),
        P(None, "lat", "lon"),
        P(None, "lat", "lon"),
        P("lat", "lon"),
    )
    return jax.shard_map(
        functools.partial(shards, tuple(mesh.axis_names)),
        mesh=mesh,
        in_specs=placed,
        out_specs=(
            P(None, "lat", "lon"),
            P(None, "lat", "lon"),
            P(None, "lat", "lon"),
            P(None, "lat", "lon"),
        ),
        check_vma=False,
    )
```

```python
import functools
import math

import jax
import jax.numpy as jnp
from jax import lax
from jax.experimental import pallas as pl
from jax.experimental.pallas import tpu as pltpu
from jax.sharding import PartitionSpec as P

time_step = 0.2
biharmonic = 0.01
signs = (1.0, 1.0, -1.0, -1.0)
top = 8


def when(cond, fn):
    if cond is True:
        fn()
    else:
        pl.when(cond)(fn)


def exchange_kernel(axes, nlat, nlon, t_hbm, s_hbm, u_hbm, v_hbm, d_hbm,
                    hs_o, hn_o, hw_o, he_o, cor_o,
                    xin, d_ref, top_b, bot_b, lft_b, rgt_b, hs, hn, hw, he, cor,
                    send_sem, recv_sem, in_sem):
    a = lax.axis_index("lat")
    b = lax.axis_index("lon")
    last = nlat - 1
    levels, rows, cols = t_hbm.shape
    left = (b + nlon - 1) % nlon
    right = (b + 1) % nlon
    loads = [pltpu.make_async_copy(src, xin.at[n], in_sem.at[n])
             for n, src in enumerate((t_hbm, s_hbm, u_hbm, v_hbm))]
    loads.append(pltpu.make_async_copy(d_hbm, d_ref, in_sem.at[4]))
    for copy in loads:
        copy.start()

    def dev(la, lo):
        return tuple(la if ax == "lat" else lo for ax in axes)

    def zero_south():
        hs[...] = jnp.zeros_like(hs)
        cor[0] = jnp.zeros_like(cor[0])
        cor[1] = jnp.zeros_like(cor[1])

    when(a == 0, zero_south)

    def zero_north():
        hn[...] = jnp.zeros_like(hn)
        cor[2] = jnp.zeros_like(cor[2])
        cor[3] = jnp.zeros_like(cor[3])

    when(a == last, zero_north)

    partners = [
        (a < last, (a + 1, b)), (a > 0, (a - 1, b)), (True, (a, left)), (True, (a, right)),
        (a < last, (a + 1, right)), (a < last, (a + 1, left)),
        (a > 0, (a - 1, right)), (a > 0, (a - 1, left)),
    ]
    barrier = pltpu.get_barrier_semaphore()
    for cond, target in partners:
        when(cond, lambda target=target: pl.semaphore_signal(
            barrier, 1, device_id=dev(*target), device_id_type=pl.DeviceIdType.MESH))

    for copy in loads:
        copy.wait()

    def body(k, carry):
        wet = jnp.where(d_ref[...] > k, 1.0, 0.0).astype(jnp.float32)
        for n in range(4):
            x = xin[n, k] * wet
            top_b[n, k] = x[0:2]
            bot_b[n, k] = x[rows - 2:rows]
            xt = jnp.transpose(x)
            lft_b[n, k] = xt[0:2]
            rgt_b[n, k] = xt[cols - 2:cols]
        return carry

    lax.fori_loop(0, levels, body, 0)

    below = (a + last) // (last + 1)
    above = (2 * last - a) // (last + 1)
    peers = 2 + 3 * below + 3 * above
    pl.semaphore_wait(barrier, peers)

    relations = [
        (a < last, a > 0, bot_b, hs, (a + 1, b)),
        (a > 0, a < last, top_b, hn, (a - 1, b)),
        (True, True, lft_b, he, (a, left)),
        (True, True, rgt_b, hw, (a, right)),
        (a < last, a > 0, rgt_b.at[:, :, 1:2], cor.at[0], (a + 1, right)),
        (a < last, a > 0, lft_b.at[:, :, 0:1], cor.at[1], (a + 1, left)),
        (a > 0, a < last, rgt_b.at[:, :, 1:2], cor.at[2], (a - 1, right)),
        (a > 0, a < last, lft_b.at[:, :, 0:1], cor.at[3], (a - 1, left)),
    ]
    copies = []
    for idx, (send, recv, src, dst, target) in enumerate(relations):
        copy = pltpu.make_async_remote_copy(
            src_ref=src, dst_ref=dst, send_sem=send_sem.at[idx], recv_sem=recv_sem.at[idx],
            device_id=dev(*target), device_id_type=pl.DeviceIdType.MESH)
        copies.append((send, recv, copy))
        when(send, copy.start)
    for send, recv, copy in copies:
        when(send, copy.wait_send)
        when(recv, copy.wait_recv)
    hs_o[...] = hs[...]
    hn_o[...] = hn[...]
    hw_o[...] = hw[...]
    he_o[...] = he[...]
    cor_o[...] = cor[...]


def step_kernel(nlat, t_ref, s_ref, u_ref, v_ref, d_ref, f_ref, hs_ref, hn_ref, hw_ref, he_ref,
                cor_ref, fr_ref, fc_ref, to_ref, so_ref, uo_ref, vo_ref,
                base, vp1, vm1, vp2, vm2, accx, accy, mt, tf):
    k = pl.program_id(0)
    frame, width = base.shape[1], base.shape[2]
    rows = t_ref.shape[1]
    at_lat = lax.axis_index("lat")
    south = at_lat > 0
    fold = at_lat == nlat - 1

    @pl.when(k == 0)
    def _():
        base[...] = jnp.zeros_like(base)
        accx[...] = jnp.zeros_like(accx)
        accy[...] = jnp.zeros_like(accy)
        mt[...] = jnp.zeros_like(mt)
        tf[...] = jnp.zeros_like(tf)

    wet = jnp.where(d_ref[...] > k, 1.0, 0.0).astype(jnp.float32)
    lane = lax.broadcasted_iota(jnp.int32, (frame, width), 1)
    line_lane = lax.broadcasted_iota(jnp.int32, (1, width), 1)
    ins = (t_ref, s_ref, u_ref, v_ref)
    for n in range(4):
        base[n, top:top + rows, :] = ins[n][0] * wet
        base[n, top - 2:top, :] = jnp.where(south, hs_ref[n, k], 0.0)
        base[n, top + rows:top + rows + 2, :] = jnp.where(fold, fr_ref[n, k], hn_ref[n, k])
        mt[0:2] = he_ref[n, k]
        mt[width - 2:width] = hw_ref[n, k]
        tf[top:top + rows] = jnp.transpose(mt[...])
        sw_line = cor_ref[0, n, k]
        se_line = pltpu.roll(cor_ref[1, n, k], 1, 1)
        nw_line = pltpu.roll(cor_ref[2, n, k], width - 1, 1)
        ne_line = cor_ref[3, n, k]
        low = jnp.where(line_lane == width - 1, sw_line, jnp.where(line_lane == 0, se_line, 0.0))
        high = jnp.where(line_lane == width - 1, nw_line, jnp.where(line_lane == 0, ne_line, 0.0))
        tf[top - 1:top] = jnp.where(south, low, 0.0)
        tf[top + rows:top + rows + 1] = jnp.where(fold, fc_ref[n, k], high)
        whole = base[n]
        edge = tf[...]
        vp1[n] = pltpu.roll(jnp.where(lane == 0, edge, whole), width - 1, 1)
        vm1[n] = pltpu.roll(jnp.where(lane == width - 1, edge, whole), 1, 1)
        vp2[n] = pltpu.roll(jnp.where(lane < 2, edge, whole), width - 2, 1)
        vm2[n] = pltpu.roll(jnp.where(lane >= width - 2, edge, whole), 2, 1)

    def at(ref, n, d):
        return ref[n, top + d:top + d + rows, :]

    centre = [at(base, n, 0) for n in range(4)]
    first, second = centre[2], centre[3]
    parts = []
    for n in range(4):
        east, west = at(vp1, n, 0), at(vm1, n, 0)
        north, south_ = at(base, n, 1), at(base, n, -1)
        carried = 0.5 * (first * (east - west) + second * (north - south_))
        smooth = (
            20.0 * centre[n]
            - 8.0 * (east + west + north + south_)
            + 2.0 * (at(vp1, n, 1) + at(vp1, n, -1) + at(vm1, n, 1) + at(vm1, n, -1))
            + at(base, n, 2) + at(base, n, -2) + at(vp2, n, 0) + at(vm2, n, 0)
        )
        parts.append((east, west, north, south_, carried, smooth))

    def density(a, b):
        return -0.2 * a + 0.8 * b

    dx = density(parts[0][0], parts[1][0]) - density(parts[0][1], parts[1][1])
    dy = density(parts[0][2], parts[1][2]) - density(parts[0][3], parts[1][3])
    totx = accx[...] + dx
    toty = accy[...] + dy
    accx[...] = totx
    accy[...] = toty
    grad_x = 0.5 * (totx - 0.5 * dx)
    grad_y = 0.5 * (toty - 0.5 * dy)
    coriolis = f_ref[...]
    to_ref[0] = (centre[0] - time_step * parts[0][4] - biharmonic * parts[0][5]) * wet
    so_ref[0] = (centre[1] - time_step * parts[1][4] - biharmonic * parts[1][5]) * wet
    uo_ref[0] = (
        first + time_step * (coriolis * second - grad_x - parts[2][4]) - biharmonic * parts[2][5]
    ) * wet
    vo_ref[0] = (
        second + time_step * (-coriolis * first - grad_y - parts[3][4]) - biharmonic * parts[3][5]
    ) * wet


def shards(axes, temp, salt, uvel, vvel, depth_levels):
    levels, rows_dev, cols_dev = temp.shape
    nlat = lax.axis_size("lat")
    nlon = lax.axis_size("lon")
    at_lat = lax.axis_index("lat")
    f32 = jnp.float32
    vmem = pl.BlockSpec(memory_space=pltpu.VMEM)
    strip = jax.ShapeDtypeStruct((4, levels, 2, cols_dev), f32)
    corners = jax.ShapeDtypeStruct((4, 4, levels, 1, cols_dev), f32)
    hs, hn, hw, he, cor = pl.pallas_call(
        functools.partial(exchange_kernel, axes, nlat, nlon),
        out_shape=[strip] * 4 + [corners],
        in_specs=[pl.BlockSpec(memory_space=pl.ANY)] * 5,
        out_specs=[vmem] * 5,
        scratch_shapes=[pltpu.VMEM((4,) + temp.shape, f32),
                        pltpu.VMEM(depth_levels.shape, jnp.int32)]
        + [pltpu.VMEM(strip.shape, f32)] * 8
        + [pltpu.VMEM(corners.shape, f32)]
        + [pltpu.SemaphoreType.DMA((8,)), pltpu.SemaphoreType.DMA((8,)),
           pltpu.SemaphoreType.DMA((5,))],
        compiler_params=pltpu.CompilerParams(collective_id=0, has_side_effects=True),
    )(temp, salt, uvel, vvel, depth_levels)

    temp_, salt_, uvel_, vvel_, depth_, hs = lax.optimization_barrier(
        (temp, salt, uvel, vvel, depth_levels, hs))
    fields = (temp_, salt_, uvel_, vvel_)
    level_index = jnp.arange(levels, dtype=jnp.int32)[:, None, None]
    wet_tail = jnp.where(depth_[None, rows_dev - 2:, :] > level_index, 1.0, 0.0).astype(f32)
    tail = jnp.stack([x[:, rows_dev - 2:, :] * wet_tail for x in fields])
    sign = jnp.array(signs, f32)[:, None, None, None]
    piece = tail[:, :, ::-1, ::-1] * sign
    ends = jnp.concatenate([tail[:, :, 1:, :1], tail[:, :, 1:, -1:]], axis=3) * sign
    last = nlat - 1

    def on_fold(value, target):
        pairs = [(i * nlat + last, target(i) * nlat + last) for i in range(nlon)]
        return lax.ppermute(value, ("lon", "lat"), pairs)

    fold_rows = on_fold(piece, lambda i: nlon - 1 - i)
    fold_nw = on_fold(ends[..., 0:1], lambda i: (nlon - i) % nlon)
    fold_ne = on_fold(ends[..., 1:2], lambda i: (2 * nlon - 2 - i) % nlon)
    fold_corners = jnp.concatenate(
        [fold_ne, jnp.zeros((4, levels, 1, cols_dev - 2), f32), fold_nw], axis=3)

    total_rows = rows_dev * nlat
    global_rows = (at_lat * rows_dev + jnp.arange(rows_dev, dtype=jnp.int32)).astype(f32)
    coriolis = (0.5 * jnp.sin(math.pi * (global_rows + 0.5) / total_rows - 0.5 * math.pi))[:, None]
    coriolis = jnp.broadcast_to(coriolis, (rows_dev, cols_dev))

    frame = rows_dev + 2 * top
    level_block = pl.BlockSpec((1, rows_dev, cols_dev), lambda k: (k, 0, 0))
    plane = pl.BlockSpec((rows_dev, cols_dev), lambda k: (0, 0))
    out = pl.pallas_call(
        functools.partial(step_kernel, nlat),
        grid=(levels,),
        in_specs=[level_block] * 4 + [plane] * 2 + [vmem] * 7,
        out_specs=[level_block] * 4,
        out_shape=[jax.ShapeDtypeStruct(temp.shape, f32)] * 4,
        scratch_shapes=[pltpu.VMEM((4, frame, cols_dev), f32)] * 5
        + [pltpu.VMEM((rows_dev, cols_dev), f32)] * 2
        + [pltpu.VMEM((cols_dev, cols_dev), f32), pltpu.VMEM((frame, cols_dev), f32)],
        compiler_params=pltpu.CompilerParams(dimension_semantics=("arbitrary",)),
    )(temp, salt, uvel, vvel, depth_levels, coriolis, hs, hn, hw, he, cor, fold_rows, fold_corners)
    return tuple(out)


def solution(mesh):
    placed = (
        P(None, "lat", "lon"),
        P(None, "lat", "lon"),
        P(None, "lat", "lon"),
        P(None, "lat", "lon"),
        P("lat", "lon"),
    )
    return jax.shard_map(
        functools.partial(shards, tuple(mesh.axis_names)),
        mesh=mesh,
        in_specs=placed,
        out_specs=(
            P(None, "lat", "lon"),
            P(None, "lat", "lon"),
            P(None, "lat", "lon"),
            P(None, "lat", "lon"),
        ),
        check_vma=False,
    )
```

```python
import functools
import math

import jax
import jax.numpy as jnp
from jax import lax
from jax.experimental import pallas as pl
from jax.experimental.pallas import tpu as pltpu
from jax.sharding import PartitionSpec as P

time_step = 0.2
biharmonic = 0.01
signs = (1.0, 1.0, -1.0, -1.0)
top = 8


def when(cond, fn):
    if cond is True:
        fn()
    else:
        pl.when(cond)(fn)


def reverse_lanes(x):
    lane = lax.broadcasted_iota(jnp.int32, x.shape, 1)
    width = x.shape[1]
    bit = 1
    while bit < width:
        x = jnp.where((lane & bit) != 0, pltpu.roll(x, bit, 1), pltpu.roll(x, width - bit, 1))
        bit *= 2
    return x


def exchange_kernel(axes, nlat, nlon, t_hbm, s_hbm, u_hbm, v_hbm, d_hbm,
                    hs_o, hn_o, hw_o, he_o, cor_o,
                    xin, d_ref, top_b, bot_b, fold_b, lft_b, rgt_b, hs, hn, hw, he, cor,
                    send_sem, recv_sem, in_sem, local_sem):
    a = lax.axis_index("lat")
    b = lax.axis_index("lon")
    last = nlat - 1
    levels, rows, cols = t_hbm.shape
    left = (b + nlon - 1) % nlon
    right = (b + 1) % nlon
    mirror = nlon - 1 - b
    ne = (2 * nlon - 2 - b) % nlon
    nw = (nlon - b) % nlon
    fold = a == last
    loads = [pltpu.make_async_copy(src, xin.at[n], in_sem.at[n])
             for n, src in enumerate((t_hbm, s_hbm, u_hbm, v_hbm))]
    loads.append(pltpu.make_async_copy(d_hbm, d_ref, in_sem.at[4]))
    for copy in loads:
        copy.start()

    def dev(la, lo):
        return tuple(la if ax == "lat" else lo for ax in axes)

    def zero_south():
        hs[...] = jnp.zeros_like(hs)
        cor[0] = jnp.zeros_like(cor[0])
        cor[1] = jnp.zeros_like(cor[1])

    when(a == 0, zero_south)

    partners = [
        (a < last, (a + 1, b)), (a > 0, (a - 1, b)), (True, (a, left)), (True, (a, right)),
        (a < last, (a + 1, right)), (a < last, (a + 1, left)),
        (a > 0, (a - 1, right)), (a > 0, (a - 1, left)),
        (fold, (last, mirror)), (fold & (ne != b), (last, ne)), (fold & (nw != b), (last, nw)),
    ]
    barrier = pltpu.get_barrier_semaphore()
    for cond, target in partners:
        when(cond, lambda target=target: pl.semaphore_signal(
            barrier, 1, device_id=dev(*target), device_id_type=pl.DeviceIdType.MESH))

    for copy in loads:
        copy.wait()

    def body(k, carry):
        wet = jnp.where(d_ref[...] > k, 1.0, 0.0).astype(jnp.float32)
        for n in range(4):
            x = xin[n, k] * wet
            top_b[n, k] = x[0:2]
            bot_b[n, k] = x[rows - 2:rows]
            flipped = reverse_lanes(x[rows - 8:rows])
            fold_b[n, k, 0:1] = signs[n] * flipped[7:8]
            fold_b[n, k, 1:2] = signs[n] * flipped[6:7]
            xt = jnp.transpose(x)
            lft_b[n, k] = xt[0:2]
            rgt_b[n, k] = xt[cols - 2:cols]
        return carry

    lax.fori_loop(0, levels, body, 0)

    below = (a + last) // (last + 1)
    above = (2 * last - a) // (last + 1)
    at_fold = a // last
    ne_apart = ((2 * b + 2) % nlon + nlon - 1) // nlon
    nw_apart = ((2 * b) % nlon + nlon - 1) // nlon
    peers = 2 + 3 * below + 3 * above + at_fold * (1 + ne_apart + nw_apart)
    pl.semaphore_wait(barrier, peers)

    relations = [
        (a < last, a > 0, bot_b, hs, (a + 1, b)),
        (a > 0, a < last, top_b, hn, (a - 1, b)),
        (fold, fold, fold_b, hn, (last, mirror)),
        (True, True, lft_b, he, (a, left)),
        (True, True, rgt_b, hw, (a, right)),
        (a < last, a > 0, rgt_b.at[:, :, 1:2], cor.at[0], (a + 1, right)),
        (a < last, a > 0, lft_b.at[:, :, 0:1], cor.at[1], (a + 1, left)),
        (a > 0, a < last, rgt_b.at[:, :, 1:2], cor.at[2], (a - 1, right)),
        (a > 0, a < last, lft_b.at[:, :, 0:1], cor.at[3], (a - 1, left)),
        (fold & (ne != b), fold & (ne != b), rgt_b.at[:, :, 1:2], cor.at[3], (last, ne)),
        (fold & (nw != b), fold & (nw != b), lft_b.at[:, :, 0:1], cor.at[2], (last, nw)),
    ]
    copies = []
    for idx, (send, recv, src, dst, target) in enumerate(relations):
        copy = pltpu.make_async_remote_copy(
            src_ref=src, dst_ref=dst, send_sem=send_sem.at[idx], recv_sem=recv_sem.at[idx],
            device_id=dev(*target), device_id_type=pl.DeviceIdType.MESH)
        copies.append((send, recv, copy))
        when(send, copy.start)
    own = [
        (fold & (ne == b), pltpu.make_async_copy(rgt_b.at[:, :, 1:2], cor.at[3], local_sem.at[0])),
        (fold & (nw == b), pltpu.make_async_copy(lft_b.at[:, :, 0:1], cor.at[2], local_sem.at[1])),
    ]
    for cond, copy in own:
        when(cond, copy.start)
    for send, recv, copy in copies:
        when(send, copy.wait_send)
        when(recv, copy.wait_recv)
    for cond, copy in own:
        when(cond, copy.wait)
    hs_o[...] = hs[...]
    hn_o[...] = hn[...]
    hw_o[...] = hw[...]
    he_o[...] = he[...]
    cor_o[...] = cor[...]


def step_kernel(nlat, t_ref, s_ref, u_ref, v_ref, d_ref, f_ref, hs_ref, hn_ref, hw_ref, he_ref,
                cor_ref, to_ref, so_ref, uo_ref, vo_ref,
                base, vp1, vm1, vp2, vm2, accx, accy, mt, tf):
    k = pl.program_id(0)
    frame, width = base.shape[1], base.shape[2]
    rows = t_ref.shape[1]
    at_lat = lax.axis_index("lat")
    south = at_lat > 0
    fold = at_lat == nlat - 1

    @pl.when(k == 0)
    def _():
        base[...] = jnp.zeros_like(base)
        accx[...] = jnp.zeros_like(accx)
        accy[...] = jnp.zeros_like(accy)
        mt[...] = jnp.zeros_like(mt)
        tf[...] = jnp.zeros_like(tf)

    wet = jnp.where(d_ref[...] > k, 1.0, 0.0).astype(jnp.float32)
    lane = lax.broadcasted_iota(jnp.int32, (frame, width), 1)
    line_lane = lax.broadcasted_iota(jnp.int32, (1, width), 1)
    ins = (t_ref, s_ref, u_ref, v_ref)
    for n in range(4):
        base[n, top:top + rows, :] = ins[n][0] * wet
        base[n, top - 2:top, :] = jnp.where(south, hs_ref[n, k], 0.0)
        base[n, top + rows:top + rows + 2, :] = hn_ref[n, k]
        mt[0:2] = he_ref[n, k]
        mt[width - 2:width] = hw_ref[n, k]
        tf[top:top + rows] = jnp.transpose(mt[...])
        nw_raw = cor_ref[2, n, k]
        ne_raw = cor_ref[3, n, k]
        sw_line = cor_ref[0, n, k]
        se_line = pltpu.roll(cor_ref[1, n, k], 1, 1)
        nw_line = pltpu.roll(cor_ref[2, n, k], width - 1, 1)
        ne_line = cor_ref[3, n, k]
        low = jnp.where(line_lane == width - 1, sw_line, jnp.where(line_lane == 0, se_line, 0.0))
        high = jnp.where(line_lane == width - 1, nw_line, jnp.where(line_lane == 0, ne_line, 0.0))
        tf[top - 1:top] = jnp.where(south, low, 0.0)
        mirrored = jnp.where(line_lane == width - 1, nw_raw,
                             jnp.where(line_lane == 0, pltpu.roll(ne_raw, 1, 1), 0.0))
        tf[top + rows:top + rows + 1] = jnp.where(fold, signs[n] * mirrored, high)
        whole = base[n]
        edge = tf[...]
        vp1[n] = pltpu.roll(jnp.where(lane == 0, edge, whole), width - 1, 1)
        vm1[n] = pltpu.roll(jnp.where(lane == width - 1, edge, whole), 1, 1)
        vp2[n] = pltpu.roll(jnp.where(lane < 2, edge, whole), width - 2, 1)
        vm2[n] = pltpu.roll(jnp.where(lane >= width - 2, edge, whole), 2, 1)

    def at(ref, n, d):
        return ref[n, top + d:top + d + rows, :]

    centre = [at(base, n, 0) for n in range(4)]
    first, second = centre[2], centre[3]
    parts = []
    for n in range(4):
        east, west = at(vp1, n, 0), at(vm1, n, 0)
        north, south_ = at(base, n, 1), at(base, n, -1)
        carried = 0.5 * (first * (east - west) + second * (north - south_))
        smooth = (
            20.0 * centre[n]
            - 8.0 * (east + west + north + south_)
            + 2.0 * (at(vp1, n, 1) + at(vp1, n, -1) + at(vm1, n, 1) + at(vm1, n, -1))
            + at(base, n, 2) + at(base, n, -2) + at(vp2, n, 0) + at(vm2, n, 0)
        )
        parts.append((east, west, north, south_, carried, smooth))

    def density(a, b):
        return -0.2 * a + 0.8 * b

    dx = density(parts[0][0], parts[1][0]) - density(parts[0][1], parts[1][1])
    dy = density(parts[0][2], parts[1][2]) - density(parts[0][3], parts[1][3])
    totx = accx[...] + dx
    toty = accy[...] + dy
    accx[...] = totx
    accy[...] = toty
    grad_x = 0.5 * (totx - 0.5 * dx)
    grad_y = 0.5 * (toty - 0.5 * dy)
    coriolis = f_ref[...]
    to_ref[0] = (centre[0] - time_step * parts[0][4] - biharmonic * parts[0][5]) * wet
    so_ref[0] = (centre[1] - time_step * parts[1][4] - biharmonic * parts[1][5]) * wet
    uo_ref[0] = (
        first + time_step * (coriolis * second - grad_x - parts[2][4]) - biharmonic * parts[2][5]
    ) * wet
    vo_ref[0] = (
        second + time_step * (-coriolis * first - grad_y - parts[3][4]) - biharmonic * parts[3][5]
    ) * wet


def shards(axes, temp, salt, uvel, vvel, depth_levels):
    levels, rows_dev, cols_dev = temp.shape
    nlat = lax.axis_size("lat")
    nlon = lax.axis_size("lon")
    at_lat = lax.axis_index("lat")
    f32 = jnp.float32
    vmem = pl.BlockSpec(memory_space=pltpu.VMEM)
    strip = jax.ShapeDtypeStruct((4, levels, 2, cols_dev), f32)
    corners = jax.ShapeDtypeStruct((4, 4, levels, 1, cols_dev), f32)
    hs, hn, hw, he, cor = pl.pallas_call(
        functools.partial(exchange_kernel, axes, nlat, nlon),
        out_shape=[strip] * 4 + [corners],
        in_specs=[pl.BlockSpec(memory_space=pl.ANY)] * 5,
        out_specs=[vmem] * 5,
        scratch_shapes=[pltpu.VMEM((4,) + temp.shape, f32),
                        pltpu.VMEM(depth_levels.shape, jnp.int32)]
        + [pltpu.VMEM(strip.shape, f32)] * 9
        + [pltpu.VMEM(corners.shape, f32)]
        + [pltpu.SemaphoreType.DMA((11,)), pltpu.SemaphoreType.DMA((11,)),
           pltpu.SemaphoreType.DMA((5,)), pltpu.SemaphoreType.DMA((2,))],
        compiler_params=pltpu.CompilerParams(collective_id=0, has_side_effects=True),
    )(temp, salt, uvel, vvel, depth_levels)

    total_rows = rows_dev * nlat
    global_rows = (at_lat * rows_dev + jnp.arange(rows_dev, dtype=jnp.int32)).astype(f32)
    coriolis = (0.5 * jnp.sin(math.pi * (global_rows + 0.5) / total_rows - 0.5 * math.pi))[:, None]
    coriolis = jnp.broadcast_to(coriolis, (rows_dev, cols_dev))

    frame = rows_dev + 2 * top
    level_block = pl.BlockSpec((1, rows_dev, cols_dev), lambda k: (k, 0, 0))
    plane = pl.BlockSpec((rows_dev, cols_dev), lambda k: (0, 0))
    out = pl.pallas_call(
        functools.partial(step_kernel, nlat),
        grid=(levels,),
        in_specs=[level_block] * 4 + [plane] * 2 + [vmem] * 5,
        out_specs=[level_block] * 4,
        out_shape=[jax.ShapeDtypeStruct(temp.shape, f32)] * 4,
        scratch_shapes=[pltpu.VMEM((4, frame, cols_dev), f32)] * 5
        + [pltpu.VMEM((rows_dev, cols_dev), f32)] * 2
        + [pltpu.VMEM((cols_dev, cols_dev), f32), pltpu.VMEM((frame, cols_dev), f32)],
        compiler_params=pltpu.CompilerParams(dimension_semantics=("arbitrary",)),
    )(temp, salt, uvel, vvel, depth_levels, coriolis, hs, hn, hw, he, cor)
    return tuple(out)


def solution(mesh):
    placed = (
        P(None, "lat", "lon"),
        P(None, "lat", "lon"),
        P(None, "lat", "lon"),
        P(None, "lat", "lon"),
        P("lat", "lon"),
    )
    return jax.shard_map(
        functools.partial(shards, tuple(mesh.axis_names)),
        mesh=mesh,
        in_specs=placed,
        out_specs=(
            P(None, "lat", "lon"),
            P(None, "lat", "lon"),
            P(None, "lat", "lon"),
            P(None, "lat", "lon"),
        ),
        check_vma=False,
    )
```

```python
import functools
import math

import jax
import jax.numpy as jnp
from jax import lax
from jax.experimental import pallas as pl
from jax.experimental.pallas import tpu as pltpu
from jax.sharding import PartitionSpec as P

time_step = 0.2
biharmonic = 0.01
signs = (1.0, 1.0, -1.0, -1.0)
top = 8


def when(cond, fn):
    if cond is True:
        fn()
    else:
        pl.when(cond)(fn)


def reverse_lanes(x):
    lane = lax.broadcasted_iota(jnp.int32, x.shape, 1)
    width = x.shape[1]
    bit = 1
    while bit < width:
        x = jnp.where((lane & bit) != 0, pltpu.roll(x, bit, 1), pltpu.roll(x, width - bit, 1))
        bit *= 2
    return x


def exchange_kernel(axes, nlat, nlon, t_hbm, s_hbm, u_hbm, v_hbm, d_hbm,
                    hs_o, hn_o, hw_o, he_o, cor_o,
                    xin, d_ref, top_b, bot_b, fold_b, lft_b, rgt_b, hs, hn, hw, he, cor,
                    send_sem, recv_sem, in_sem, local_sem):
    a = lax.axis_index("lat")
    b = lax.axis_index("lon")
    last = nlat - 1
    levels, rows, cols = t_hbm.shape
    left = (b + nlon - 1) % nlon
    right = (b + 1) % nlon
    mirror = nlon - 1 - b
    ne = (2 * nlon - 2 - b) % nlon
    nw = (nlon - b) % nlon
    fold = a == last
    loads = [pltpu.make_async_copy(src, xin.at[n], in_sem.at[n])
             for n, src in enumerate((t_hbm, s_hbm, u_hbm, v_hbm))]
    loads.append(pltpu.make_async_copy(d_hbm, d_ref, in_sem.at[4]))
    for copy in loads:
        copy.start()

    def dev(la, lo):
        return tuple(la if ax == "lat" else lo for ax in axes)

    def zero_south():
        hs[...] = jnp.zeros_like(hs)
        cor[0] = jnp.zeros_like(cor[0])
        cor[1] = jnp.zeros_like(cor[1])

    when(a == 0, zero_south)

    partners = [
        (a < last, (a + 1, b)), (a > 0, (a - 1, b)), (True, (a, left)), (True, (a, right)),
        (a < last, (a + 1, right)), (a < last, (a + 1, left)),
        (a > 0, (a - 1, right)), (a > 0, (a - 1, left)),
        (fold, (last, mirror)), (fold & (ne != b), (last, ne)), (fold & (nw != b), (last, nw)),
    ]
    barrier = pltpu.get_barrier_semaphore()
    for cond, target in partners:
        when(cond, lambda target=target: pl.semaphore_signal(
            barrier, 1, device_id=dev(*target), device_id_type=pl.DeviceIdType.MESH))

    for copy in loads:
        copy.wait()

    def rows_body(k, carry):
        wet = jnp.where(d_ref[...] > k, 1.0, 0.0).astype(jnp.float32)
        for n in range(4):
            x = xin[n, k] * wet
            top_b[n, k] = x[0:2]
            bot_b[n, k] = x[rows - 2:rows]
            flipped = reverse_lanes(x[rows - 8:rows])
            fold_b[n, k, 0:1] = signs[n] * flipped[7:8]
            fold_b[n, k, 1:2] = signs[n] * flipped[6:7]
        return carry

    def cols_body(k, carry):
        wet = jnp.where(d_ref[...] > k, 1.0, 0.0).astype(jnp.float32)
        for n in range(4):
            xt = jnp.transpose(xin[n, k] * wet)
            lft_b[n, k] = xt[0:2]
            rgt_b[n, k] = xt[cols - 2:cols]
        return carry

    lax.fori_loop(0, levels, rows_body, 0)

    below = (a + last) // (last + 1)
    above = (2 * last - a) // (last + 1)
    at_fold = a // last
    ne_apart = ((2 * b + 2) % nlon + nlon - 1) // nlon
    nw_apart = ((2 * b) % nlon + nlon - 1) // nlon
    peers = 2 + 3 * below + 3 * above + at_fold * (1 + ne_apart + nw_apart)
    pl.semaphore_wait(barrier, peers)

    relations = [
        (a < last, a > 0, bot_b, hs, (a + 1, b)),
        (a > 0, a < last, top_b, hn, (a - 1, b)),
        (fold, fold, fold_b, hn, (last, mirror)),
        (True, True, lft_b, he, (a, left)),
        (True, True, rgt_b, hw, (a, right)),
        (a < last, a > 0, rgt_b.at[:, :, 1:2], cor.at[0], (a + 1, right)),
        (a < last, a > 0, lft_b.at[:, :, 0:1], cor.at[1], (a + 1, left)),
        (a > 0, a < last, rgt_b.at[:, :, 1:2], cor.at[2], (a - 1, right)),
        (a > 0, a < last, lft_b.at[:, :, 0:1], cor.at[3], (a - 1, left)),
        (fold & (ne != b), fold & (ne != b), rgt_b.at[:, :, 1:2], cor.at[3], (last, ne)),
        (fold & (nw != b), fold & (nw != b), lft_b.at[:, :, 0:1], cor.at[2], (last, nw)),
    ]
    copies = []
    for idx, (send, recv, src, dst, target) in enumerate(relations):
        if idx == 3:
            lax.fori_loop(0, levels, cols_body, 0)
        copy = pltpu.make_async_remote_copy(
            src_ref=src, dst_ref=dst, send_sem=send_sem.at[idx], recv_sem=recv_sem.at[idx],
            device_id=dev(*target), device_id_type=pl.DeviceIdType.MESH)
        copies.append((send, recv, copy))
        when(send, copy.start)
    own = [
        (fold & (ne == b), pltpu.make_async_copy(rgt_b.at[:, :, 1:2], cor.at[3], local_sem.at[0])),
        (fold & (nw == b), pltpu.make_async_copy(lft_b.at[:, :, 0:1], cor.at[2], local_sem.at[1])),
    ]
    for cond, copy in own:
        when(cond, copy.start)
    for send, recv, copy in copies:
        when(send, copy.wait_send)
        when(recv, copy.wait_recv)
    for cond, copy in own:
        when(cond, copy.wait)
    hs_o[...] = hs[...]
    hn_o[...] = hn[...]
    hw_o[...] = hw[...]
    he_o[...] = he[...]
    cor_o[...] = cor[...]


def step_kernel(nlat, t_ref, s_ref, u_ref, v_ref, d_ref, f_ref, hs_ref, hn_ref, hw_ref, he_ref,
                cor_ref, to_ref, so_ref, uo_ref, vo_ref,
                base, vp1, vm1, vp2, vm2, accx, accy, mt, tf):
    k = pl.program_id(0)
    frame, width = base.shape[1], base.shape[2]
    rows = t_ref.shape[1]
    at_lat = lax.axis_index("lat")
    south = at_lat > 0
    fold = at_lat == nlat - 1

    @pl.when(k == 0)
    def _():
        base[...] = jnp.zeros_like(base)
        accx[...] = jnp.zeros_like(accx)
        accy[...] = jnp.zeros_like(accy)
        mt[...] = jnp.zeros_like(mt)
        tf[...] = jnp.zeros_like(tf)

    wet = jnp.where(d_ref[...] > k, 1.0, 0.0).astype(jnp.float32)
    lane = lax.broadcasted_iota(jnp.int32, (frame, width), 1)
    line_lane = lax.broadcasted_iota(jnp.int32, (1, width), 1)
    ins = (t_ref, s_ref, u_ref, v_ref)
    for n in range(4):
        base[n, top:top + rows, :] = ins[n][0] * wet
        base[n, top - 2:top, :] = jnp.where(south, hs_ref[n, k], 0.0)
        base[n, top + rows:top + rows + 2, :] = hn_ref[n, k]
        mt[0:2] = he_ref[n, k]
        mt[width - 2:width] = hw_ref[n, k]
        tf[top:top + rows] = jnp.transpose(mt[...])
        nw_raw = cor_ref[2, n, k]
        ne_raw = cor_ref[3, n, k]
        sw_line = cor_ref[0, n, k]
        se_line = pltpu.roll(cor_ref[1, n, k], 1, 1)
        nw_line = pltpu.roll(cor_ref[2, n, k], width - 1, 1)
        ne_line = cor_ref[3, n, k]
        low = jnp.where(line_lane == width - 1, sw_line, jnp.where(line_lane == 0, se_line, 0.0))
        high = jnp.where(line_lane == width - 1, nw_line, jnp.where(line_lane == 0, ne_line, 0.0))
        tf[top - 1:top] = jnp.where(south, low, 0.0)
        mirrored = jnp.where(line_lane == width - 1, nw_raw,
                             jnp.where(line_lane == 0, pltpu.roll(ne_raw, 1, 1), 0.0))
        tf[top + rows:top + rows + 1] = jnp.where(fold, signs[n] * mirrored, high)
        whole = base[n]
        edge = tf[...]
        vp1[n] = pltpu.roll(jnp.where(lane == 0, edge, whole), width - 1, 1)
        vm1[n] = pltpu.roll(jnp.where(lane == width - 1, edge, whole), 1, 1)
        vp2[n] = pltpu.roll(jnp.where(lane < 2, edge, whole), width - 2, 1)
        vm2[n] = pltpu.roll(jnp.where(lane >= width - 2, edge, whole), 2, 1)

    def at(ref, n, d):
        return ref[n, top + d:top + d + rows, :]

    centre = [at(base, n, 0) for n in range(4)]
    first, second = centre[2], centre[3]
    parts = []
    for n in range(4):
        east, west = at(vp1, n, 0), at(vm1, n, 0)
        north, south_ = at(base, n, 1), at(base, n, -1)
        carried = 0.5 * (first * (east - west) + second * (north - south_))
        smooth = (
            20.0 * centre[n]
            - 8.0 * (east + west + north + south_)
            + 2.0 * (at(vp1, n, 1) + at(vp1, n, -1) + at(vm1, n, 1) + at(vm1, n, -1))
            + at(base, n, 2) + at(base, n, -2) + at(vp2, n, 0) + at(vm2, n, 0)
        )
        parts.append((east, west, north, south_, carried, smooth))

    def density(a, b):
        return -0.2 * a + 0.8 * b

    dx = density(parts[0][0], parts[1][0]) - density(parts[0][1], parts[1][1])
    dy = density(parts[0][2], parts[1][2]) - density(parts[0][3], parts[1][3])
    totx = accx[...] + dx
    toty = accy[...] + dy
    accx[...] = totx
    accy[...] = toty
    grad_x = 0.5 * (totx - 0.5 * dx)
    grad_y = 0.5 * (toty - 0.5 * dy)
    coriolis = jnp.broadcast_to(f_ref[...], (rows, width))
    to_ref[0] = (centre[0] - time_step * parts[0][4] - biharmonic * parts[0][5]) * wet
    so_ref[0] = (centre[1] - time_step * parts[1][4] - biharmonic * parts[1][5]) * wet
    uo_ref[0] = (
        first + time_step * (coriolis * second - grad_x - parts[2][4]) - biharmonic * parts[2][5]
    ) * wet
    vo_ref[0] = (
        second + time_step * (-coriolis * first - grad_y - parts[3][4]) - biharmonic * parts[3][5]
    ) * wet


def shards(axes, temp, salt, uvel, vvel, depth_levels):
    levels, rows_dev, cols_dev = temp.shape
    nlat = lax.axis_size("lat")
    nlon = lax.axis_size("lon")
    at_lat = lax.axis_index("lat")
    f32 = jnp.float32
    vmem = pl.BlockSpec(memory_space=pltpu.VMEM)
    strip = jax.ShapeDtypeStruct((4, levels, 2, cols_dev), f32)
    corners = jax.ShapeDtypeStruct((4, 4, levels, 1, cols_dev), f32)
    hs, hn, hw, he, cor = pl.pallas_call(
        functools.partial(exchange_kernel, axes, nlat, nlon),
        out_shape=[strip] * 4 + [corners],
        in_specs=[pl.BlockSpec(memory_space=pl.ANY)] * 5,
        out_specs=[vmem] * 5,
        scratch_shapes=[pltpu.VMEM((4,) + temp.shape, f32),
                        pltpu.VMEM(depth_levels.shape, jnp.int32)]
        + [pltpu.VMEM(strip.shape, f32)] * 9
        + [pltpu.VMEM(corners.shape, f32)]
        + [pltpu.SemaphoreType.DMA((11,)), pltpu.SemaphoreType.DMA((11,)),
           pltpu.SemaphoreType.DMA((5,)), pltpu.SemaphoreType.DMA((2,))],
        compiler_params=pltpu.CompilerParams(collective_id=0, has_side_effects=True),
    )(temp, salt, uvel, vvel, depth_levels)

    total_rows = rows_dev * nlat
    global_rows = (at_lat * rows_dev + jnp.arange(rows_dev, dtype=jnp.int32)).astype(f32)
    coriolis = (0.5 * jnp.sin(math.pi * (global_rows + 0.5) / total_rows - 0.5 * math.pi))[:, None]

    frame = rows_dev + 2 * top
    level_block = pl.BlockSpec((1, rows_dev, cols_dev), lambda k: (k, 0, 0))
    plane = pl.BlockSpec((rows_dev, cols_dev), lambda k: (0, 0))
    column = pl.BlockSpec((rows_dev, 1), lambda k: (0, 0))
    out = pl.pallas_call(
        functools.partial(step_kernel, nlat),
        grid=(levels,),
        in_specs=[level_block] * 4 + [plane, column] + [vmem] * 5,
        out_specs=[level_block] * 4,
        out_shape=[jax.ShapeDtypeStruct(temp.shape, f32)] * 4,
        scratch_shapes=[pltpu.VMEM((4, frame, cols_dev), f32)] * 5
        + [pltpu.VMEM((rows_dev, cols_dev), f32)] * 2
        + [pltpu.VMEM((cols_dev, cols_dev), f32), pltpu.VMEM((frame, cols_dev), f32)],
        compiler_params=pltpu.CompilerParams(dimension_semantics=("arbitrary",)),
    )(temp, salt, uvel, vvel, depth_levels, coriolis, hs, hn, hw, he, cor)
    return tuple(out)


def solution(mesh):
    placed = (
        P(None, "lat", "lon"),
        P(None, "lat", "lon"),
        P(None, "lat", "lon"),
        P(None, "lat", "lon"),
        P("lat", "lon"),
    )
    return jax.shard_map(
        functools.partial(shards, tuple(mesh.axis_names)),
        mesh=mesh,
        in_specs=placed,
        out_specs=(
            P(None, "lat", "lon"),
            P(None, "lat", "lon"),
            P(None, "lat", "lon"),
            P(None, "lat", "lon"),
        ),
        check_vma=False,
    )
```

```python
import functools
import math

import jax
import jax.numpy as jnp
from jax import lax
from jax.experimental import pallas as pl
from jax.experimental.pallas import tpu as pltpu
from jax.sharding import PartitionSpec as P

time_step = 0.2
biharmonic = 0.01
signs = (1.0, 1.0, -1.0, -1.0)
top = 8


def when(cond, fn):
    if cond is True:
        fn()
    else:
        pl.when(cond)(fn)


def reverse_lanes(x):
    lane = lax.broadcasted_iota(jnp.int32, x.shape, 1)
    width = x.shape[1]
    bit = 1
    while bit < width:
        x = jnp.where((lane & bit) != 0, pltpu.roll(x, bit, 1), pltpu.roll(x, width - bit, 1))
        bit *= 2
    return x


def exchange_kernel(axes, nlat, nlon, t_hbm, s_hbm, u_hbm, v_hbm, d_hbm,
                    hs_o, hn_o, hw_o, he_o, cor_o,
                    xin, d_ref, top_b, bot_b, fold_b, lft_b, rgt_b, hs, hn, hw, he, cor,
                    send_sem, recv_sem, in_sem, local_sem):
    a = lax.axis_index("lat")
    b = lax.axis_index("lon")
    last = nlat - 1
    levels, rows, cols = t_hbm.shape
    left = (b + nlon - 1) % nlon
    right = (b + 1) % nlon
    mirror = nlon - 1 - b
    ne = (2 * nlon - 2 - b) % nlon
    nw = (nlon - b) % nlon
    fold = a == last
    loads = [pltpu.make_async_copy(src, xin.at[n], in_sem.at[n])
             for n, src in enumerate((t_hbm, s_hbm, u_hbm, v_hbm))]
    loads.append(pltpu.make_async_copy(d_hbm, d_ref, in_sem.at[4]))
    for copy in loads:
        copy.start()

    def dev(la, lo):
        return tuple(la if ax == "lat" else lo for ax in axes)

    def zero_south():
        hs[...] = jnp.zeros_like(hs)
        cor[0] = jnp.zeros_like(cor[0])
        cor[1] = jnp.zeros_like(cor[1])

    when(a == 0, zero_south)

    partners = [
        (a < last, (a + 1, b)), (a > 0, (a - 1, b)), (True, (a, left)), (True, (a, right)),
        (a < last, (a + 1, right)), (a < last, (a + 1, left)),
        (a > 0, (a - 1, right)), (a > 0, (a - 1, left)),
        (fold, (last, mirror)), (fold & (ne != b), (last, ne)), (fold & (nw != b), (last, nw)),
    ]
    barrier = pltpu.get_barrier_semaphore()
    for cond, target in partners:
        when(cond, lambda target=target: pl.semaphore_signal(
            barrier, 1, device_id=dev(*target), device_id_type=pl.DeviceIdType.MESH))

    for copy in loads:
        copy.wait()

    def rows_body(k, carry):
        wet = jnp.where(d_ref[...] > k, 1.0, 0.0).astype(jnp.float32)
        for n in range(4):
            x = xin[n, k] * wet
            top_b[n, k] = x[0:2]
            bot_b[n, k] = x[rows - 2:rows]
            flipped = reverse_lanes(x[rows - 8:rows])
            fold_b[n, k, 0:1] = signs[n] * flipped[7:8]
            fold_b[n, k, 1:2] = signs[n] * flipped[6:7]
        return carry

    def cols_body(k, carry):
        wet = jnp.where(d_ref[...] > k, 1.0, 0.0).astype(jnp.float32)
        for n in range(4):
            xt = jnp.transpose(xin[n, k] * wet)
            lft_b[n, k] = xt[0:2]
            rgt_b[n, k] = xt[cols - 2:cols]
        return carry

    lax.fori_loop(0, levels, rows_body, 0)

    below = (a + last) // (last + 1)
    above = (2 * last - a) // (last + 1)
    at_fold = a // last
    ne_apart = ((2 * b + 2) % nlon + nlon - 1) // nlon
    nw_apart = ((2 * b) % nlon + nlon - 1) // nlon
    peers = 2 + 3 * below + 3 * above + at_fold * (1 + ne_apart + nw_apart)
    pl.semaphore_wait(barrier, peers)

    relations = [
        (a < last, a > 0, bot_b, hs, (a + 1, b)),
        (a > 0, a < last, top_b, hn, (a - 1, b)),
        (fold, fold, fold_b, hn, (last, mirror)),
        (True, True, lft_b, he, (a, left)),
        (True, True, rgt_b, hw, (a, right)),
        (a < last, a > 0, rgt_b.at[:, :, 1:2], cor.at[0], (a + 1, right)),
        (a < last, a > 0, lft_b.at[:, :, 0:1], cor.at[1], (a + 1, left)),
        (a > 0, a < last, rgt_b.at[:, :, 1:2], cor.at[2], (a - 1, right)),
        (a > 0, a < last, lft_b.at[:, :, 0:1], cor.at[3], (a - 1, left)),
        (fold & (ne != b), fold & (ne != b), rgt_b.at[:, :, 1:2], cor.at[3], (last, ne)),
        (fold & (nw != b), fold & (nw != b), lft_b.at[:, :, 0:1], cor.at[2], (last, nw)),
    ]
    copies = []
    for idx, (send, recv, src, dst, target) in enumerate(relations):
        if idx == 3:
            lax.fori_loop(0, levels, cols_body, 0)
        copy = pltpu.make_async_remote_copy(
            src_ref=src, dst_ref=dst, send_sem=send_sem.at[idx], recv_sem=recv_sem.at[idx],
            device_id=dev(*target), device_id_type=pl.DeviceIdType.MESH)
        copies.append((send, recv, copy))
        when(send, copy.start)
    own = [
        (fold & (ne == b), pltpu.make_async_copy(rgt_b.at[:, :, 1:2], cor.at[3], local_sem.at[0])),
        (fold & (nw == b), pltpu.make_async_copy(lft_b.at[:, :, 0:1], cor.at[2], local_sem.at[1])),
    ]
    for cond, copy in own:
        when(cond, copy.start)
    for send, recv, copy in copies:
        when(send, copy.wait_send)
        when(recv, copy.wait_recv)
    for cond, copy in own:
        when(cond, copy.wait)
    hs_o[...] = hs[...]
    hn_o[...] = hn[...]
    hw_o[...] = hw[...]
    he_o[...] = he[...]
    cor_o[...] = cor[...]


def step_kernel(nlat, t_ref, s_ref, u_ref, v_ref, d_ref, f_ref, hs_ref, hn_ref, hw_ref, he_ref,
                cor_ref, to_ref, so_ref, uo_ref, vo_ref,
                base, vp1, vm1, vp2, vm2, accx, accy, mt, tf):
    step = pl.program_id(0)
    per_step = t_ref.shape[0]
    frame, width = base.shape[1], base.shape[2]
    rows = t_ref.shape[1]
    at_lat = lax.axis_index("lat")
    south = at_lat > 0
    fold = at_lat == nlat - 1

    @pl.when(step == 0)
    def _():
        base[...] = jnp.zeros_like(base)
        accx[...] = jnp.zeros_like(accx)
        accy[...] = jnp.zeros_like(accy)
        mt[...] = jnp.zeros_like(mt)
        tf[...] = jnp.zeros_like(tf)

    for sub in range(per_step):
        k = step * per_step + sub
        wet = jnp.where(d_ref[...] > k, 1.0, 0.0).astype(jnp.float32)
        lane = lax.broadcasted_iota(jnp.int32, (frame, width), 1)
        line_lane = lax.broadcasted_iota(jnp.int32, (1, width), 1)
        ins = (t_ref, s_ref, u_ref, v_ref)
        for n in range(4):
            base[n, top:top + rows, :] = ins[n][sub] * wet
            base[n, top - 2:top, :] = jnp.where(south, hs_ref[n, k], 0.0)
            base[n, top + rows:top + rows + 2, :] = hn_ref[n, k]
            mt[0:2] = he_ref[n, k]
            mt[width - 2:width] = hw_ref[n, k]
            tf[top:top + rows] = jnp.transpose(mt[...])
            nw_raw = cor_ref[2, n, k]
            ne_raw = cor_ref[3, n, k]
            sw_line = cor_ref[0, n, k]
            se_line = pltpu.roll(cor_ref[1, n, k], 1, 1)
            nw_line = pltpu.roll(cor_ref[2, n, k], width - 1, 1)
            ne_line = cor_ref[3, n, k]
            low = jnp.where(line_lane == width - 1, sw_line, jnp.where(line_lane == 0, se_line, 0.0))
            high = jnp.where(line_lane == width - 1, nw_line, jnp.where(line_lane == 0, ne_line, 0.0))
            tf[top - 1:top] = jnp.where(south, low, 0.0)
            mirrored = jnp.where(line_lane == width - 1, nw_raw,
                                 jnp.where(line_lane == 0, pltpu.roll(ne_raw, 1, 1), 0.0))
            tf[top + rows:top + rows + 1] = jnp.where(fold, signs[n] * mirrored, high)
            whole = base[n]
            edge = tf[...]
            vp1[n] = pltpu.roll(jnp.where(lane == 0, edge, whole), width - 1, 1)
            vm1[n] = pltpu.roll(jnp.where(lane == width - 1, edge, whole), 1, 1)
            vp2[n] = pltpu.roll(jnp.where(lane < 2, edge, whole), width - 2, 1)
            vm2[n] = pltpu.roll(jnp.where(lane >= width - 2, edge, whole), 2, 1)

        def at(ref, n, d):
            return ref[n, top + d:top + d + rows, :]

        centre = [at(base, n, 0) for n in range(4)]
        first, second = centre[2], centre[3]
        parts = []
        for n in range(4):
            east, west = at(vp1, n, 0), at(vm1, n, 0)
            north, south_ = at(base, n, 1), at(base, n, -1)
            carried = 0.5 * (first * (east - west) + second * (north - south_))
            smooth = (
                20.0 * centre[n]
                - 8.0 * (east + west + north + south_)
                + 2.0 * (at(vp1, n, 1) + at(vp1, n, -1) + at(vm1, n, 1) + at(vm1, n, -1))
                + at(base, n, 2) + at(base, n, -2) + at(vp2, n, 0) + at(vm2, n, 0)
            )
            parts.append((east, west, north, south_, carried, smooth))

        def density(a, b):
            return -0.2 * a + 0.8 * b

        dx = density(parts[0][0], parts[1][0]) - density(parts[0][1], parts[1][1])
        dy = density(parts[0][2], parts[1][2]) - density(parts[0][3], parts[1][3])
        totx = accx[...] + dx
        toty = accy[...] + dy
        accx[...] = totx
        accy[...] = toty
        grad_x = 0.5 * (totx - 0.5 * dx)
        grad_y = 0.5 * (toty - 0.5 * dy)
        coriolis = jnp.broadcast_to(f_ref[...], (rows, width))
        to_ref[sub] = (centre[0] - time_step * parts[0][4] - biharmonic * parts[0][5]) * wet
        so_ref[sub] = (centre[1] - time_step * parts[1][4] - biharmonic * parts[1][5]) * wet
        uo_ref[sub] = (
            first + time_step * (coriolis * second - grad_x - parts[2][4]) - biharmonic * parts[2][5]
        ) * wet
        vo_ref[sub] = (
            second + time_step * (-coriolis * first - grad_y - parts[3][4]) - biharmonic * parts[3][5]
        ) * wet


def shards(axes, temp, salt, uvel, vvel, depth_levels):
    levels, rows_dev, cols_dev = temp.shape
    nlat = lax.axis_size("lat")
    nlon = lax.axis_size("lon")
    at_lat = lax.axis_index("lat")
    f32 = jnp.float32
    vmem = pl.BlockSpec(memory_space=pltpu.VMEM)
    strip = jax.ShapeDtypeStruct((4, levels, 2, cols_dev), f32)
    corners = jax.ShapeDtypeStruct((4, 4, levels, 1, cols_dev), f32)
    hs, hn, hw, he, cor = pl.pallas_call(
        functools.partial(exchange_kernel, axes, nlat, nlon),
        out_shape=[strip] * 4 + [corners],
        in_specs=[pl.BlockSpec(memory_space=pl.ANY)] * 5,
        out_specs=[vmem] * 5,
        scratch_shapes=[pltpu.VMEM((4,) + temp.shape, f32),
                        pltpu.VMEM(depth_levels.shape, jnp.int32)]
        + [pltpu.VMEM(strip.shape, f32)] * 9
        + [pltpu.VMEM(corners.shape, f32)]
        + [pltpu.SemaphoreType.DMA((11,)), pltpu.SemaphoreType.DMA((11,)),
           pltpu.SemaphoreType.DMA((5,)), pltpu.SemaphoreType.DMA((2,))],
        compiler_params=pltpu.CompilerParams(collective_id=0, has_side_effects=True),
    )(temp, salt, uvel, vvel, depth_levels)

    total_rows = rows_dev * nlat
    global_rows = (at_lat * rows_dev + jnp.arange(rows_dev, dtype=jnp.int32)).astype(f32)
    coriolis = (0.5 * jnp.sin(math.pi * (global_rows + 0.5) / total_rows - 0.5 * math.pi))[:, None]

    frame = rows_dev + 2 * top
    per_step = 2
    level_block = pl.BlockSpec((per_step, rows_dev, cols_dev), lambda k: (k, 0, 0))
    plane = pl.BlockSpec((rows_dev, cols_dev), lambda k: (0, 0))
    column = pl.BlockSpec((rows_dev, 1), lambda k: (0, 0))
    out = pl.pallas_call(
        functools.partial(step_kernel, nlat),
        grid=(levels // per_step,),
        in_specs=[level_block] * 4 + [plane, column] + [vmem] * 5,
        out_specs=[level_block] * 4,
        out_shape=[jax.ShapeDtypeStruct(temp.shape, f32)] * 4,
        scratch_shapes=[pltpu.VMEM((4, frame, cols_dev), f32)] * 5
        + [pltpu.VMEM((rows_dev, cols_dev), f32)] * 2
        + [pltpu.VMEM((cols_dev, cols_dev), f32), pltpu.VMEM((frame, cols_dev), f32)],
        compiler_params=pltpu.CompilerParams(dimension_semantics=("arbitrary",)),
    )(temp, salt, uvel, vvel, depth_levels, coriolis, hs, hn, hw, he, cor)
    return tuple(out)


def solution(mesh):
    placed = (
        P(None, "lat", "lon"),
        P(None, "lat", "lon"),
        P(None, "lat", "lon"),
        P(None, "lat", "lon"),
        P("lat", "lon"),
    )
    return jax.shard_map(
        functools.partial(shards, tuple(mesh.axis_names)),
        mesh=mesh,
        in_specs=placed,
        out_specs=(
            P(None, "lat", "lon"),
            P(None, "lat", "lon"),
            P(None, "lat", "lon"),
            P(None, "lat", "lon"),
        ),
        check_vma=False,
    )
```

```python
import functools
import math

import jax
import jax.numpy as jnp
from jax import lax
from jax.experimental import pallas as pl
from jax.experimental.pallas import tpu as pltpu
from jax.sharding import PartitionSpec as P

time_step = 0.2
biharmonic = 0.01
signs = (1.0, 1.0, -1.0, -1.0)
top = 8


def when(cond, fn):
    if cond is True:
        fn()
    else:
        pl.when(cond)(fn)


def reverse_lanes(x):
    lane = lax.broadcasted_iota(jnp.int32, x.shape, 1)
    width = x.shape[1]
    bit = 1
    while bit < width:
        x = jnp.where((lane & bit) != 0, pltpu.roll(x, bit, 1), pltpu.roll(x, width - bit, 1))
        bit *= 2
    return x


def exchange_kernel(axes, nlat, nlon, t_hbm, s_hbm, u_hbm, v_hbm, d_hbm,
                    hs_o, hn_o, hw_o, he_o, cor_o,
                    xin, d_ref, top_b, bot_b, fold_b, lft_b, rgt_b, hs, hn, hw, he, cor,
                    send_sem, recv_sem, in_sem, local_sem):
    a = lax.axis_index("lat")
    b = lax.axis_index("lon")
    last = nlat - 1
    levels, rows, cols = t_hbm.shape
    left = (b + nlon - 1) % nlon
    right = (b + 1) % nlon
    mirror = nlon - 1 - b
    ne = (2 * nlon - 2 - b) % nlon
    nw = (nlon - b) % nlon
    fold = a == last
    loads = [pltpu.make_async_copy(src, xin.at[n], in_sem.at[n])
             for n, src in enumerate((t_hbm, s_hbm, u_hbm, v_hbm))]
    loads.append(pltpu.make_async_copy(d_hbm, d_ref, in_sem.at[4]))
    for copy in loads:
        copy.start()

    def dev(la, lo):
        return tuple(la if ax == "lat" else lo for ax in axes)

    def zero_south():
        hs[...] = jnp.zeros_like(hs)
        cor[0] = jnp.zeros_like(cor[0])
        cor[1] = jnp.zeros_like(cor[1])

    when(a == 0, zero_south)

    partners = [
        (a < last, (a + 1, b)), (a > 0, (a - 1, b)), (True, (a, left)), (True, (a, right)),
        (a < last, (a + 1, right)), (a < last, (a + 1, left)),
        (a > 0, (a - 1, right)), (a > 0, (a - 1, left)),
        (fold, (last, mirror)), (fold & (ne != b), (last, ne)), (fold & (nw != b), (last, nw)),
    ]
    barrier = pltpu.get_barrier_semaphore()
    for cond, target in partners:
        when(cond, lambda target=target: pl.semaphore_signal(
            barrier, 1, device_id=dev(*target), device_id_type=pl.DeviceIdType.MESH))

    for copy in loads:
        copy.wait()

    def rows_body(k, carry):
        wet = jnp.where(d_ref[...] > k, 1.0, 0.0).astype(jnp.float32)
        for n in range(4):
            x = xin[n, k] * wet
            top_b[n, k] = x[0:2]
            bot_b[n, k] = x[rows - 2:rows]
            flipped = reverse_lanes(x[rows - 8:rows])
            fold_b[n, k, 0:1] = signs[n] * flipped[7:8]
            fold_b[n, k, 1:2] = signs[n] * flipped[6:7]
        return carry

    def cols_body(k, carry):
        wet = jnp.where(d_ref[...] > k, 1.0, 0.0).astype(jnp.float32)
        for n in range(4):
            xt = jnp.transpose(xin[n, k] * wet)
            lft_b[n, k] = xt[0:2]
            rgt_b[n, k] = xt[cols - 2:cols]
        return carry

    lax.fori_loop(0, levels, rows_body, 0)

    below = (a + last) // (last + 1)
    above = (2 * last - a) // (last + 1)
    at_fold = a // last
    ne_apart = ((2 * b + 2) % nlon + nlon - 1) // nlon
    nw_apart = ((2 * b) % nlon + nlon - 1) // nlon
    peers = 2 + 3 * below + 3 * above + at_fold * (1 + ne_apart + nw_apart)
    pl.semaphore_wait(barrier, peers)

    relations = [
        (a < last, a > 0, bot_b, hs, (a + 1, b)),
        (a > 0, a < last, top_b, hn, (a - 1, b)),
        (fold, fold, fold_b, hn, (last, mirror)),
        (True, True, lft_b, he, (a, left)),
        (True, True, rgt_b, hw, (a, right)),
        (a < last, a > 0, rgt_b.at[:, :, 1:2], cor.at[0], (a + 1, right)),
        (a < last, a > 0, lft_b.at[:, :, 0:1], cor.at[1], (a + 1, left)),
        (a > 0, a < last, rgt_b.at[:, :, 1:2], cor.at[2], (a - 1, right)),
        (a > 0, a < last, lft_b.at[:, :, 0:1], cor.at[3], (a - 1, left)),
        (fold & (ne != b), fold & (ne != b), rgt_b.at[:, :, 1:2], cor.at[3], (last, ne)),
        (fold & (nw != b), fold & (nw != b), lft_b.at[:, :, 0:1], cor.at[2], (last, nw)),
    ]
    copies = []
    for idx, (send, recv, src, dst, target) in enumerate(relations):
        if idx == 3:
            lax.fori_loop(0, levels, cols_body, 0)
        copy = pltpu.make_async_remote_copy(
            src_ref=src, dst_ref=dst, send_sem=send_sem.at[idx], recv_sem=recv_sem.at[idx],
            device_id=dev(*target), device_id_type=pl.DeviceIdType.MESH)
        copies.append((send, recv, copy))
        when(send, copy.start)
    own = [
        (fold & (ne == b), pltpu.make_async_copy(rgt_b.at[:, :, 1:2], cor.at[3], local_sem.at[0])),
        (fold & (nw == b), pltpu.make_async_copy(lft_b.at[:, :, 0:1], cor.at[2], local_sem.at[1])),
    ]
    for cond, copy in own:
        when(cond, copy.start)
    for send, recv, copy in copies:
        when(send, copy.wait_send)
        when(recv, copy.wait_recv)
    for cond, copy in own:
        when(cond, copy.wait)
    hs_o[...] = hs[...]
    hn_o[...] = hn[...]
    hw_o[...] = hw[...]
    he_o[...] = he[...]
    cor_o[...] = cor[...]


def step_kernel(nlat, t_ref, s_ref, u_ref, v_ref, d_ref, f_ref, hs_ref, hn_ref, hw_ref, he_ref,
                cor_ref, to_ref, so_ref, uo_ref, vo_ref,
                base, vp1, vm1, vp2, vm2, accx, accy, mt, tf):
    step = pl.program_id(0)
    per_step = t_ref.shape[0]
    frame, width = base.shape[1], base.shape[2]
    rows = t_ref.shape[1]
    at_lat = lax.axis_index("lat")
    south = at_lat > 0
    fold = at_lat == nlat - 1

    @pl.when(step == 0)
    def _():
        base[...] = jnp.zeros_like(base)
        accx[...] = jnp.zeros_like(accx)
        accy[...] = jnp.zeros_like(accy)
        mt[...] = jnp.zeros_like(mt)
        tf[...] = jnp.zeros_like(tf)

    for sub in range(per_step):
        k = step * per_step + sub
        wet = jnp.where(d_ref[...] > k, 1.0, 0.0).astype(jnp.float32)
        lane = lax.broadcasted_iota(jnp.int32, (frame, width), 1)
        line_lane = lax.broadcasted_iota(jnp.int32, (1, width), 1)
        ins = (t_ref, s_ref, u_ref, v_ref)
        for n in range(4):
            base[n, top:top + rows, :] = ins[n][sub] * wet
            base[n, top - 2:top, :] = jnp.where(south, hs_ref[n, k], 0.0)
            base[n, top + rows:top + rows + 2, :] = hn_ref[n, k]
            mt[0:2] = he_ref[n, k]
            mt[width - 2:width] = hw_ref[n, k]
            tf[top:top + rows] = jnp.transpose(mt[...])
            nw_raw = cor_ref[2, n, k]
            ne_raw = cor_ref[3, n, k]
            sw_line = cor_ref[0, n, k]
            se_line = pltpu.roll(cor_ref[1, n, k], 1, 1)
            nw_line = pltpu.roll(cor_ref[2, n, k], width - 1, 1)
            ne_line = cor_ref[3, n, k]
            low = jnp.where(line_lane == width - 1, sw_line, jnp.where(line_lane == 0, se_line, 0.0))
            high = jnp.where(line_lane == width - 1, nw_line, jnp.where(line_lane == 0, ne_line, 0.0))
            tf[top - 1:top] = jnp.where(south, low, 0.0)
            mirrored = jnp.where(line_lane == width - 1, nw_raw,
                                 jnp.where(line_lane == 0, pltpu.roll(ne_raw, 1, 1), 0.0))
            tf[top + rows:top + rows + 1] = jnp.where(fold, signs[n] * mirrored, high)
            whole = base[n]
            edge = tf[...]
            vp1[n] = pltpu.roll(jnp.where(lane == 0, edge, whole), width - 1, 1)
            vm1[n] = pltpu.roll(jnp.where(lane == width - 1, edge, whole), 1, 1)
            vp2[n] = pltpu.roll(jnp.where(lane < 2, edge, whole), width - 2, 1)
            vm2[n] = pltpu.roll(jnp.where(lane >= width - 2, edge, whole), 2, 1)

        def at(ref, n, d):
            return ref[n, top + d:top + d + rows, :]

        centre = [at(base, n, 0) for n in range(4)]
        first, second = centre[2], centre[3]
        parts = []
        for n in range(4):
            east, west = at(vp1, n, 0), at(vm1, n, 0)
            north, south_ = at(base, n, 1), at(base, n, -1)
            carried = 0.5 * (first * (east - west) + second * (north - south_))
            smooth = (
                20.0 * centre[n]
                - 8.0 * (east + west + north + south_)
                + 2.0 * (at(vp1, n, 1) + at(vp1, n, -1) + at(vm1, n, 1) + at(vm1, n, -1))
                + at(base, n, 2) + at(base, n, -2) + at(vp2, n, 0) + at(vm2, n, 0)
            )
            parts.append((east, west, north, south_, carried, smooth))

        def density(a, b):
            return -0.2 * a + 0.8 * b

        dx = density(parts[0][0], parts[1][0]) - density(parts[0][1], parts[1][1])
        dy = density(parts[0][2], parts[1][2]) - density(parts[0][3], parts[1][3])
        totx = accx[...] + dx
        toty = accy[...] + dy
        accx[...] = totx
        accy[...] = toty
        grad_x = 0.5 * (totx - 0.5 * dx)
        grad_y = 0.5 * (toty - 0.5 * dy)
        coriolis = jnp.broadcast_to(f_ref[...], (rows, width))
        to_ref[sub] = (centre[0] - time_step * parts[0][4] - biharmonic * parts[0][5]) * wet
        so_ref[sub] = (centre[1] - time_step * parts[1][4] - biharmonic * parts[1][5]) * wet
        uo_ref[sub] = (
            first + time_step * (coriolis * second - grad_x - parts[2][4]) - biharmonic * parts[2][5]
        ) * wet
        vo_ref[sub] = (
            second + time_step * (-coriolis * first - grad_y - parts[3][4]) - biharmonic * parts[3][5]
        ) * wet


def shards(axes, temp, salt, uvel, vvel, depth_levels):
    levels, rows_dev, cols_dev = temp.shape
    nlat = lax.axis_size("lat")
    nlon = lax.axis_size("lon")
    at_lat = lax.axis_index("lat")
    f32 = jnp.float32
    vmem = pl.BlockSpec(memory_space=pltpu.VMEM)
    strip = jax.ShapeDtypeStruct((4, levels, 2, cols_dev), f32)
    corners = jax.ShapeDtypeStruct((4, 4, levels, 1, cols_dev), f32)
    hs, hn, hw, he, cor = pl.pallas_call(
        functools.partial(exchange_kernel, axes, nlat, nlon),
        out_shape=[strip] * 4 + [corners],
        in_specs=[pl.BlockSpec(memory_space=pl.ANY)] * 5,
        out_specs=[vmem] * 5,
        scratch_shapes=[pltpu.VMEM((4,) + temp.shape, f32),
                        pltpu.VMEM(depth_levels.shape, jnp.int32)]
        + [pltpu.VMEM(strip.shape, f32)] * 9
        + [pltpu.VMEM(corners.shape, f32)]
        + [pltpu.SemaphoreType.DMA((11,)), pltpu.SemaphoreType.DMA((11,)),
           pltpu.SemaphoreType.DMA((5,)), pltpu.SemaphoreType.DMA((2,))],
        compiler_params=pltpu.CompilerParams(collective_id=0, has_side_effects=True),
    )(temp, salt, uvel, vvel, depth_levels)

    total_rows = rows_dev * nlat
    global_rows = (at_lat * rows_dev + jnp.arange(rows_dev, dtype=jnp.int32)).astype(f32)
    coriolis = (0.5 * jnp.sin(math.pi * (global_rows + 0.5) / total_rows - 0.5 * math.pi))[:, None]

    frame = rows_dev + 2 * top
    per_step = 4
    level_block = pl.BlockSpec((per_step, rows_dev, cols_dev), lambda k: (k, 0, 0))
    plane = pl.BlockSpec((rows_dev, cols_dev), lambda k: (0, 0))
    column = pl.BlockSpec((rows_dev, 1), lambda k: (0, 0))
    out = pl.pallas_call(
        functools.partial(step_kernel, nlat),
        grid=(levels // per_step,),
        in_specs=[level_block] * 4 + [plane, column] + [vmem] * 5,
        out_specs=[level_block] * 4,
        out_shape=[jax.ShapeDtypeStruct(temp.shape, f32)] * 4,
        scratch_shapes=[pltpu.VMEM((4, frame, cols_dev), f32)] * 5
        + [pltpu.VMEM((rows_dev, cols_dev), f32)] * 2
        + [pltpu.VMEM((cols_dev, cols_dev), f32), pltpu.VMEM((frame, cols_dev), f32)],
        compiler_params=pltpu.CompilerParams(dimension_semantics=("arbitrary",)),
    )(temp, salt, uvel, vvel, depth_levels, coriolis, hs, hn, hw, he, cor)
    return tuple(out)


def solution(mesh):
    placed = (
        P(None, "lat", "lon"),
        P(None, "lat", "lon"),
        P(None, "lat", "lon"),
        P(None, "lat", "lon"),
        P("lat", "lon"),
    )
    return jax.shard_map(
        functools.partial(shards, tuple(mesh.axis_names)),
        mesh=mesh,
        in_specs=placed,
        out_specs=(
            P(None, "lat", "lon"),
            P(None, "lat", "lon"),
            P(None, "lat", "lon"),
            P(None, "lat", "lon"),
        ),
        check_vma=False,
    )
```

```python
import functools
import math

import jax
import jax.numpy as jnp
from jax import lax
from jax.experimental import pallas as pl
from jax.experimental.pallas import tpu as pltpu
from jax.sharding import PartitionSpec as P

time_step = 0.2
biharmonic = 0.01
signs = (1.0, 1.0, -1.0, -1.0)
top = 8


def when(cond, fn):
    if cond is True:
        fn()
    else:
        pl.when(cond)(fn)


def reverse_lanes(x):
    lane = lax.broadcasted_iota(jnp.int32, x.shape, 1)
    width = x.shape[1]
    bit = 1
    while bit < width:
        x = jnp.where((lane & bit) != 0, pltpu.roll(x, bit, 1), pltpu.roll(x, width - bit, 1))
        bit *= 2
    return x


def exchange_kernel(axes, nlat, nlon, t_hbm, s_hbm, u_hbm, v_hbm, d_hbm,
                    hs_o, hn_o, hw_o, he_o, cor_o,
                    xin, d_ref, top_b, bot_b, fold_b, lft_b, rgt_b, hs, hn, hw, he, cor,
                    send_sem, recv_sem, in_sem, local_sem):
    a = lax.axis_index("lat")
    b = lax.axis_index("lon")
    last = nlat - 1
    levels, rows, cols = t_hbm.shape
    left = (b + nlon - 1) % nlon
    right = (b + 1) % nlon
    mirror = nlon - 1 - b
    ne = (2 * nlon - 2 - b) % nlon
    nw = (nlon - b) % nlon
    fold = a == last
    loads = [pltpu.make_async_copy(src, xin.at[n], in_sem.at[n])
             for n, src in enumerate((t_hbm, s_hbm, u_hbm, v_hbm))]
    loads.append(pltpu.make_async_copy(d_hbm, d_ref, in_sem.at[4]))
    for copy in loads:
        copy.start()

    def dev(la, lo):
        return tuple(la if ax == "lat" else lo for ax in axes)

    def zero_south():
        hs[...] = jnp.zeros_like(hs)
        cor[0] = jnp.zeros_like(cor[0])
        cor[1] = jnp.zeros_like(cor[1])

    when(a == 0, zero_south)

    partners = [
        (a < last, (a + 1, b)), (a > 0, (a - 1, b)), (True, (a, left)), (True, (a, right)),
        (a < last, (a + 1, right)), (a < last, (a + 1, left)),
        (a > 0, (a - 1, right)), (a > 0, (a - 1, left)),
        (fold, (last, mirror)), (fold & (ne != b), (last, ne)), (fold & (nw != b), (last, nw)),
    ]
    barrier = pltpu.get_barrier_semaphore()
    for cond, target in partners:
        when(cond, lambda target=target: pl.semaphore_signal(
            barrier, 1, device_id=dev(*target), device_id_type=pl.DeviceIdType.MESH))

    for copy in loads:
        copy.wait()

    def rows_body(k, carry):
        wet = jnp.where(d_ref[...] > k, 1.0, 0.0).astype(jnp.float32)
        for n in range(4):
            x = xin[n, k] * wet
            top_b[n, k] = x[0:2]
            bot_b[n, k] = x[rows - 2:rows]
            flipped = reverse_lanes(x[rows - 8:rows])
            fold_b[n, k, 0:1] = signs[n] * flipped[7:8]
            fold_b[n, k, 1:2] = signs[n] * flipped[6:7]
        return carry

    group = cols // 16

    def cols_body(g, carry):
        lane = lax.broadcasted_iota(jnp.int32, (rows, cols), 1)
        packed = jnp.zeros((rows, cols), jnp.float32)
        for kk in range(group):
            k = g * group + kk
            wet = jnp.where(d_ref[...] > k, 1.0, 0.0).astype(jnp.float32)
            for n in range(4):
                slot = 16 * kk + 4 * n
                x = xin[n, k] * wet
                packed = jnp.where((lane >= slot) & (lane < slot + 4),
                                   pltpu.roll(x, (slot + 2) % cols, 1), packed)
        pt = jnp.transpose(packed)
        for kk in range(group):
            k = g * group + kk
            for n in range(4):
                slot = 16 * kk + 4 * n
                rgt_b[n, k] = pt[slot:slot + 2]
                lft_b[n, k] = pt[slot + 2:slot + 4]
        return carry

    lax.fori_loop(0, levels, rows_body, 0)

    below = (a + last) // (last + 1)
    above = (2 * last - a) // (last + 1)
    at_fold = a // last
    ne_apart = ((2 * b + 2) % nlon + nlon - 1) // nlon
    nw_apart = ((2 * b) % nlon + nlon - 1) // nlon
    peers = 2 + 3 * below + 3 * above + at_fold * (1 + ne_apart + nw_apart)
    pl.semaphore_wait(barrier, peers)

    relations = [
        (a < last, a > 0, bot_b, hs, (a + 1, b)),
        (a > 0, a < last, top_b, hn, (a - 1, b)),
        (fold, fold, fold_b, hn, (last, mirror)),
        (True, True, lft_b, he, (a, left)),
        (True, True, rgt_b, hw, (a, right)),
        (a < last, a > 0, rgt_b.at[:, :, 1:2], cor.at[0], (a + 1, right)),
        (a < last, a > 0, lft_b.at[:, :, 0:1], cor.at[1], (a + 1, left)),
        (a > 0, a < last, rgt_b.at[:, :, 1:2], cor.at[2], (a - 1, right)),
        (a > 0, a < last, lft_b.at[:, :, 0:1], cor.at[3], (a - 1, left)),
        (fold & (ne != b), fold & (ne != b), rgt_b.at[:, :, 1:2], cor.at[3], (last, ne)),
        (fold & (nw != b), fold & (nw != b), lft_b.at[:, :, 0:1], cor.at[2], (last, nw)),
    ]
    copies = []
    for idx, (send, recv, src, dst, target) in enumerate(relations):
        if idx == 3:
            lax.fori_loop(0, levels // group, cols_body, 0)
        copy = pltpu.make_async_remote_copy(
            src_ref=src, dst_ref=dst, send_sem=send_sem.at[idx], recv_sem=recv_sem.at[idx],
            device_id=dev(*target), device_id_type=pl.DeviceIdType.MESH)
        copies.append((send, recv, copy))
        when(send, copy.start)
    own = [
        (fold & (ne == b), pltpu.make_async_copy(rgt_b.at[:, :, 1:2], cor.at[3], local_sem.at[0])),
        (fold & (nw == b), pltpu.make_async_copy(lft_b.at[:, :, 0:1], cor.at[2], local_sem.at[1])),
    ]
    for cond, copy in own:
        when(cond, copy.start)
    for send, recv, copy in copies:
        when(send, copy.wait_send)
        when(recv, copy.wait_recv)
    for cond, copy in own:
        when(cond, copy.wait)
    hs_o[...] = hs[...]
    hn_o[...] = hn[...]
    hw_o[...] = hw[...]
    he_o[...] = he[...]
    cor_o[...] = cor[...]


def step_kernel(nlat, t_ref, s_ref, u_ref, v_ref, d_ref, f_ref, hs_ref, hn_ref, hw_ref, he_ref,
                cor_ref, to_ref, so_ref, uo_ref, vo_ref,
                base, vp1, vm1, vp2, vm2, accx, accy, mt, tf):
    step = pl.program_id(0)
    per_step = t_ref.shape[0]
    frame, width = base.shape[1], base.shape[2]
    rows = t_ref.shape[1]
    at_lat = lax.axis_index("lat")
    south = at_lat > 0
    fold = at_lat == nlat - 1

    @pl.when(step == 0)
    def _():
        base[...] = jnp.zeros_like(base)
        accx[...] = jnp.zeros_like(accx)
        accy[...] = jnp.zeros_like(accy)
        mt[...] = jnp.zeros_like(mt)
        tf[...] = jnp.zeros_like(tf)

    for sub in range(per_step):
        k = step * per_step + sub
        wet = jnp.where(d_ref[...] > k, 1.0, 0.0).astype(jnp.float32)
        lane = lax.broadcasted_iota(jnp.int32, (frame, width), 1)
        line_lane = lax.broadcasted_iota(jnp.int32, (1, width), 1)
        ins = (t_ref, s_ref, u_ref, v_ref)
        for n in range(4):
            base[n, top:top + rows, :] = ins[n][sub] * wet
            base[n, top - 2:top, :] = jnp.where(south, hs_ref[n, k], 0.0)
            base[n, top + rows:top + rows + 2, :] = hn_ref[n, k]
            mt[0:2] = he_ref[n, k]
            mt[width - 2:width] = hw_ref[n, k]
            tf[top:top + rows] = jnp.transpose(mt[...])
            nw_raw = cor_ref[2, n, k]
            ne_raw = cor_ref[3, n, k]
            sw_line = cor_ref[0, n, k]
            se_line = pltpu.roll(cor_ref[1, n, k], 1, 1)
            nw_line = pltpu.roll(cor_ref[2, n, k], width - 1, 1)
            ne_line = cor_ref[3, n, k]
            low = jnp.where(line_lane == width - 1, sw_line, jnp.where(line_lane == 0, se_line, 0.0))
            high = jnp.where(line_lane == width - 1, nw_line, jnp.where(line_lane == 0, ne_line, 0.0))
            tf[top - 1:top] = jnp.where(south, low, 0.0)
            mirrored = jnp.where(line_lane == width - 1, nw_raw,
                                 jnp.where(line_lane == 0, pltpu.roll(ne_raw, 1, 1), 0.0))
            tf[top + rows:top + rows + 1] = jnp.where(fold, signs[n] * mirrored, high)
            whole = base[n]
            edge = tf[...]
            vp1[n] = pltpu.roll(jnp.where(lane == 0, edge, whole), width - 1, 1)
            vm1[n] = pltpu.roll(jnp.where(lane == width - 1, edge, whole), 1, 1)
            vp2[n] = pltpu.roll(jnp.where(lane < 2, edge, whole), width - 2, 1)
            vm2[n] = pltpu.roll(jnp.where(lane >= width - 2, edge, whole), 2, 1)

        def at(ref, n, d):
            return ref[n, top + d:top + d + rows, :]

        centre = [at(base, n, 0) for n in range(4)]
        first, second = centre[2], centre[3]
        parts = []
        for n in range(4):
            east, west = at(vp1, n, 0), at(vm1, n, 0)
            north, south_ = at(base, n, 1), at(base, n, -1)
            carried = 0.5 * (first * (east - west) + second * (north - south_))
            smooth = (
                20.0 * centre[n]
                - 8.0 * (east + west + north + south_)
                + 2.0 * (at(vp1, n, 1) + at(vp1, n, -1) + at(vm1, n, 1) + at(vm1, n, -1))
                + at(base, n, 2) + at(base, n, -2) + at(vp2, n, 0) + at(vm2, n, 0)
            )
            parts.append((east, west, north, south_, carried, smooth))

        def density(a, b):
            return -0.2 * a + 0.8 * b

        dx = density(parts[0][0], parts[1][0]) - density(parts[0][1], parts[1][1])
        dy = density(parts[0][2], parts[1][2]) - density(parts[0][3], parts[1][3])
        totx = accx[...] + dx
        toty = accy[...] + dy
        accx[...] = totx
        accy[...] = toty
        grad_x = 0.5 * (totx - 0.5 * dx)
        grad_y = 0.5 * (toty - 0.5 * dy)
        coriolis = jnp.broadcast_to(f_ref[...], (rows, width))
        to_ref[sub] = (centre[0] - time_step * parts[0][4] - biharmonic * parts[0][5]) * wet
        so_ref[sub] = (centre[1] - time_step * parts[1][4] - biharmonic * parts[1][5]) * wet
        uo_ref[sub] = (
            first + time_step * (coriolis * second - grad_x - parts[2][4]) - biharmonic * parts[2][5]
        ) * wet
        vo_ref[sub] = (
            second + time_step * (-coriolis * first - grad_y - parts[3][4]) - biharmonic * parts[3][5]
        ) * wet


def shards(axes, temp, salt, uvel, vvel, depth_levels):
    levels, rows_dev, cols_dev = temp.shape
    nlat = lax.axis_size("lat")
    nlon = lax.axis_size("lon")
    at_lat = lax.axis_index("lat")
    f32 = jnp.float32
    vmem = pl.BlockSpec(memory_space=pltpu.VMEM)
    strip = jax.ShapeDtypeStruct((4, levels, 2, cols_dev), f32)
    corners = jax.ShapeDtypeStruct((4, 4, levels, 1, cols_dev), f32)
    hs, hn, hw, he, cor = pl.pallas_call(
        functools.partial(exchange_kernel, axes, nlat, nlon),
        out_shape=[strip] * 4 + [corners],
        in_specs=[pl.BlockSpec(memory_space=pl.ANY)] * 5,
        out_specs=[vmem] * 5,
        scratch_shapes=[pltpu.VMEM((4,) + temp.shape, f32),
                        pltpu.VMEM(depth_levels.shape, jnp.int32)]
        + [pltpu.VMEM(strip.shape, f32)] * 9
        + [pltpu.VMEM(corners.shape, f32)]
        + [pltpu.SemaphoreType.DMA((11,)), pltpu.SemaphoreType.DMA((11,)),
           pltpu.SemaphoreType.DMA((5,)), pltpu.SemaphoreType.DMA((2,))],
        compiler_params=pltpu.CompilerParams(collective_id=0, has_side_effects=True),
    )(temp, salt, uvel, vvel, depth_levels)

    total_rows = rows_dev * nlat
    global_rows = (at_lat * rows_dev + jnp.arange(rows_dev, dtype=jnp.int32)).astype(f32)
    coriolis = (0.5 * jnp.sin(math.pi * (global_rows + 0.5) / total_rows - 0.5 * math.pi))[:, None]

    frame = rows_dev + 2 * top
    per_step = 4
    level_block = pl.BlockSpec((per_step, rows_dev, cols_dev), lambda k: (k, 0, 0))
    plane = pl.BlockSpec((rows_dev, cols_dev), lambda k: (0, 0))
    column = pl.BlockSpec((rows_dev, 1), lambda k: (0, 0))
    out = pl.pallas_call(
        functools.partial(step_kernel, nlat),
        grid=(levels // per_step,),
        in_specs=[level_block] * 4 + [plane, column] + [vmem] * 5,
        out_specs=[level_block] * 4,
        out_shape=[jax.ShapeDtypeStruct(temp.shape, f32)] * 4,
        scratch_shapes=[pltpu.VMEM((4, frame, cols_dev), f32)] * 5
        + [pltpu.VMEM((rows_dev, cols_dev), f32)] * 2
        + [pltpu.VMEM((cols_dev, cols_dev), f32), pltpu.VMEM((frame, cols_dev), f32)],
        compiler_params=pltpu.CompilerParams(dimension_semantics=("arbitrary",)),
    )(temp, salt, uvel, vvel, depth_levels, coriolis, hs, hn, hw, he, cor)
    return tuple(out)


def solution(mesh):
    placed = (
        P(None, "lat", "lon"),
        P(None, "lat", "lon"),
        P(None, "lat", "lon"),
        P(None, "lat", "lon"),
        P("lat", "lon"),
    )
    return jax.shard_map(
        functools.partial(shards, tuple(mesh.axis_names)),
        mesh=mesh,
        in_specs=placed,
        out_specs=(
            P(None, "lat", "lon"),
            P(None, "lat", "lon"),
            P(None, "lat", "lon"),
            P(None, "lat", "lon"),
        ),
        check_vma=False,
    )
```

```python
import functools
import math

import jax
import jax.numpy as jnp
from jax import lax
from jax.experimental import pallas as pl
from jax.experimental.pallas import tpu as pltpu
from jax.sharding import PartitionSpec as P

time_step = 0.2
biharmonic = 0.01
signs = (1.0, 1.0, -1.0, -1.0)
top = 8


def when(cond, fn):
    if cond is True:
        fn()
    else:
        pl.when(cond)(fn)


def reverse_lanes(x):
    lane = lax.broadcasted_iota(jnp.int32, x.shape, 1)
    width = x.shape[1]
    bit = 1
    while bit < width:
        x = jnp.where((lane & bit) != 0, pltpu.roll(x, bit, 1), pltpu.roll(x, width - bit, 1))
        bit *= 2
    return x


def exchange_kernel(axes, nlat, nlon, t_hbm, s_hbm, u_hbm, v_hbm, d_hbm,
                    hs_o, hn_o, hw_o, he_o, cor_o,
                    xin, d_ref, top_b, bot_b, fold_b, lft_b, rgt_b, lc, rc, hs, hn, hw, he, cor,
                    send_sem, recv_sem, in_sem, local_sem):
    a = lax.axis_index("lat")
    b = lax.axis_index("lon")
    last = nlat - 1
    levels, rows, cols = t_hbm.shape
    left = (b + nlon - 1) % nlon
    right = (b + 1) % nlon
    mirror = nlon - 1 - b
    ne = (2 * nlon - 2 - b) % nlon
    nw = (nlon - b) % nlon
    fold = a == last
    loads = [pltpu.make_async_copy(src, xin.at[n], in_sem.at[n])
             for n, src in enumerate((t_hbm, s_hbm, u_hbm, v_hbm))]
    loads.append(pltpu.make_async_copy(d_hbm, d_ref, in_sem.at[4]))
    for copy in loads:
        copy.start()

    def dev(la, lo):
        return tuple(la if ax == "lat" else lo for ax in axes)

    def zero_south():
        hs[...] = jnp.zeros_like(hs)
        cor[0] = jnp.zeros_like(cor[0])
        cor[1] = jnp.zeros_like(cor[1])

    when(a == 0, zero_south)
    lc[...] = jnp.zeros_like(lc)
    rc[...] = jnp.zeros_like(rc)

    partners = [
        (a < last, (a + 1, b)), (a > 0, (a - 1, b)), (True, (a, left)), (True, (a, right)),
        (a < last, (a + 1, right)), (a < last, (a + 1, left)),
        (a > 0, (a - 1, right)), (a > 0, (a - 1, left)),
        (fold, (last, mirror)), (fold & (ne != b), (last, ne)), (fold & (nw != b), (last, nw)),
    ]
    barrier = pltpu.get_barrier_semaphore()
    for cond, target in partners:
        when(cond, lambda target=target: pl.semaphore_signal(
            barrier, 1, device_id=dev(*target), device_id_type=pl.DeviceIdType.MESH))

    for copy in loads:
        copy.wait()

    def rows_body(k, carry):
        wet = jnp.where(d_ref[...] > k, 1.0, 0.0).astype(jnp.float32)
        for n in range(4):
            x = xin[n, k] * wet
            top_b[k, 2 * n:2 * n + 2] = x[0:2]
            bot_b[k, 2 * n:2 * n + 2] = x[rows - 2:rows]
            flipped = reverse_lanes(x[rows - 8:rows])
            fold_b[k, 2 * n:2 * n + 1] = signs[n] * flipped[7:8]
            fold_b[k, 2 * n + 1:2 * n + 2] = signs[n] * flipped[6:7]
        return carry

    group = cols // 16

    def cols_body(g, carry):
        lane = lax.broadcasted_iota(jnp.int32, (rows, cols), 1)
        packed = jnp.zeros((rows, cols), jnp.float32)
        for kk in range(group):
            k = g * group + kk
            wet = jnp.where(d_ref[...] > k, 1.0, 0.0).astype(jnp.float32)
            for n in range(4):
                slot = 16 * kk + 4 * n
                x = xin[n, k] * wet
                packed = jnp.where((lane >= slot) & (lane < slot + 4),
                                   pltpu.roll(x, (slot + 2) % cols, 1), packed)
        pt = jnp.transpose(packed)
        for kk in range(group):
            k = g * group + kk
            for n in range(4):
                slot = 16 * kk + 4 * n
                rgt_b[k, 2 * n:2 * n + 2] = pt[slot:slot + 2]
                lft_b[k, 2 * n:2 * n + 2] = pt[slot + 2:slot + 4]
                rc[k, n:n + 1] = pt[slot + 1:slot + 2]
                lc[k, n:n + 1] = pt[slot + 2:slot + 3]
        return carry

    lax.fori_loop(0, levels, rows_body, 0)

    below = (a + last) // (last + 1)
    above = (2 * last - a) // (last + 1)
    at_fold = a // last
    ne_apart = ((2 * b + 2) % nlon + nlon - 1) // nlon
    nw_apart = ((2 * b) % nlon + nlon - 1) // nlon
    peers = 2 + 3 * below + 3 * above + at_fold * (1 + ne_apart + nw_apart)
    pl.semaphore_wait(barrier, peers)

    relations = [
        (a < last, a > 0, bot_b, hs, (a + 1, b)),
        (a > 0, a < last, top_b, hn, (a - 1, b)),
        (fold, fold, fold_b, hn, (last, mirror)),
        (True, True, lft_b, he, (a, left)),
        (True, True, rgt_b, hw, (a, right)),
        (a < last, a > 0, rc, cor.at[0], (a + 1, right)),
        (a < last, a > 0, lc, cor.at[1], (a + 1, left)),
        (a > 0, a < last, rc, cor.at[2], (a - 1, right)),
        (a > 0, a < last, lc, cor.at[3], (a - 1, left)),
        (fold & (ne != b), fold & (ne != b), rc, cor.at[3], (last, ne)),
        (fold & (nw != b), fold & (nw != b), lc, cor.at[2], (last, nw)),
    ]
    copies = []
    for idx, (send, recv, src, dst, target) in enumerate(relations):
        if idx == 3:
            lax.fori_loop(0, levels // group, cols_body, 0)
        copy = pltpu.make_async_remote_copy(
            src_ref=src, dst_ref=dst, send_sem=send_sem.at[idx], recv_sem=recv_sem.at[idx],
            device_id=dev(*target), device_id_type=pl.DeviceIdType.MESH)
        copies.append((send, recv, copy))
        when(send, copy.start)
    own = [
        (fold & (ne == b), pltpu.make_async_copy(rc, cor.at[3], local_sem.at[0])),
        (fold & (nw == b), pltpu.make_async_copy(lc, cor.at[2], local_sem.at[1])),
    ]
    for cond, copy in own:
        when(cond, copy.start)
    for send, recv, copy in copies:
        when(send, copy.wait_send)
        when(recv, copy.wait_recv)
    for cond, copy in own:
        when(cond, copy.wait)
    hs_o[...] = hs[...]
    hn_o[...] = hn[...]
    hw_o[...] = hw[...]
    he_o[...] = he[...]
    cor_o[...] = cor[...]


def step_kernel(nlat, t_ref, s_ref, u_ref, v_ref, d_ref, f_ref, hs_ref, hn_ref, hw_ref, he_ref,
                cor_ref, to_ref, so_ref, uo_ref, vo_ref,
                base, vp1, vm1, vp2, vm2, accx, accy, mt, tf):
    step = pl.program_id(0)
    per_step = t_ref.shape[0]
    frame, width = base.shape[1], base.shape[2]
    rows = t_ref.shape[1]
    at_lat = lax.axis_index("lat")
    south = at_lat > 0
    fold = at_lat == nlat - 1

    @pl.when(step == 0)
    def _():
        base[...] = jnp.zeros_like(base)
        accx[...] = jnp.zeros_like(accx)
        accy[...] = jnp.zeros_like(accy)
        mt[...] = jnp.zeros_like(mt)
        tf[...] = jnp.zeros_like(tf)

    for sub in range(per_step):
        k = step * per_step + sub
        wet = jnp.where(d_ref[...] > k, 1.0, 0.0).astype(jnp.float32)
        lane = lax.broadcasted_iota(jnp.int32, (frame, width), 1)
        line_lane = lax.broadcasted_iota(jnp.int32, (1, width), 1)
        ins = (t_ref, s_ref, u_ref, v_ref)
        for n in range(4):
            base[n, top:top + rows, :] = ins[n][sub] * wet
            base[n, top - 2:top, :] = jnp.where(south, hs_ref[k, 2 * n:2 * n + 2], 0.0)
            base[n, top + rows:top + rows + 2, :] = hn_ref[k, 2 * n:2 * n + 2]
            mt[0:2] = he_ref[k, 2 * n:2 * n + 2]
            mt[width - 2:width] = hw_ref[k, 2 * n:2 * n + 2]
            tf[top:top + rows] = jnp.transpose(mt[...])
            nw_raw = cor_ref[2, k, n:n + 1]
            ne_raw = cor_ref[3, k, n:n + 1]
            sw_line = cor_ref[0, k, n:n + 1]
            se_line = pltpu.roll(cor_ref[1, k, n:n + 1], 1, 1)
            nw_line = pltpu.roll(nw_raw, width - 1, 1)
            ne_line = ne_raw
            low = jnp.where(line_lane == width - 1, sw_line, jnp.where(line_lane == 0, se_line, 0.0))
            high = jnp.where(line_lane == width - 1, nw_line, jnp.where(line_lane == 0, ne_line, 0.0))
            tf[top - 1:top] = jnp.where(south, low, 0.0)
            mirrored = jnp.where(line_lane == width - 1, nw_raw,
                                 jnp.where(line_lane == 0, pltpu.roll(ne_raw, 1, 1), 0.0))
            tf[top + rows:top + rows + 1] = jnp.where(fold, signs[n] * mirrored, high)
            whole = base[n]
            edge = tf[...]
            vp1[n] = pltpu.roll(jnp.where(lane == 0, edge, whole), width - 1, 1)
            vm1[n] = pltpu.roll(jnp.where(lane == width - 1, edge, whole), 1, 1)
            vp2[n] = pltpu.roll(jnp.where(lane < 2, edge, whole), width - 2, 1)
            vm2[n] = pltpu.roll(jnp.where(lane >= width - 2, edge, whole), 2, 1)

        def at(ref, n, d):
            return ref[n, top + d:top + d + rows, :]

        centre = [at(base, n, 0) for n in range(4)]
        first, second = centre[2], centre[3]
        parts = []
        for n in range(4):
            east, west = at(vp1, n, 0), at(vm1, n, 0)
            north, south_ = at(base, n, 1), at(base, n, -1)
            carried = 0.5 * (first * (east - west) + second * (north - south_))
            smooth = (
                20.0 * centre[n]
                - 8.0 * (east + west + north + south_)
                + 2.0 * (at(vp1, n, 1) + at(vp1, n, -1) + at(vm1, n, 1) + at(vm1, n, -1))
                + at(base, n, 2) + at(base, n, -2) + at(vp2, n, 0) + at(vm2, n, 0)
            )
            parts.append((east, west, north, south_, carried, smooth))

        def density(a, b):
            return -0.2 * a + 0.8 * b

        dx = density(parts[0][0], parts[1][0]) - density(parts[0][1], parts[1][1])
        dy = density(parts[0][2], parts[1][2]) - density(parts[0][3], parts[1][3])
        totx = accx[...] + dx
        toty = accy[...] + dy
        accx[...] = totx
        accy[...] = toty
        grad_x = 0.5 * (totx - 0.5 * dx)
        grad_y = 0.5 * (toty - 0.5 * dy)
        coriolis = jnp.broadcast_to(f_ref[...], (rows, width))
        to_ref[sub] = (centre[0] - time_step * parts[0][4] - biharmonic * parts[0][5]) * wet
        so_ref[sub] = (centre[1] - time_step * parts[1][4] - biharmonic * parts[1][5]) * wet
        uo_ref[sub] = (
            first + time_step * (coriolis * second - grad_x - parts[2][4]) - biharmonic * parts[2][5]
        ) * wet
        vo_ref[sub] = (
            second + time_step * (-coriolis * first - grad_y - parts[3][4]) - biharmonic * parts[3][5]
        ) * wet


def shards(axes, temp, salt, uvel, vvel, depth_levels):
    levels, rows_dev, cols_dev = temp.shape
    nlat = lax.axis_size("lat")
    nlon = lax.axis_size("lon")
    at_lat = lax.axis_index("lat")
    f32 = jnp.float32
    vmem = pl.BlockSpec(memory_space=pltpu.VMEM)
    strip = jax.ShapeDtypeStruct((levels, 8, cols_dev), f32)
    corners = jax.ShapeDtypeStruct((4, levels, 8, cols_dev), f32)
    hs, hn, hw, he, cor = pl.pallas_call(
        functools.partial(exchange_kernel, axes, nlat, nlon),
        out_shape=[strip] * 4 + [corners],
        in_specs=[pl.BlockSpec(memory_space=pl.ANY)] * 5,
        out_specs=[vmem] * 5,
        scratch_shapes=[pltpu.VMEM((4,) + temp.shape, f32),
                        pltpu.VMEM(depth_levels.shape, jnp.int32)]
        + [pltpu.VMEM(strip.shape, f32)] * 11
        + [pltpu.VMEM(corners.shape, f32)]
        + [pltpu.SemaphoreType.DMA((11,)), pltpu.SemaphoreType.DMA((11,)),
           pltpu.SemaphoreType.DMA((5,)), pltpu.SemaphoreType.DMA((2,))],
        compiler_params=pltpu.CompilerParams(collective_id=0, has_side_effects=True),
    )(temp, salt, uvel, vvel, depth_levels)

    total_rows = rows_dev * nlat
    global_rows = (at_lat * rows_dev + jnp.arange(rows_dev, dtype=jnp.int32)).astype(f32)
    coriolis = (0.5 * jnp.sin(math.pi * (global_rows + 0.5) / total_rows - 0.5 * math.pi))[:, None]

    frame = rows_dev + 2 * top
    per_step = 4
    level_block = pl.BlockSpec((per_step, rows_dev, cols_dev), lambda k: (k, 0, 0))
    plane = pl.BlockSpec((rows_dev, cols_dev), lambda k: (0, 0))
    column = pl.BlockSpec((rows_dev, 1), lambda k: (0, 0))
    out = pl.pallas_call(
        functools.partial(step_kernel, nlat),
        grid=(levels // per_step,),
        in_specs=[level_block] * 4 + [plane, column] + [vmem] * 5,
        out_specs=[level_block] * 4,
        out_shape=[jax.ShapeDtypeStruct(temp.shape, f32)] * 4,
        scratch_shapes=[pltpu.VMEM((4, frame, cols_dev), f32)] * 5
        + [pltpu.VMEM((rows_dev, cols_dev), f32)] * 2
        + [pltpu.VMEM((cols_dev, cols_dev), f32), pltpu.VMEM((frame, cols_dev), f32)],
        compiler_params=pltpu.CompilerParams(dimension_semantics=("arbitrary",)),
    )(temp, salt, uvel, vvel, depth_levels, coriolis, hs, hn, hw, he, cor)
    return tuple(out)


def solution(mesh):
    placed = (
        P(None, "lat", "lon"),
        P(None, "lat", "lon"),
        P(None, "lat", "lon"),
        P(None, "lat", "lon"),
        P("lat", "lon"),
    )
    return jax.shard_map(
        functools.partial(shards, tuple(mesh.axis_names)),
        mesh=mesh,
        in_specs=placed,
        out_specs=(
            P(None, "lat", "lon"),
            P(None, "lat", "lon"),
            P(None, "lat", "lon"),
            P(None, "lat", "lon"),
        ),
        check_vma=False,
    )
```

```python
import functools
import math

import jax
import jax.numpy as jnp
from jax import lax
from jax.experimental import pallas as pl
from jax.experimental.pallas import tpu as pltpu
from jax.sharding import PartitionSpec as P

time_step = 0.2
biharmonic = 0.01
signs = (1.0, 1.0, -1.0, -1.0)
top = 8


def when(cond, fn):
    if cond is True:
        fn()
    else:
        pl.when(cond)(fn)


def reverse_lanes(x):
    lane = lax.broadcasted_iota(jnp.int32, x.shape, 1)
    width = x.shape[1]
    bit = 1
    while bit < width:
        x = jnp.where((lane & bit) != 0, pltpu.roll(x, bit, 1), pltpu.roll(x, width - bit, 1))
        bit *= 2
    return x


def exchange_kernel(axes, nlat, nlon, t_hbm, s_hbm, u_hbm, v_hbm, d_hbm,
                    hs_o, hn_o, hw_o, he_o, cor_o,
                    xin, d_ref, top_b, bot_b, fold_b, lft_b, rgt_b, hs, hn, hw, he, csrc, cor,
                    send_sem, recv_sem, in_sem, local_sem):
    a = lax.axis_index("lat")
    b = lax.axis_index("lon")
    last = nlat - 1
    levels, rows, cols = t_hbm.shape
    left = (b + nlon - 1) % nlon
    right = (b + 1) % nlon
    mirror = nlon - 1 - b
    ne = (2 * nlon - 2 - b) % nlon
    nw = (nlon - b) % nlon
    fold = a == last
    loads = [pltpu.make_async_copy(src, xin.at[n], in_sem.at[n])
             for n, src in enumerate((t_hbm, s_hbm, u_hbm, v_hbm))]
    loads.append(pltpu.make_async_copy(d_hbm, d_ref, in_sem.at[4]))
    for copy in loads:
        copy.start()

    def dev(la, lo):
        return tuple(la if ax == "lat" else lo for ax in axes)

    def zero_south():
        hs[...] = jnp.zeros_like(hs)
        cor[0] = jnp.zeros_like(cor[0])
        cor[1] = jnp.zeros_like(cor[1])

    when(a == 0, zero_south)
    csrc[...] = jnp.zeros_like(csrc)

    partners = [
        (a < last, (a + 1, b)), (a > 0, (a - 1, b)), (True, (a, left)), (True, (a, right)),
        (a < last, (a + 1, right)), (a < last, (a + 1, left)),
        (a > 0, (a - 1, right)), (a > 0, (a - 1, left)),
        (fold, (last, mirror)), (fold & (ne != b), (last, ne)), (fold & (nw != b), (last, nw)),
    ]
    barrier = pltpu.get_barrier_semaphore()
    for cond, target in partners:
        when(cond, lambda target=target: pl.semaphore_signal(
            barrier, 1, device_id=dev(*target), device_id_type=pl.DeviceIdType.MESH))

    for copy in loads:
        copy.wait()

    def rows_body(k, carry):
        wet = jnp.where(d_ref[...] > k, 1.0, 0.0).astype(jnp.float32)
        for n in range(4):
            x = xin[n, k] * wet
            top_b[n, k] = x[0:2]
            bot_b[n, k] = x[rows - 2:rows]
            flipped = reverse_lanes(x[rows - 8:rows])
            fold_b[n, k, 0:1] = signs[n] * flipped[7:8]
            fold_b[n, k, 1:2] = signs[n] * flipped[6:7]
        return carry

    group = cols // 16

    def cols_body(g, carry):
        lane = lax.broadcasted_iota(jnp.int32, (rows, cols), 1)
        packed = jnp.zeros((rows, cols), jnp.float32)
        for kk in range(group):
            k = g * group + kk
            wet = jnp.where(d_ref[...] > k, 1.0, 0.0).astype(jnp.float32)
            for n in range(4):
                slot = 16 * kk + 4 * n
                x = xin[n, k] * wet
                packed = jnp.where((lane >= slot) & (lane < slot + 4),
                                   pltpu.roll(x, (slot + 2) % cols, 1), packed)
        pt = jnp.transpose(packed)
        csrc[g, 0:1] = packed[0:1]
        csrc[g, 1:2] = packed[rows - 1:rows]
        for kk in range(group):
            k = g * group + kk
            for n in range(4):
                slot = 16 * kk + 4 * n
                rgt_b[n, k] = pt[slot:slot + 2]
                lft_b[n, k] = pt[slot + 2:slot + 4]
        return carry

    lax.fori_loop(0, levels, rows_body, 0)

    below = (a + last) // (last + 1)
    above = (2 * last - a) // (last + 1)
    at_fold = a // last
    ne_apart = ((2 * b + 2) % nlon + nlon - 1) // nlon
    nw_apart = ((2 * b) % nlon + nlon - 1) // nlon
    peers = 2 + 3 * below + 3 * above + at_fold * (1 + ne_apart + nw_apart)
    pl.semaphore_wait(barrier, peers)

    relations = [
        (a < last, a > 0, bot_b, hs, (a + 1, b)),
        (a > 0, a < last, top_b, hn, (a - 1, b)),
        (fold, fold, fold_b, hn, (last, mirror)),
        (True, True, lft_b, he, (a, left)),
        (True, True, rgt_b, hw, (a, right)),
        (a < last, a > 0, csrc, cor.at[0], (a + 1, right)),
        (a < last, a > 0, csrc, cor.at[1], (a + 1, left)),
        (a > 0, a < last, csrc, cor.at[2], (a - 1, right)),
        (a > 0, a < last, csrc, cor.at[3], (a - 1, left)),
        (fold & (ne != b), fold & (ne != b), csrc, cor.at[3], (last, ne)),
        (fold & (nw != b), fold & (nw != b), csrc, cor.at[2], (last, nw)),
    ]
    copies = []
    for idx, (send, recv, src, dst, target) in enumerate(relations):
        if idx == 3:
            lax.fori_loop(0, levels // group, cols_body, 0)
        copy = pltpu.make_async_remote_copy(
            src_ref=src, dst_ref=dst, send_sem=send_sem.at[idx], recv_sem=recv_sem.at[idx],
            device_id=dev(*target), device_id_type=pl.DeviceIdType.MESH)
        copies.append((send, recv, copy))
        when(send, copy.start)
    own = [
        (fold & (ne == b), pltpu.make_async_copy(csrc, cor.at[3], local_sem.at[0])),
        (fold & (nw == b), pltpu.make_async_copy(csrc, cor.at[2], local_sem.at[1])),
    ]
    for cond, copy in own:
        when(cond, copy.start)
    for send, recv, copy in copies:
        when(send, copy.wait_send)
        when(recv, copy.wait_recv)
    for cond, copy in own:
        when(cond, copy.wait)
    hs_o[...] = hs[...]
    hn_o[...] = hn[...]
    hw_o[...] = hw[...]
    he_o[...] = he[...]
    cor_o[...] = cor[...]


def step_kernel(nlat, t_ref, s_ref, u_ref, v_ref, d_ref, f_ref, hs_ref, hn_ref, hw_ref, he_ref,
                cor_ref, to_ref, so_ref, uo_ref, vo_ref,
                base, vp1, vm1, vp2, vm2, accx, accy, mt, tf):
    step = pl.program_id(0)
    per_step = t_ref.shape[0]
    frame, width = base.shape[1], base.shape[2]
    rows = t_ref.shape[1]
    at_lat = lax.axis_index("lat")
    south = at_lat > 0
    fold = at_lat == nlat - 1

    @pl.when(step == 0)
    def _():
        base[...] = jnp.zeros_like(base)
        accx[...] = jnp.zeros_like(accx)
        accy[...] = jnp.zeros_like(accy)
        mt[...] = jnp.zeros_like(mt)
        tf[...] = jnp.zeros_like(tf)

    for sub in range(per_step):
        k = step * per_step + sub
        wet = jnp.where(d_ref[...] > k, 1.0, 0.0).astype(jnp.float32)
        lane = lax.broadcasted_iota(jnp.int32, (frame, width), 1)
        line_lane = lax.broadcasted_iota(jnp.int32, (1, width), 1)
        ins = (t_ref, s_ref, u_ref, v_ref)
        for n in range(4):
            base[n, top:top + rows, :] = ins[n][sub] * wet
            base[n, top - 2:top, :] = jnp.where(south, hs_ref[n, k], 0.0)
            base[n, top + rows:top + rows + 2, :] = hn_ref[n, k]
            mt[0:2] = he_ref[n, k]
            mt[width - 2:width] = hw_ref[n, k]
            tf[top:top + rows] = jnp.transpose(mt[...])
            slot = 16 * sub + 4 * n

            def to_lane(line, src, dst):
                return pltpu.roll(line, (dst - src) % width, 1)

            sw_line = to_lane(cor_ref[0, step, 1:2], slot + 1, width - 1)
            se_line = to_lane(cor_ref[1, step, 1:2], slot + 2, 0)
            nw_line = to_lane(cor_ref[2, step, 0:1], slot + 1, width - 1)
            ne_line = to_lane(cor_ref[3, step, 0:1], slot + 2, 0)
            nw_raw = to_lane(cor_ref[2, step, 1:2], slot + 2, width - 1)
            ne_raw = to_lane(cor_ref[3, step, 1:2], slot + 1, 0)
            low = jnp.where(line_lane == width - 1, sw_line, jnp.where(line_lane == 0, se_line, 0.0))
            high = jnp.where(line_lane == width - 1, nw_line, jnp.where(line_lane == 0, ne_line, 0.0))
            tf[top - 1:top] = jnp.where(south, low, 0.0)
            mirrored = jnp.where(line_lane == width - 1, nw_raw,
                                 jnp.where(line_lane == 0, ne_raw, 0.0))
            tf[top + rows:top + rows + 1] = jnp.where(fold, signs[n] * mirrored, high)
            whole = base[n]
            edge = tf[...]
            vp1[n] = pltpu.roll(jnp.where(lane == 0, edge, whole), width - 1, 1)
            vm1[n] = pltpu.roll(jnp.where(lane == width - 1, edge, whole), 1, 1)
            vp2[n] = pltpu.roll(jnp.where(lane < 2, edge, whole), width - 2, 1)
            vm2[n] = pltpu.roll(jnp.where(lane >= width - 2, edge, whole), 2, 1)

        def at(ref, n, d):
            return ref[n, top + d:top + d + rows, :]

        centre = [at(base, n, 0) for n in range(4)]
        first, second = centre[2], centre[3]
        parts = []
        for n in range(4):
            east, west = at(vp1, n, 0), at(vm1, n, 0)
            north, south_ = at(base, n, 1), at(base, n, -1)
            carried = 0.5 * (first * (east - west) + second * (north - south_))
            smooth = (
                20.0 * centre[n]
                - 8.0 * (east + west + north + south_)
                + 2.0 * (at(vp1, n, 1) + at(vp1, n, -1) + at(vm1, n, 1) + at(vm1, n, -1))
                + at(base, n, 2) + at(base, n, -2) + at(vp2, n, 0) + at(vm2, n, 0)
            )
            parts.append((east, west, north, south_, carried, smooth))

        def density(a, b):
            return -0.2 * a + 0.8 * b

        dx = density(parts[0][0], parts[1][0]) - density(parts[0][1], parts[1][1])
        dy = density(parts[0][2], parts[1][2]) - density(parts[0][3], parts[1][3])
        totx = accx[...] + dx
        toty = accy[...] + dy
        accx[...] = totx
        accy[...] = toty
        grad_x = 0.5 * (totx - 0.5 * dx)
        grad_y = 0.5 * (toty - 0.5 * dy)
        coriolis = jnp.broadcast_to(f_ref[...], (rows, width))
        to_ref[sub] = (centre[0] - time_step * parts[0][4] - biharmonic * parts[0][5]) * wet
        so_ref[sub] = (centre[1] - time_step * parts[1][4] - biharmonic * parts[1][5]) * wet
        uo_ref[sub] = (
            first + time_step * (coriolis * second - grad_x - parts[2][4]) - biharmonic * parts[2][5]
        ) * wet
        vo_ref[sub] = (
            second + time_step * (-coriolis * first - grad_y - parts[3][4]) - biharmonic * parts[3][5]
        ) * wet


def shards(axes, temp, salt, uvel, vvel, depth_levels):
    levels, rows_dev, cols_dev = temp.shape
    nlat = lax.axis_size("lat")
    nlon = lax.axis_size("lon")
    at_lat = lax.axis_index("lat")
    f32 = jnp.float32
    vmem = pl.BlockSpec(memory_space=pltpu.VMEM)
    strip = jax.ShapeDtypeStruct((4, levels, 2, cols_dev), f32)
    corners = jax.ShapeDtypeStruct((4, levels * 16 // cols_dev, 8, cols_dev), f32)
    hs, hn, hw, he, cor = pl.pallas_call(
        functools.partial(exchange_kernel, axes, nlat, nlon),
        out_shape=[strip] * 4 + [corners],
        in_specs=[pl.BlockSpec(memory_space=pl.ANY)] * 5,
        out_specs=[vmem] * 5,
        scratch_shapes=[pltpu.VMEM((4,) + temp.shape, f32),
                        pltpu.VMEM(depth_levels.shape, jnp.int32)]
        + [pltpu.VMEM(strip.shape, f32)] * 9
        + [pltpu.VMEM(corners.shape[1:], f32), pltpu.VMEM(corners.shape, f32)]
        + [pltpu.SemaphoreType.DMA((11,)), pltpu.SemaphoreType.DMA((11,)),
           pltpu.SemaphoreType.DMA((5,)), pltpu.SemaphoreType.DMA((2,))],
        compiler_params=pltpu.CompilerParams(collective_id=0, has_side_effects=True),
    )(temp, salt, uvel, vvel, depth_levels)

    total_rows = rows_dev * nlat
    global_rows = (at_lat * rows_dev + jnp.arange(rows_dev, dtype=jnp.int32)).astype(f32)
    coriolis = (0.5 * jnp.sin(math.pi * (global_rows + 0.5) / total_rows - 0.5 * math.pi))[:, None]

    frame = rows_dev + 2 * top
    per_step = cols_dev // 16
    level_block = pl.BlockSpec((per_step, rows_dev, cols_dev), lambda k: (k, 0, 0))
    plane = pl.BlockSpec((rows_dev, cols_dev), lambda k: (0, 0))
    column = pl.BlockSpec((rows_dev, 1), lambda k: (0, 0))
    out = pl.pallas_call(
        functools.partial(step_kernel, nlat),
        grid=(levels // per_step,),
        in_specs=[level_block] * 4 + [plane, column] + [vmem] * 5,
        out_specs=[level_block] * 4,
        out_shape=[jax.ShapeDtypeStruct(temp.shape, f32)] * 4,
        scratch_shapes=[pltpu.VMEM((4, frame, cols_dev), f32)] * 5
        + [pltpu.VMEM((rows_dev, cols_dev), f32)] * 2
        + [pltpu.VMEM((cols_dev, cols_dev), f32), pltpu.VMEM((frame, cols_dev), f32)],
        compiler_params=pltpu.CompilerParams(dimension_semantics=("arbitrary",)),
    )(temp, salt, uvel, vvel, depth_levels, coriolis, hs, hn, hw, he, cor)
    return tuple(out)


def solution(mesh):
    placed = (
        P(None, "lat", "lon"),
        P(None, "lat", "lon"),
        P(None, "lat", "lon"),
        P(None, "lat", "lon"),
        P("lat", "lon"),
    )
    return jax.shard_map(
        functools.partial(shards, tuple(mesh.axis_names)),
        mesh=mesh,
        in_specs=placed,
        out_specs=(
            P(None, "lat", "lon"),
            P(None, "lat", "lon"),
            P(None, "lat", "lon"),
            P(None, "lat", "lon"),
        ),
        check_vma=False,
    )
```

```python
import functools
import math

import jax
import jax.numpy as jnp
from jax import lax
from jax.experimental import pallas as pl
from jax.experimental.pallas import tpu as pltpu
from jax.sharding import PartitionSpec as P

time_step = 0.2
biharmonic = 0.01
signs = (1.0, 1.0, -1.0, -1.0)
top = 8


def when(cond, fn):
    if cond is True:
        fn()
    else:
        pl.when(cond)(fn)


def reverse_lanes(x):
    lane = lax.broadcasted_iota(jnp.int32, x.shape, 1)
    width = x.shape[1]
    bit = 1
    while bit < width:
        x = jnp.where((lane & bit) != 0, pltpu.roll(x, bit, 1), pltpu.roll(x, width - bit, 1))
        bit *= 2
    return x


def exchange_kernel(axes, nlat, nlon, t_hbm, s_hbm, u_hbm, v_hbm, d_hbm,
                    hs_o, hn_o, hw_o, he_o, cor_o,
                    xin, d_ref, top_b, bot_b, fold_b, lft_b, rgt_b, hs, hn, hw, he, csrc, cor,
                    send_sem, recv_sem, in_sem, local_sem):
    a = lax.axis_index("lat")
    b = lax.axis_index("lon")
    last = nlat - 1
    levels, rows, cols = t_hbm.shape
    left = (b + nlon - 1) % nlon
    right = (b + 1) % nlon
    mirror = nlon - 1 - b
    ne = (2 * nlon - 2 - b) % nlon
    nw = (nlon - b) % nlon
    fold = a == last
    loads = [pltpu.make_async_copy(src, xin.at[n], in_sem.at[n])
             for n, src in enumerate((t_hbm, s_hbm, u_hbm, v_hbm))]
    loads.append(pltpu.make_async_copy(d_hbm, d_ref, in_sem.at[4]))
    for copy in loads:
        copy.start()

    def dev(la, lo):
        return tuple(la if ax == "lat" else lo for ax in axes)

    def zero_south():
        hs[...] = jnp.zeros_like(hs)
        cor[0] = jnp.zeros_like(cor[0])
        cor[1] = jnp.zeros_like(cor[1])

    when(a == 0, zero_south)
    csrc[...] = jnp.zeros_like(csrc)

    partners = [
        (a < last, (a + 1, b)), (a > 0, (a - 1, b)), (True, (a, left)), (True, (a, right)),
        (a < last, (a + 1, right)), (a < last, (a + 1, left)),
        (a > 0, (a - 1, right)), (a > 0, (a - 1, left)),
        (fold, (last, mirror)), (fold & (ne != b), (last, ne)), (fold & (nw != b), (last, nw)),
    ]
    barrier = pltpu.get_barrier_semaphore()
    for cond, target in partners:
        when(cond, lambda target=target: pl.semaphore_signal(
            barrier, 1, device_id=dev(*target), device_id_type=pl.DeviceIdType.MESH))

    for copy in loads:
        copy.wait()

    def rows_body(k, carry):
        wet = jnp.where(d_ref[...] > k, 1.0, 0.0).astype(jnp.float32)
        for n in range(4):
            x = xin[n, k] * wet
            top_b[n, k] = x[0:2]
            bot_b[n, k] = x[rows - 2:rows]
            flipped = reverse_lanes(x[rows - 8:rows])
            fold_b[n, k, 0:1] = signs[n] * flipped[7:8]
            fold_b[n, k, 1:2] = signs[n] * flipped[6:7]
        return carry

    group = cols // 16

    def cols_body(g, carry):
        lane = lax.broadcasted_iota(jnp.int32, (rows, cols), 1)
        packed = jnp.zeros((rows, cols), jnp.float32)
        for kk in range(group):
            k = g * group + kk
            wet = jnp.where(d_ref[...] > k, 1.0, 0.0).astype(jnp.float32)
            for n in range(4):
                slot = 16 * kk + 4 * n
                x = xin[n, k] * wet
                packed = jnp.where((lane >= slot) & (lane < slot + 4),
                                   pltpu.roll(x, (slot + 2) % cols, 1), packed)
        pt = jnp.transpose(packed)
        csrc[g, 0:1] = packed[0:1]
        csrc[g, 1:2] = packed[rows - 1:rows]
        for kk in range(group):
            k = g * group + kk
            for n in range(4):
                slot = 16 * kk + 4 * n
                rgt_b[n, k] = pt[slot:slot + 2]
                lft_b[n, k] = pt[slot + 2:slot + 4]
        return carry

    lax.fori_loop(0, levels, rows_body, 0)

    below = (a + last) // (last + 1)
    above = (2 * last - a) // (last + 1)
    at_fold = a // last
    ne_apart = ((2 * b + 2) % nlon + nlon - 1) // nlon
    nw_apart = ((2 * b) % nlon + nlon - 1) // nlon
    peers = 2 + 3 * below + 3 * above + at_fold * (1 + ne_apart + nw_apart)
    pl.semaphore_wait(barrier, peers)

    relations = [
        (a < last, a > 0, bot_b, hs, (a + 1, b)),
        (a > 0, a < last, top_b, hn, (a - 1, b)),
        (fold, fold, fold_b, hn, (last, mirror)),
        (True, True, lft_b, he, (a, left)),
        (True, True, rgt_b, hw, (a, right)),
        (a < last, a > 0, csrc, cor.at[0], (a + 1, right)),
        (a < last, a > 0, csrc, cor.at[1], (a + 1, left)),
        (a > 0, a < last, csrc, cor.at[2], (a - 1, right)),
        (a > 0, a < last, csrc, cor.at[3], (a - 1, left)),
        (fold & (ne != b), fold & (ne != b), csrc, cor.at[3], (last, ne)),
        (fold & (nw != b), fold & (nw != b), csrc, cor.at[2], (last, nw)),
    ]
    copies = []
    for idx, (send, recv, src, dst, target) in enumerate(relations):
        if idx == 3:
            lax.fori_loop(0, levels // group, cols_body, 0)
        copy = pltpu.make_async_remote_copy(
            src_ref=src, dst_ref=dst, send_sem=send_sem.at[idx], recv_sem=recv_sem.at[idx],
            device_id=dev(*target), device_id_type=pl.DeviceIdType.MESH)
        copies.append((send, recv, copy))
        when(send, copy.start)
    own = [
        (fold & (ne == b), pltpu.make_async_copy(csrc, cor.at[3], local_sem.at[0])),
        (fold & (nw == b), pltpu.make_async_copy(csrc, cor.at[2], local_sem.at[1])),
    ]
    for cond, copy in own:
        when(cond, copy.start)
    for send, recv, copy in copies:
        when(send, copy.wait_send)
        when(recv, copy.wait_recv)
    for cond, copy in own:
        when(cond, copy.wait)
    hs_o[...] = hs[...]
    hn_o[...] = hn[...]
    hw_o[...] = hw[...]
    he_o[...] = he[...]
    cor_o[...] = cor[...]


def step_kernel(nlat, t_ref, s_ref, u_ref, v_ref, d_ref, f_ref, hs_ref, hn_ref, hw_ref, he_ref,
                cor_ref, to_ref, so_ref, uo_ref, vo_ref,
                base, vp1, vm1, vp2, vm2, accx, accy, mt, tf):
    step = pl.program_id(0)
    per_step = t_ref.shape[0]
    phases = (t_ref.shape[2] // 16) // per_step
    grp = step // phases
    phase = step % phases
    frame, width = base.shape[1], base.shape[2]
    rows = t_ref.shape[1]
    at_lat = lax.axis_index("lat")
    south = at_lat > 0
    fold = at_lat == nlat - 1

    @pl.when(step == 0)
    def _():
        base[...] = jnp.zeros_like(base)
        accx[...] = jnp.zeros_like(accx)
        accy[...] = jnp.zeros_like(accy)
        mt[...] = jnp.zeros_like(mt)
        tf[...] = jnp.zeros_like(tf)

    for sub in range(per_step):
        k = step * per_step + sub
        wet = jnp.where(d_ref[...] > k, 1.0, 0.0).astype(jnp.float32)
        lane = lax.broadcasted_iota(jnp.int32, (frame, width), 1)
        line_lane = lax.broadcasted_iota(jnp.int32, (1, width), 1)
        ins = (t_ref, s_ref, u_ref, v_ref)
        for n in range(4):
            base[n, top:top + rows, :] = ins[n][sub] * wet
            base[n, top - 2:top, :] = jnp.where(south, hs_ref[n, k], 0.0)
            base[n, top + rows:top + rows + 2, :] = hn_ref[n, k]
            mt[0:2] = he_ref[n, k]
            mt[width - 2:width] = hw_ref[n, k]
            tf[top:top + rows] = jnp.transpose(mt[...])
            def to_lane(kind, row, off, dst):
                line = cor_ref[kind, grp, row:row + 1]
                picked = None
                for ph in range(phases):
                    slot = 16 * (ph * per_step + sub) + 4 * n
                    moved = pltpu.roll(line, (dst - slot - off) % width, 1)
                    picked = moved if picked is None else jnp.where(phase == ph, moved, picked)
                return picked

            sw_line = to_lane(0, 1, 1, width - 1)
            se_line = to_lane(1, 1, 2, 0)
            nw_line = to_lane(2, 0, 1, width - 1)
            ne_line = to_lane(3, 0, 2, 0)
            nw_raw = to_lane(2, 1, 2, width - 1)
            ne_raw = to_lane(3, 1, 1, 0)
            low = jnp.where(line_lane == width - 1, sw_line, jnp.where(line_lane == 0, se_line, 0.0))
            high = jnp.where(line_lane == width - 1, nw_line, jnp.where(line_lane == 0, ne_line, 0.0))
            tf[top - 1:top] = jnp.where(south, low, 0.0)
            mirrored = jnp.where(line_lane == width - 1, nw_raw,
                                 jnp.where(line_lane == 0, ne_raw, 0.0))
            tf[top + rows:top + rows + 1] = jnp.where(fold, signs[n] * mirrored, high)
            whole = base[n]
            edge = tf[...]
            vp1[n] = pltpu.roll(jnp.where(lane == 0, edge, whole), width - 1, 1)
            vm1[n] = pltpu.roll(jnp.where(lane == width - 1, edge, whole), 1, 1)
            vp2[n] = pltpu.roll(jnp.where(lane < 2, edge, whole), width - 2, 1)
            vm2[n] = pltpu.roll(jnp.where(lane >= width - 2, edge, whole), 2, 1)

        def at(ref, n, d):
            return ref[n, top + d:top + d + rows, :]

        centre = [at(base, n, 0) for n in range(4)]
        first, second = centre[2], centre[3]
        parts = []
        for n in range(4):
            east, west = at(vp1, n, 0), at(vm1, n, 0)
            north, south_ = at(base, n, 1), at(base, n, -1)
            carried = 0.5 * (first * (east - west) + second * (north - south_))
            smooth = (
                20.0 * centre[n]
                - 8.0 * (east + west + north + south_)
                + 2.0 * (at(vp1, n, 1) + at(vp1, n, -1) + at(vm1, n, 1) + at(vm1, n, -1))
                + at(base, n, 2) + at(base, n, -2) + at(vp2, n, 0) + at(vm2, n, 0)
            )
            parts.append((east, west, north, south_, carried, smooth))

        def density(a, b):
            return -0.2 * a + 0.8 * b

        dx = density(parts[0][0], parts[1][0]) - density(parts[0][1], parts[1][1])
        dy = density(parts[0][2], parts[1][2]) - density(parts[0][3], parts[1][3])
        totx = accx[...] + dx
        toty = accy[...] + dy
        accx[...] = totx
        accy[...] = toty
        grad_x = 0.5 * (totx - 0.5 * dx)
        grad_y = 0.5 * (toty - 0.5 * dy)
        coriolis = jnp.broadcast_to(f_ref[...], (rows, width))
        to_ref[sub] = (centre[0] - time_step * parts[0][4] - biharmonic * parts[0][5]) * wet
        so_ref[sub] = (centre[1] - time_step * parts[1][4] - biharmonic * parts[1][5]) * wet
        uo_ref[sub] = (
            first + time_step * (coriolis * second - grad_x - parts[2][4]) - biharmonic * parts[2][5]
        ) * wet
        vo_ref[sub] = (
            second + time_step * (-coriolis * first - grad_y - parts[3][4]) - biharmonic * parts[3][5]
        ) * wet


def shards(axes, temp, salt, uvel, vvel, depth_levels):
    levels, rows_dev, cols_dev = temp.shape
    nlat = lax.axis_size("lat")
    nlon = lax.axis_size("lon")
    at_lat = lax.axis_index("lat")
    f32 = jnp.float32
    vmem = pl.BlockSpec(memory_space=pltpu.VMEM)
    strip = jax.ShapeDtypeStruct((4, levels, 2, cols_dev), f32)
    corners = jax.ShapeDtypeStruct((4, levels * 16 // cols_dev, 8, cols_dev), f32)
    hs, hn, hw, he, cor = pl.pallas_call(
        functools.partial(exchange_kernel, axes, nlat, nlon),
        out_shape=[strip] * 4 + [corners],
        in_specs=[pl.BlockSpec(memory_space=pl.ANY)] * 5,
        out_specs=[vmem] * 5,
        scratch_shapes=[pltpu.VMEM((4,) + temp.shape, f32),
                        pltpu.VMEM(depth_levels.shape, jnp.int32)]
        + [pltpu.VMEM(strip.shape, f32)] * 9
        + [pltpu.VMEM(corners.shape[1:], f32), pltpu.VMEM(corners.shape, f32)]
        + [pltpu.SemaphoreType.DMA((11,)), pltpu.SemaphoreType.DMA((11,)),
           pltpu.SemaphoreType.DMA((5,)), pltpu.SemaphoreType.DMA((2,))],
        compiler_params=pltpu.CompilerParams(collective_id=0, has_side_effects=True),
    )(temp, salt, uvel, vvel, depth_levels)

    total_rows = rows_dev * nlat
    global_rows = (at_lat * rows_dev + jnp.arange(rows_dev, dtype=jnp.int32)).astype(f32)
    coriolis = (0.5 * jnp.sin(math.pi * (global_rows + 0.5) / total_rows - 0.5 * math.pi))[:, None]

    frame = rows_dev + 2 * top
    per_step = 4
    level_block = pl.BlockSpec((per_step, rows_dev, cols_dev), lambda k: (k, 0, 0))
    plane = pl.BlockSpec((rows_dev, cols_dev), lambda k: (0, 0))
    column = pl.BlockSpec((rows_dev, 1), lambda k: (0, 0))
    out = pl.pallas_call(
        functools.partial(step_kernel, nlat),
        grid=(levels // per_step,),
        in_specs=[level_block] * 4 + [plane, column] + [vmem] * 5,
        out_specs=[level_block] * 4,
        out_shape=[jax.ShapeDtypeStruct(temp.shape, f32)] * 4,
        scratch_shapes=[pltpu.VMEM((4, frame, cols_dev), f32)] * 5
        + [pltpu.VMEM((rows_dev, cols_dev), f32)] * 2
        + [pltpu.VMEM((cols_dev, cols_dev), f32), pltpu.VMEM((frame, cols_dev), f32)],
        compiler_params=pltpu.CompilerParams(dimension_semantics=("arbitrary",)),
    )(temp, salt, uvel, vvel, depth_levels, coriolis, hs, hn, hw, he, cor)
    return tuple(out)


def solution(mesh):
    placed = (
        P(None, "lat", "lon"),
        P(None, "lat", "lon"),
        P(None, "lat", "lon"),
        P(None, "lat", "lon"),
        P("lat", "lon"),
    )
    return jax.shard_map(
        functools.partial(shards, tuple(mesh.axis_names)),
        mesh=mesh,
        in_specs=placed,
        out_specs=(
            P(None, "lat", "lon"),
            P(None, "lat", "lon"),
            P(None, "lat", "lon"),
            P(None, "lat", "lon"),
        ),
        check_vma=False,
    )
```

```python
import functools
import math

import jax
import jax.numpy as jnp
from jax import lax
from jax.experimental import pallas as pl
from jax.experimental.pallas import tpu as pltpu
from jax.sharding import PartitionSpec as P

time_step = 0.2
biharmonic = 0.01
signs = (1.0, 1.0, -1.0, -1.0)
top = 8


def when(cond, fn):
    if cond is True:
        fn()
    else:
        pl.when(cond)(fn)


def reverse_lanes(x):
    lane = lax.broadcasted_iota(jnp.int32, x.shape, 1)
    width = x.shape[1]
    bit = 1
    while bit < width:
        x = jnp.where((lane & bit) != 0, pltpu.roll(x, bit, 1), pltpu.roll(x, width - bit, 1))
        bit *= 2
    return x


def exchange_kernel(axes, nlat, nlon, t_hbm, s_hbm, u_hbm, v_hbm, d_hbm,
                    hs_o, hn_o, hw_o, he_o, cor_o,
                    xin, d_ref, top_b, bot_b, fold_b, lft_b, rgt_b, hs, hn, hw, he, csrc, cor,
                    send_sem, recv_sem, in_sem, local_sem):
    a = lax.axis_index("lat")
    b = lax.axis_index("lon")
    last = nlat - 1
    levels, rows, cols = t_hbm.shape
    left = (b + nlon - 1) % nlon
    right = (b + 1) % nlon
    mirror = nlon - 1 - b
    ne = (2 * nlon - 2 - b) % nlon
    nw = (nlon - b) % nlon
    fold = a == last
    srcs = (t_hbm, s_hbm, u_hbm, v_hbm)
    edges = [pltpu.make_async_copy(src.at[:, lo:lo + 8], xin.at[n, :, lo:lo + 8],
                                   in_sem.at[2 * n + i])
             for n, src in enumerate(srcs) for i, lo in enumerate((0, rows - 8))]
    edges.append(pltpu.make_async_copy(d_hbm, d_ref, in_sem.at[8]))
    middles = [pltpu.make_async_copy(src.at[:, 8:rows - 8], xin.at[n, :, 8:rows - 8],
                                     in_sem.at[9 + n]) for n, src in enumerate(srcs)]
    for copy in edges + middles:
        copy.start()

    def dev(la, lo):
        return tuple(la if ax == "lat" else lo for ax in axes)

    def zero_south():
        hs[...] = jnp.zeros_like(hs)
        cor[0] = jnp.zeros_like(cor[0])
        cor[1] = jnp.zeros_like(cor[1])

    when(a == 0, zero_south)
    csrc[...] = jnp.zeros_like(csrc)

    partners = [
        (a < last, (a + 1, b)), (a > 0, (a - 1, b)), (True, (a, left)), (True, (a, right)),
        (a < last, (a + 1, right)), (a < last, (a + 1, left)),
        (a > 0, (a - 1, right)), (a > 0, (a - 1, left)),
        (fold, (last, mirror)), (fold & (ne != b), (last, ne)), (fold & (nw != b), (last, nw)),
    ]
    barrier = pltpu.get_barrier_semaphore()
    for cond, target in partners:
        when(cond, lambda target=target: pl.semaphore_signal(
            barrier, 1, device_id=dev(*target), device_id_type=pl.DeviceIdType.MESH))

    for copy in edges:
        copy.wait()

    def rows_body(k, carry):
        wet = jnp.where(d_ref[...] > k, 1.0, 0.0).astype(jnp.float32)
        for n in range(4):
            x_top = xin[n, k, 0:8] * wet[0:8]
            x_bot = xin[n, k, rows - 8:rows] * wet[rows - 8:rows]
            top_b[n, k] = x_top[0:2]
            bot_b[n, k] = x_bot[6:8]
            flipped = reverse_lanes(x_bot)
            fold_b[n, k, 0:1] = signs[n] * flipped[7:8]
            fold_b[n, k, 1:2] = signs[n] * flipped[6:7]
        return carry

    group = cols // 16

    def cols_body(g, carry):
        lane = lax.broadcasted_iota(jnp.int32, (rows, cols), 1)
        packed = jnp.zeros((rows, cols), jnp.float32)
        for kk in range(group):
            k = g * group + kk
            wet = jnp.where(d_ref[...] > k, 1.0, 0.0).astype(jnp.float32)
            for n in range(4):
                slot = 16 * kk + 4 * n
                x = xin[n, k] * wet
                packed = jnp.where((lane >= slot) & (lane < slot + 4),
                                   pltpu.roll(x, (slot + 2) % cols, 1), packed)
        pt = jnp.transpose(packed)
        csrc[g, 0:1] = packed[0:1]
        csrc[g, 1:2] = packed[rows - 1:rows]
        for kk in range(group):
            k = g * group + kk
            for n in range(4):
                slot = 16 * kk + 4 * n
                rgt_b[n, k] = pt[slot:slot + 2]
                lft_b[n, k] = pt[slot + 2:slot + 4]
        return carry

    lax.fori_loop(0, levels, rows_body, 0)

    below = (a + last) // (last + 1)
    above = (2 * last - a) // (last + 1)
    at_fold = a // last
    ne_apart = ((2 * b + 2) % nlon + nlon - 1) // nlon
    nw_apart = ((2 * b) % nlon + nlon - 1) // nlon
    peers = 2 + 3 * below + 3 * above + at_fold * (1 + ne_apart + nw_apart)
    pl.semaphore_wait(barrier, peers)

    relations = [
        (a < last, a > 0, bot_b, hs, (a + 1, b)),
        (a > 0, a < last, top_b, hn, (a - 1, b)),
        (fold, fold, fold_b, hn, (last, mirror)),
        (True, True, lft_b, he, (a, left)),
        (True, True, rgt_b, hw, (a, right)),
        (a < last, a > 0, csrc, cor.at[0], (a + 1, right)),
        (a < last, a > 0, csrc, cor.at[1], (a + 1, left)),
        (a > 0, a < last, csrc, cor.at[2], (a - 1, right)),
        (a > 0, a < last, csrc, cor.at[3], (a - 1, left)),
        (fold & (ne != b), fold & (ne != b), csrc, cor.at[3], (last, ne)),
        (fold & (nw != b), fold & (nw != b), csrc, cor.at[2], (last, nw)),
    ]
    copies = []
    for idx, (send, recv, src, dst, target) in enumerate(relations):
        if idx == 3:
            for copy in middles:
                copy.wait()
            lax.fori_loop(0, levels // group, cols_body, 0)
        copy = pltpu.make_async_remote_copy(
            src_ref=src, dst_ref=dst, send_sem=send_sem.at[idx], recv_sem=recv_sem.at[idx],
            device_id=dev(*target), device_id_type=pl.DeviceIdType.MESH)
        copies.append((send, recv, copy))
        when(send, copy.start)
    own = [
        (fold & (ne == b), pltpu.make_async_copy(csrc, cor.at[3], local_sem.at[0])),
        (fold & (nw == b), pltpu.make_async_copy(csrc, cor.at[2], local_sem.at[1])),
    ]
    for cond, copy in own:
        when(cond, copy.start)
    for send, recv, copy in copies:
        when(send, copy.wait_send)
        when(recv, copy.wait_recv)
    for cond, copy in own:
        when(cond, copy.wait)
    hs_o[...] = hs[...]
    hn_o[...] = hn[...]
    hw_o[...] = hw[...]
    he_o[...] = he[...]
    cor_o[...] = cor[...]


def step_kernel(nlat, t_ref, s_ref, u_ref, v_ref, d_ref, f_ref, hs_ref, hn_ref, hw_ref, he_ref,
                cor_ref, to_ref, so_ref, uo_ref, vo_ref,
                base, vp1, vm1, vp2, vm2, accx, accy, mt, tf):
    step = pl.program_id(0)
    per_step = t_ref.shape[0]
    frame, width = base.shape[1], base.shape[2]
    rows = t_ref.shape[1]
    at_lat = lax.axis_index("lat")
    south = at_lat > 0
    fold = at_lat == nlat - 1

    @pl.when(step == 0)
    def _():
        base[...] = jnp.zeros_like(base)
        accx[...] = jnp.zeros_like(accx)
        accy[...] = jnp.zeros_like(accy)
        mt[...] = jnp.zeros_like(mt)
        tf[...] = jnp.zeros_like(tf)

    for sub in range(per_step):
        k = step * per_step + sub
        wet = jnp.where(d_ref[...] > k, 1.0, 0.0).astype(jnp.float32)
        lane = lax.broadcasted_iota(jnp.int32, (frame, width), 1)
        line_lane = lax.broadcasted_iota(jnp.int32, (1, width), 1)
        ins = (t_ref, s_ref, u_ref, v_ref)
        for n in range(4):
            base[n, top:top + rows, :] = ins[n][sub] * wet
            base[n, top - 2:top, :] = jnp.where(south, hs_ref[n, k], 0.0)
            base[n, top + rows:top + rows + 2, :] = hn_ref[n, k]
            mt[0:2] = he_ref[n, k]
            mt[width - 2:width] = hw_ref[n, k]
            tf[top:top + rows] = jnp.transpose(mt[...])
            slot = 16 * sub + 4 * n

            def to_lane(line, src, dst):
                return pltpu.roll(line, (dst - src) % width, 1)

            sw_line = to_lane(cor_ref[0, step, 1:2], slot + 1, width - 1)
            se_line = to_lane(cor_ref[1, step, 1:2], slot + 2, 0)
            nw_line = to_lane(cor_ref[2, step, 0:1], slot + 1, width - 1)
            ne_line = to_lane(cor_ref[3, step, 0:1], slot + 2, 0)
            nw_raw = to_lane(cor_ref[2, step, 1:2], slot + 2, width - 1)
            ne_raw = to_lane(cor_ref[3, step, 1:2], slot + 1, 0)
            low = jnp.where(line_lane == width - 1, sw_line, jnp.where(line_lane == 0, se_line, 0.0))
            high = jnp.where(line_lane == width - 1, nw_line, jnp.where(line_lane == 0, ne_line, 0.0))
            tf[top - 1:top] = jnp.where(south, low, 0.0)
            mirrored = jnp.where(line_lane == width - 1, nw_raw,
                                 jnp.where(line_lane == 0, ne_raw, 0.0))
            tf[top + rows:top + rows + 1] = jnp.where(fold, signs[n] * mirrored, high)
            whole = base[n]
            edge = tf[...]
            vp1[n] = pltpu.roll(jnp.where(lane == 0, edge, whole), width - 1, 1)
            vm1[n] = pltpu.roll(jnp.where(lane == width - 1, edge, whole), 1, 1)
            vp2[n] = pltpu.roll(jnp.where(lane < 2, edge, whole), width - 2, 1)
            vm2[n] = pltpu.roll(jnp.where(lane >= width - 2, edge, whole), 2, 1)

        def at(ref, n, d):
            return ref[n, top + d:top + d + rows, :]

        centre = [at(base, n, 0) for n in range(4)]
        first, second = centre[2], centre[3]
        parts = []
        for n in range(4):
            east, west = at(vp1, n, 0), at(vm1, n, 0)
            north, south_ = at(base, n, 1), at(base, n, -1)
            carried = 0.5 * (first * (east - west) + second * (north - south_))
            smooth = (
                20.0 * centre[n]
                - 8.0 * (east + west + north + south_)
                + 2.0 * (at(vp1, n, 1) + at(vp1, n, -1) + at(vm1, n, 1) + at(vm1, n, -1))
                + at(base, n, 2) + at(base, n, -2) + at(vp2, n, 0) + at(vm2, n, 0)
            )
            parts.append((east, west, north, south_, carried, smooth))

        def density(a, b):
            return -0.2 * a + 0.8 * b

        dx = density(parts[0][0], parts[1][0]) - density(parts[0][1], parts[1][1])
        dy = density(parts[0][2], parts[1][2]) - density(parts[0][3], parts[1][3])
        totx = accx[...] + dx
        toty = accy[...] + dy
        accx[...] = totx
        accy[...] = toty
        grad_x = 0.5 * (totx - 0.5 * dx)
        grad_y = 0.5 * (toty - 0.5 * dy)
        coriolis = jnp.broadcast_to(f_ref[...], (rows, width))
        to_ref[sub] = (centre[0] - time_step * parts[0][4] - biharmonic * parts[0][5]) * wet
        so_ref[sub] = (centre[1] - time_step * parts[1][4] - biharmonic * parts[1][5]) * wet
        uo_ref[sub] = (
            first + time_step * (coriolis * second - grad_x - parts[2][4]) - biharmonic * parts[2][5]
        ) * wet
        vo_ref[sub] = (
            second + time_step * (-coriolis * first - grad_y - parts[3][4]) - biharmonic * parts[3][5]
        ) * wet


def shards(axes, temp, salt, uvel, vvel, depth_levels):
    levels, rows_dev, cols_dev = temp.shape
    nlat = lax.axis_size("lat")
    nlon = lax.axis_size("lon")
    at_lat = lax.axis_index("lat")
    f32 = jnp.float32
    vmem = pl.BlockSpec(memory_space=pltpu.VMEM)
    strip = jax.ShapeDtypeStruct((4, levels, 2, cols_dev), f32)
    corners = jax.ShapeDtypeStruct((4, levels * 16 // cols_dev, 8, cols_dev), f32)
    hs, hn, hw, he, cor = pl.pallas_call(
        functools.partial(exchange_kernel, axes, nlat, nlon),
        out_shape=[strip] * 4 + [corners],
        in_specs=[pl.BlockSpec(memory_space=pl.ANY)] * 5,
        out_specs=[vmem] * 5,
        scratch_shapes=[pltpu.VMEM((4,) + temp.shape, f32),
                        pltpu.VMEM(depth_levels.shape, jnp.int32)]
        + [pltpu.VMEM(strip.shape, f32)] * 9
        + [pltpu.VMEM(corners.shape[1:], f32), pltpu.VMEM(corners.shape, f32)]
        + [pltpu.SemaphoreType.DMA((11,)), pltpu.SemaphoreType.DMA((11,)),
           pltpu.SemaphoreType.DMA((13,)), pltpu.SemaphoreType.DMA((2,))],
        compiler_params=pltpu.CompilerParams(collective_id=0, has_side_effects=True),
    )(temp, salt, uvel, vvel, depth_levels)

    total_rows = rows_dev * nlat
    global_rows = (at_lat * rows_dev + jnp.arange(rows_dev, dtype=jnp.int32)).astype(f32)
    coriolis = (0.5 * jnp.sin(math.pi * (global_rows + 0.5) / total_rows - 0.5 * math.pi))[:, None]

    frame = rows_dev + 2 * top
    per_step = cols_dev // 16
    level_block = pl.BlockSpec((per_step, rows_dev, cols_dev), lambda k: (k, 0, 0))
    plane = pl.BlockSpec((rows_dev, cols_dev), lambda k: (0, 0))
    column = pl.BlockSpec((rows_dev, 1), lambda k: (0, 0))
    out = pl.pallas_call(
        functools.partial(step_kernel, nlat),
        grid=(levels // per_step,),
        in_specs=[level_block] * 4 + [plane, column] + [vmem] * 5,
        out_specs=[level_block] * 4,
        out_shape=[jax.ShapeDtypeStruct(temp.shape, f32)] * 4,
        scratch_shapes=[pltpu.VMEM((4, frame, cols_dev), f32)] * 5
        + [pltpu.VMEM((rows_dev, cols_dev), f32)] * 2
        + [pltpu.VMEM((cols_dev, cols_dev), f32), pltpu.VMEM((frame, cols_dev), f32)],
        compiler_params=pltpu.CompilerParams(dimension_semantics=("arbitrary",)),
    )(temp, salt, uvel, vvel, depth_levels, coriolis, hs, hn, hw, he, cor)
    return tuple(out)


def solution(mesh):
    placed = (
        P(None, "lat", "lon"),
        P(None, "lat", "lon"),
        P(None, "lat", "lon"),
        P(None, "lat", "lon"),
        P("lat", "lon"),
    )
    return jax.shard_map(
        functools.partial(shards, tuple(mesh.axis_names)),
        mesh=mesh,
        in_specs=placed,
        out_specs=(
            P(None, "lat", "lon"),
            P(None, "lat", "lon"),
            P(None, "lat", "lon"),
            P(None, "lat", "lon"),
        ),
        check_vma=False,
    )
```

```python
import functools
import math

import jax
import jax.numpy as jnp
from jax import lax
from jax.experimental import pallas as pl
from jax.experimental.pallas import tpu as pltpu
from jax.sharding import PartitionSpec as P

time_step = 0.2
biharmonic = 0.01
signs = (1.0, 1.0, -1.0, -1.0)
top = 8


def when(cond, fn):
    if cond is True:
        fn()
    else:
        pl.when(cond)(fn)


def reverse_lanes(x):
    lane = lax.broadcasted_iota(jnp.int32, x.shape, 1)
    width = x.shape[1]
    bit = 1
    while bit < width:
        x = jnp.where((lane & bit) != 0, pltpu.roll(x, bit, 1), pltpu.roll(x, width - bit, 1))
        bit *= 2
    return x


def exchange_kernel(axes, nlat, nlon, t_hbm, s_hbm, u_hbm, v_hbm, d_hbm,
                    hs_o, hn_o, hw_o, he_o, cor_o,
                    xin, d_ref, top_b, bot_b, fold_b, lft_b, rgt_b, hs, hn, hw, he, csrc, cor,
                    send_sem, recv_sem, in_sem, local_sem):
    a = lax.axis_index("lat")
    b = lax.axis_index("lon")
    last = nlat - 1
    levels, rows, cols = t_hbm.shape
    left = (b + nlon - 1) % nlon
    right = (b + 1) % nlon
    mirror = nlon - 1 - b
    ne = (2 * nlon - 2 - b) % nlon
    nw = (nlon - b) % nlon
    fold = a == last
    srcs = (t_hbm, s_hbm, u_hbm, v_hbm)
    edges = [pltpu.make_async_copy(src.at[:, lo:lo + 8], xin.at[n, :, lo:lo + 8],
                                   in_sem.at[2 * n + i])
             for n, src in enumerate(srcs) for i, lo in enumerate((0, rows - 8))]
    edges.append(pltpu.make_async_copy(d_hbm, d_ref, in_sem.at[8]))
    middles = [pltpu.make_async_copy(src.at[:, 8:rows - 8], xin.at[n, :, 8:rows - 8],
                                     in_sem.at[9 + n]) for n, src in enumerate(srcs)]
    for copy in edges + middles:
        copy.start()

    def dev(la, lo):
        return tuple(la if ax == "lat" else lo for ax in axes)

    def zero_south():
        hs[...] = jnp.zeros_like(hs)
        cor[0] = jnp.zeros_like(cor[0])
        cor[1] = jnp.zeros_like(cor[1])

    when(a == 0, zero_south)
    csrc[...] = jnp.zeros_like(csrc)

    partners = [
        (a < last, (a + 1, b)), (a > 0, (a - 1, b)), (True, (a, left)), (True, (a, right)),
        (a < last, (a + 1, right)), (a < last, (a + 1, left)),
        (a > 0, (a - 1, right)), (a > 0, (a - 1, left)),
        (fold, (last, mirror)), (fold & (ne != b), (last, ne)), (fold & (nw != b), (last, nw)),
    ]
    barrier = pltpu.get_barrier_semaphore()
    for cond, target in partners:
        when(cond, lambda target=target: pl.semaphore_signal(
            barrier, 1, device_id=dev(*target), device_id_type=pl.DeviceIdType.MESH))

    for copy in edges:
        copy.wait()

    def rows_body(k, carry):
        wet = jnp.where(d_ref[...] > k, 1.0, 0.0).astype(jnp.float32)
        for n in range(4):
            x_top = xin[n, k, 0:8] * wet[0:8]
            x_bot = xin[n, k, rows - 8:rows] * wet[rows - 8:rows]
            top_b[n, k] = x_top[0:2]
            bot_b[n, k] = x_bot[6:8]
            flipped = reverse_lanes(x_bot)
            fold_b[n, k, 0:1] = signs[n] * flipped[7:8]
            fold_b[n, k, 1:2] = signs[n] * flipped[6:7]
        return carry

    group = cols // 16

    def cols_body(g, carry):
        lane = lax.broadcasted_iota(jnp.int32, (rows, cols), 1)
        packed = jnp.zeros((rows, cols), jnp.float32)
        for kk in range(group):
            k = g * group + kk
            wet = jnp.where(d_ref[...] > k, 1.0, 0.0).astype(jnp.float32)
            for n in range(4):
                slot = 16 * kk + 4 * n
                x = xin[n, k] * wet
                packed = jnp.where((lane >= slot) & (lane < slot + 4),
                                   pltpu.roll(x, (slot + 2) % cols, 1), packed)
        pt = jnp.transpose(packed)
        csrc[g, 0:1] = packed[0:1]
        csrc[g, 1:2] = packed[rows - 1:rows]
        for kk in range(group):
            k = g * group + kk
            for n in range(4):
                slot = 16 * kk + 4 * n
                rgt_b[n, k] = pt[slot:slot + 2]
                lft_b[n, k] = pt[slot + 2:slot + 4]
        return carry

    lax.fori_loop(0, levels, rows_body, 0)

    below = (a + last) // (last + 1)
    above = (2 * last - a) // (last + 1)
    at_fold = a // last
    ne_apart = ((2 * b + 2) % nlon + nlon - 1) // nlon
    nw_apart = ((2 * b) % nlon + nlon - 1) // nlon
    peers = 2 + 3 * below + 3 * above + at_fold * (1 + ne_apart + nw_apart)
    pl.semaphore_wait(barrier, peers)

    ngroups = levels // group
    rows_rel = [
        (a < last, a > 0, bot_b, hs, (a + 1, b)),
        (a > 0, a < last, top_b, hn, (a - 1, b)),
        (fold, fold, fold_b, hn, (last, mirror)),
    ]
    corner_rel = [
        (a < last, a > 0, csrc, cor.at[0], (a + 1, right)),
        (a < last, a > 0, csrc, cor.at[1], (a + 1, left)),
        (a > 0, a < last, csrc, cor.at[2], (a - 1, right)),
        (a > 0, a < last, csrc, cor.at[3], (a - 1, left)),
        (fold & (ne != b), fold & (ne != b), csrc, cor.at[3], (last, ne)),
        (fold & (nw != b), fold & (nw != b), csrc, cor.at[2], (last, nw)),
    ]
    copies = []

    def send_all(relations):
        for send, recv, src, dst, target in relations:
            idx = len(copies)
            copy = pltpu.make_async_remote_copy(
                src_ref=src, dst_ref=dst, send_sem=send_sem.at[idx], recv_sem=recv_sem.at[idx],
                device_id=dev(*target), device_id_type=pl.DeviceIdType.MESH)
            copies.append((send, recv, copy))
            when(send, copy.start)

    send_all(rows_rel)
    for copy in middles:
        copy.wait()
    for g in range(ngroups):
        cols_body(g, 0)
        span = slice(g * group, (g + 1) * group)
        send_all([
            (True, True, lft_b.at[:, span], he.at[:, span], (a, left)),
            (True, True, rgt_b.at[:, span], hw.at[:, span], (a, right)),
        ])
    send_all(corner_rel)
    own = [
        (fold & (ne == b), pltpu.make_async_copy(csrc, cor.at[3], local_sem.at[0])),
        (fold & (nw == b), pltpu.make_async_copy(csrc, cor.at[2], local_sem.at[1])),
    ]
    for cond, copy in own:
        when(cond, copy.start)
    for send, recv, copy in copies:
        when(send, copy.wait_send)
        when(recv, copy.wait_recv)
    for cond, copy in own:
        when(cond, copy.wait)
    hs_o[...] = hs[...]
    hn_o[...] = hn[...]
    hw_o[...] = hw[...]
    he_o[...] = he[...]
    cor_o[...] = cor[...]


def step_kernel(nlat, t_ref, s_ref, u_ref, v_ref, d_ref, f_ref, hs_ref, hn_ref, hw_ref, he_ref,
                cor_ref, to_ref, so_ref, uo_ref, vo_ref,
                base, vp1, vm1, vp2, vm2, accx, accy, mt, tf):
    step = pl.program_id(0)
    per_step = t_ref.shape[0]
    frame, width = base.shape[1], base.shape[2]
    rows = t_ref.shape[1]
    at_lat = lax.axis_index("lat")
    south = at_lat > 0
    fold = at_lat == nlat - 1

    @pl.when(step == 0)
    def _():
        base[...] = jnp.zeros_like(base)
        accx[...] = jnp.zeros_like(accx)
        accy[...] = jnp.zeros_like(accy)
        mt[...] = jnp.zeros_like(mt)
        tf[...] = jnp.zeros_like(tf)

    for sub in range(per_step):
        k = step * per_step + sub
        wet = jnp.where(d_ref[...] > k, 1.0, 0.0).astype(jnp.float32)
        lane = lax.broadcasted_iota(jnp.int32, (frame, width), 1)
        line_lane = lax.broadcasted_iota(jnp.int32, (1, width), 1)
        ins = (t_ref, s_ref, u_ref, v_ref)
        for n in range(4):
            base[n, top:top + rows, :] = ins[n][sub] * wet
            base[n, top - 2:top, :] = jnp.where(south, hs_ref[n, k], 0.0)
            base[n, top + rows:top + rows + 2, :] = hn_ref[n, k]
            mt[0:2] = he_ref[n, k]
            mt[width - 2:width] = hw_ref[n, k]
            tf[top:top + rows] = jnp.transpose(mt[...])
            slot = 16 * sub + 4 * n

            def to_lane(line, src, dst):
                return pltpu.roll(line, (dst - src) % width, 1)

            sw_line = to_lane(cor_ref[0, step, 1:2], slot + 1, width - 1)
            se_line = to_lane(cor_ref[1, step, 1:2], slot + 2, 0)
            nw_line = to_lane(cor_ref[2, step, 0:1], slot + 1, width - 1)
            ne_line = to_lane(cor_ref[3, step, 0:1], slot + 2, 0)
            nw_raw = to_lane(cor_ref[2, step, 1:2], slot + 2, width - 1)
            ne_raw = to_lane(cor_ref[3, step, 1:2], slot + 1, 0)
            low = jnp.where(line_lane == width - 1, sw_line, jnp.where(line_lane == 0, se_line, 0.0))
            high = jnp.where(line_lane == width - 1, nw_line, jnp.where(line_lane == 0, ne_line, 0.0))
            tf[top - 1:top] = jnp.where(south, low, 0.0)
            mirrored = jnp.where(line_lane == width - 1, nw_raw,
                                 jnp.where(line_lane == 0, ne_raw, 0.0))
            tf[top + rows:top + rows + 1] = jnp.where(fold, signs[n] * mirrored, high)
            whole = base[n]
            edge = tf[...]
            vp1[n] = pltpu.roll(jnp.where(lane == 0, edge, whole), width - 1, 1)
            vm1[n] = pltpu.roll(jnp.where(lane == width - 1, edge, whole), 1, 1)
            vp2[n] = pltpu.roll(jnp.where(lane < 2, edge, whole), width - 2, 1)
            vm2[n] = pltpu.roll(jnp.where(lane >= width - 2, edge, whole), 2, 1)

        def at(ref, n, d):
            return ref[n, top + d:top + d + rows, :]

        centre = [at(base, n, 0) for n in range(4)]
        first, second = centre[2], centre[3]
        parts = []
        for n in range(4):
            east, west = at(vp1, n, 0), at(vm1, n, 0)
            north, south_ = at(base, n, 1), at(base, n, -1)
            carried = 0.5 * (first * (east - west) + second * (north - south_))
            smooth = (
                20.0 * centre[n]
                - 8.0 * (east + west + north + south_)
                + 2.0 * (at(vp1, n, 1) + at(vp1, n, -1) + at(vm1, n, 1) + at(vm1, n, -1))
                + at(base, n, 2) + at(base, n, -2) + at(vp2, n, 0) + at(vm2, n, 0)
            )
            parts.append((east, west, north, south_, carried, smooth))

        def density(a, b):
            return -0.2 * a + 0.8 * b

        dx = density(parts[0][0], parts[1][0]) - density(parts[0][1], parts[1][1])
        dy = density(parts[0][2], parts[1][2]) - density(parts[0][3], parts[1][3])
        totx = accx[...] + dx
        toty = accy[...] + dy
        accx[...] = totx
        accy[...] = toty
        grad_x = 0.5 * (totx - 0.5 * dx)
        grad_y = 0.5 * (toty - 0.5 * dy)
        coriolis = jnp.broadcast_to(f_ref[...], (rows, width))
        to_ref[sub] = (centre[0] - time_step * parts[0][4] - biharmonic * parts[0][5]) * wet
        so_ref[sub] = (centre[1] - time_step * parts[1][4] - biharmonic * parts[1][5]) * wet
        uo_ref[sub] = (
            first + time_step * (coriolis * second - grad_x - parts[2][4]) - biharmonic * parts[2][5]
        ) * wet
        vo_ref[sub] = (
            second + time_step * (-coriolis * first - grad_y - parts[3][4]) - biharmonic * parts[3][5]
        ) * wet


def shards(axes, temp, salt, uvel, vvel, depth_levels):
    levels, rows_dev, cols_dev = temp.shape
    nlat = lax.axis_size("lat")
    nlon = lax.axis_size("lon")
    at_lat = lax.axis_index("lat")
    f32 = jnp.float32
    vmem = pl.BlockSpec(memory_space=pltpu.VMEM)
    strip = jax.ShapeDtypeStruct((4, levels, 2, cols_dev), f32)
    corners = jax.ShapeDtypeStruct((4, levels * 16 // cols_dev, 8, cols_dev), f32)
    hs, hn, hw, he, cor = pl.pallas_call(
        functools.partial(exchange_kernel, axes, nlat, nlon),
        out_shape=[strip] * 4 + [corners],
        in_specs=[pl.BlockSpec(memory_space=pl.ANY)] * 5,
        out_specs=[vmem] * 5,
        scratch_shapes=[pltpu.VMEM((4,) + temp.shape, f32),
                        pltpu.VMEM(depth_levels.shape, jnp.int32)]
        + [pltpu.VMEM(strip.shape, f32)] * 9
        + [pltpu.VMEM(corners.shape[1:], f32), pltpu.VMEM(corners.shape, f32)]
        + [pltpu.SemaphoreType.DMA((9 + levels * 32 // cols_dev,)),
           pltpu.SemaphoreType.DMA((9 + levels * 32 // cols_dev,)),
           pltpu.SemaphoreType.DMA((13,)), pltpu.SemaphoreType.DMA((2,))],
        compiler_params=pltpu.CompilerParams(collective_id=0, has_side_effects=True),
    )(temp, salt, uvel, vvel, depth_levels)

    total_rows = rows_dev * nlat
    global_rows = (at_lat * rows_dev + jnp.arange(rows_dev, dtype=jnp.int32)).astype(f32)
    coriolis = (0.5 * jnp.sin(math.pi * (global_rows + 0.5) / total_rows - 0.5 * math.pi))[:, None]

    frame = rows_dev + 2 * top
    per_step = cols_dev // 16
    level_block = pl.BlockSpec((per_step, rows_dev, cols_dev), lambda k: (k, 0, 0))
    plane = pl.BlockSpec((rows_dev, cols_dev), lambda k: (0, 0))
    column = pl.BlockSpec((rows_dev, 1), lambda k: (0, 0))
    out = pl.pallas_call(
        functools.partial(step_kernel, nlat),
        grid=(levels // per_step,),
        in_specs=[level_block] * 4 + [plane, column] + [vmem] * 5,
        out_specs=[level_block] * 4,
        out_shape=[jax.ShapeDtypeStruct(temp.shape, f32)] * 4,
        scratch_shapes=[pltpu.VMEM((4, frame, cols_dev), f32)] * 5
        + [pltpu.VMEM((rows_dev, cols_dev), f32)] * 2
        + [pltpu.VMEM((cols_dev, cols_dev), f32), pltpu.VMEM((frame, cols_dev), f32)],
        compiler_params=pltpu.CompilerParams(dimension_semantics=("arbitrary",)),
    )(temp, salt, uvel, vvel, depth_levels, coriolis, hs, hn, hw, he, cor)
    return tuple(out)


def solution(mesh):
    placed = (
        P(None, "lat", "lon"),
        P(None, "lat", "lon"),
        P(None, "lat", "lon"),
        P(None, "lat", "lon"),
        P("lat", "lon"),
    )
    return jax.shard_map(
        functools.partial(shards, tuple(mesh.axis_names)),
        mesh=mesh,
        in_specs=placed,
        out_specs=(
            P(None, "lat", "lon"),
            P(None, "lat", "lon"),
            P(None, "lat", "lon"),
            P(None, "lat", "lon"),
        ),
        check_vma=False,
    )
```

```python
import functools
import math

import jax
import jax.numpy as jnp
from jax import lax
from jax.experimental import pallas as pl
from jax.experimental.pallas import tpu as pltpu
from jax.sharding import PartitionSpec as P

time_step = 0.2
biharmonic = 0.01
signs = (1.0, 1.0, -1.0, -1.0)
top = 8


def when(cond, fn):
    if cond is True:
        fn()
    else:
        pl.when(cond)(fn)


def reverse_lanes(x):
    lane = lax.broadcasted_iota(jnp.int32, x.shape, 1)
    width = x.shape[1]
    bit = 1
    while bit < width:
        x = jnp.where((lane & bit) != 0, pltpu.roll(x, bit, 1), pltpu.roll(x, width - bit, 1))
        bit *= 2
    return x


def exchange_kernel(axes, nlat, nlon, t_hbm, s_hbm, u_hbm, v_hbm, d_hbm,
                    hs_o, hn_o, hw_o, he_o, cor_o,
                    xin, d_ref, top_b, bot_b, fold_b, lft_b, rgt_b, hs, hn, hw, he, csrc, cor,
                    send_sem, recv_sem, in_sem, local_sem):
    a = lax.axis_index("lat")
    b = lax.axis_index("lon")
    last = nlat - 1
    levels, rows, cols = t_hbm.shape
    left = (b + nlon - 1) % nlon
    right = (b + 1) % nlon
    mirror = nlon - 1 - b
    ne = (2 * nlon - 2 - b) % nlon
    nw = (nlon - b) % nlon
    fold = a == last
    srcs = (t_hbm, s_hbm, u_hbm, v_hbm)
    edges = [pltpu.make_async_copy(src.at[:, lo:lo + 8], xin.at[n, :, lo:lo + 8],
                                   in_sem.at[2 * n + i])
             for n, src in enumerate(srcs) for i, lo in enumerate((0, rows - 8))]
    edges.append(pltpu.make_async_copy(d_hbm, d_ref, in_sem.at[8]))
    middles = [pltpu.make_async_copy(src.at[:, 8:rows - 8], xin.at[n, :, 8:rows - 8],
                                     in_sem.at[9 + n]) for n, src in enumerate(srcs)]
    for copy in edges + middles:
        copy.start()

    def dev(la, lo):
        return tuple(la if ax == "lat" else lo for ax in axes)

    def zero_south():
        hs[...] = jnp.zeros_like(hs)
        cor[0] = jnp.zeros_like(cor[0])
        cor[1] = jnp.zeros_like(cor[1])

    when(a == 0, zero_south)
    csrc[...] = jnp.zeros_like(csrc)

    partners = [
        (a < last, (a + 1, b)), (a > 0, (a - 1, b)), (True, (a, left)), (True, (a, right)),
        (a < last, (a + 1, right)), (a < last, (a + 1, left)),
        (a > 0, (a - 1, right)), (a > 0, (a - 1, left)),
        (fold, (last, mirror)), (fold & (ne != b), (last, ne)), (fold & (nw != b), (last, nw)),
    ]
    barrier = pltpu.get_barrier_semaphore()
    for cond, target in partners:
        when(cond, lambda target=target: pl.semaphore_signal(
            barrier, 1, device_id=dev(*target), device_id_type=pl.DeviceIdType.MESH))

    for copy in edges:
        copy.wait()

    def rows_body(k, carry):
        wet = jnp.where(d_ref[...] > k, 1.0, 0.0).astype(jnp.float32)
        for n in range(4):
            x_top = xin[n, k, 0:8] * wet[0:8]
            x_bot = xin[n, k, rows - 8:rows] * wet[rows - 8:rows]
            top_b[n, k] = x_top[0:2]
            bot_b[n, k] = x_bot[6:8]
            flipped = reverse_lanes(x_bot)
            fold_b[n, k, 0:1] = signs[n] * flipped[7:8]
            fold_b[n, k, 1:2] = signs[n] * flipped[6:7]
        return carry

    group = cols // 16

    def cols_body(g, carry):
        lane = lax.broadcasted_iota(jnp.int32, (rows, cols), 1)
        packed = jnp.zeros((rows, cols), jnp.float32)
        for kk in range(group):
            k = g * group + kk
            wet = jnp.where(d_ref[...] > k, 1.0, 0.0).astype(jnp.float32)
            for n in range(4):
                slot = 16 * kk + 4 * n
                x = xin[n, k] * wet
                packed = jnp.where((lane >= slot) & (lane < slot + 4),
                                   pltpu.roll(x, (slot + 2) % cols, 1), packed)
        pt = jnp.transpose(packed)
        csrc[g, 0:1] = packed[0:1]
        csrc[g, 1:2] = packed[rows - 1:rows]
        for kk in range(group):
            k = g * group + kk
            for n in range(4):
                slot = 16 * kk + 4 * n
                rgt_b[n, k] = pt[slot:slot + 2]
                lft_b[n, k] = pt[slot + 2:slot + 4]
        return carry

    lax.fori_loop(0, levels, rows_body, 0)

    below = (a + last) // (last + 1)
    above = (2 * last - a) // (last + 1)
    at_fold = a // last
    ne_apart = ((2 * b + 2) % nlon + nlon - 1) // nlon
    nw_apart = ((2 * b) % nlon + nlon - 1) // nlon
    peers = 2 + 3 * below + 3 * above + at_fold * (1 + ne_apart + nw_apart)
    pl.semaphore_wait(barrier, peers)

    relations = [
        (a < last, a > 0, bot_b, hs, (a + 1, b)),
        (a > 0, a < last, top_b, hn, (a - 1, b)),
        (fold, fold, fold_b, hn, (last, mirror)),
        (True, True, lft_b, he, (a, left)),
        (True, True, rgt_b, hw, (a, right)),
        (a < last, a > 0, csrc, cor.at[0], (a + 1, right)),
        (a < last, a > 0, csrc, cor.at[1], (a + 1, left)),
        (a > 0, a < last, csrc, cor.at[2], (a - 1, right)),
        (a > 0, a < last, csrc, cor.at[3], (a - 1, left)),
        (fold & (ne != b), fold & (ne != b), csrc, cor.at[3], (last, ne)),
        (fold & (nw != b), fold & (nw != b), csrc, cor.at[2], (last, nw)),
    ]
    copies = []
    for idx, (send, recv, src, dst, target) in enumerate(relations):
        if idx == 3:
            for copy in middles:
                copy.wait()
            lax.fori_loop(0, levels // group, cols_body, 0)
        copy = pltpu.make_async_remote_copy(
            src_ref=src, dst_ref=dst, send_sem=send_sem.at[idx], recv_sem=recv_sem.at[idx],
            device_id=dev(*target), device_id_type=pl.DeviceIdType.MESH)
        copies.append((send, recv, copy))
        when(send, copy.start)
    own = [
        (fold & (ne == b), pltpu.make_async_copy(csrc, cor.at[3], local_sem.at[0])),
        (fold & (nw == b), pltpu.make_async_copy(csrc, cor.at[2], local_sem.at[1])),
    ]
    for cond, copy in own:
        when(cond, copy.start)
    for send, recv, copy in copies:
        when(send, copy.wait_send)
        when(recv, copy.wait_recv)
    for cond, copy in own:
        when(cond, copy.wait)
    hs_o[...] = hs[...]
    hn_o[...] = hn[...]
    hw_o[...] = hw[...]
    he_o[...] = he[...]
    cor_o[...] = cor[...]


def step_kernel(nlat, t_ref, s_ref, u_ref, v_ref, d_ref, f_ref, hs_ref, hn_ref, hw_ref, he_ref,
                cor_ref, to_ref, so_ref, uo_ref, vo_ref,
                base, vp1, vm1, vp2, vm2, accx, accy, mt, tf):
    step = pl.program_id(0)
    per_step = t_ref.shape[0]
    phases = (t_ref.shape[2] // 16) // per_step
    grp = step // phases
    phase = step % phases
    frame, width = base.shape[1], base.shape[2]
    rows = t_ref.shape[1]
    at_lat = lax.axis_index("lat")
    south = at_lat > 0
    fold = at_lat == nlat - 1

    @pl.when(step == 0)
    def _():
        base[...] = jnp.zeros_like(base)
        accx[...] = jnp.zeros_like(accx)
        accy[...] = jnp.zeros_like(accy)
        mt[...] = jnp.zeros_like(mt)
        tf[...] = jnp.zeros_like(tf)

    for sub in range(per_step):
        k = step * per_step + sub
        wet = jnp.where(d_ref[...] > k, 1.0, 0.0).astype(jnp.float32)
        lane = lax.broadcasted_iota(jnp.int32, (frame, width), 1)
        line_lane = lax.broadcasted_iota(jnp.int32, (1, width), 1)
        ins = (t_ref, s_ref, u_ref, v_ref)
        for n in range(4):
            base[n, top:top + rows, :] = ins[n][sub] * wet
            base[n, top - 2:top, :] = jnp.where(south, hs_ref[n, k], 0.0)
            base[n, top + rows:top + rows + 2, :] = hn_ref[n, k]
            mt[0:2] = he_ref[n, k]
            mt[width - 2:width] = hw_ref[n, k]
            tf[top:top + rows] = jnp.transpose(mt[...])
            def to_lane(kind, row, off, dst):
                line = cor_ref[kind, grp, row:row + 1]
                picked = None
                for ph in range(phases):
                    slot = 16 * (ph * per_step + sub) + 4 * n
                    moved = pltpu.roll(line, (dst - slot - off) % width, 1)
                    picked = moved if picked is None else jnp.where(phase == ph, moved, picked)
                return picked

            sw_line = to_lane(0, 1, 1, width - 1)
            se_line = to_lane(1, 1, 2, 0)
            nw_line = to_lane(2, 0, 1, width - 1)
            ne_line = to_lane(3, 0, 2, 0)
            nw_raw = to_lane(2, 1, 2, width - 1)
            ne_raw = to_lane(3, 1, 1, 0)
            low = jnp.where(line_lane == width - 1, sw_line, jnp.where(line_lane == 0, se_line, 0.0))
            high = jnp.where(line_lane == width - 1, nw_line, jnp.where(line_lane == 0, ne_line, 0.0))
            tf[top - 1:top] = jnp.where(south, low, 0.0)
            mirrored = jnp.where(line_lane == width - 1, nw_raw,
                                 jnp.where(line_lane == 0, ne_raw, 0.0))
            tf[top + rows:top + rows + 1] = jnp.where(fold, signs[n] * mirrored, high)
            whole = base[n]
            edge = tf[...]
            vp1[n] = pltpu.roll(jnp.where(lane == 0, edge, whole), width - 1, 1)
            vm1[n] = pltpu.roll(jnp.where(lane == width - 1, edge, whole), 1, 1)
            vp2[n] = pltpu.roll(jnp.where(lane < 2, edge, whole), width - 2, 1)
            vm2[n] = pltpu.roll(jnp.where(lane >= width - 2, edge, whole), 2, 1)

        def at(ref, n, d):
            return ref[n, top + d:top + d + rows, :]

        centre = [at(base, n, 0) for n in range(4)]
        first, second = centre[2], centre[3]
        parts = []
        for n in range(4):
            east, west = at(vp1, n, 0), at(vm1, n, 0)
            north, south_ = at(base, n, 1), at(base, n, -1)
            carried = 0.5 * (first * (east - west) + second * (north - south_))
            smooth = (
                20.0 * centre[n]
                - 8.0 * (east + west + north + south_)
                + 2.0 * (at(vp1, n, 1) + at(vp1, n, -1) + at(vm1, n, 1) + at(vm1, n, -1))
                + at(base, n, 2) + at(base, n, -2) + at(vp2, n, 0) + at(vm2, n, 0)
            )
            parts.append((east, west, north, south_, carried, smooth))

        def density(a, b):
            return -0.2 * a + 0.8 * b

        dx = density(parts[0][0], parts[1][0]) - density(parts[0][1], parts[1][1])
        dy = density(parts[0][2], parts[1][2]) - density(parts[0][3], parts[1][3])
        totx = accx[...] + dx
        toty = accy[...] + dy
        accx[...] = totx
        accy[...] = toty
        grad_x = 0.5 * (totx - 0.5 * dx)
        grad_y = 0.5 * (toty - 0.5 * dy)
        coriolis = jnp.broadcast_to(f_ref[...], (rows, width))
        to_ref[sub] = (centre[0] - time_step * parts[0][4] - biharmonic * parts[0][5]) * wet
        so_ref[sub] = (centre[1] - time_step * parts[1][4] - biharmonic * parts[1][5]) * wet
        uo_ref[sub] = (
            first + time_step * (coriolis * second - grad_x - parts[2][4]) - biharmonic * parts[2][5]
        ) * wet
        vo_ref[sub] = (
            second + time_step * (-coriolis * first - grad_y - parts[3][4]) - biharmonic * parts[3][5]
        ) * wet


def shards(axes, temp, salt, uvel, vvel, depth_levels):
    levels, rows_dev, cols_dev = temp.shape
    nlat = lax.axis_size("lat")
    nlon = lax.axis_size("lon")
    at_lat = lax.axis_index("lat")
    f32 = jnp.float32
    vmem = pl.BlockSpec(memory_space=pltpu.VMEM)
    strip = jax.ShapeDtypeStruct((4, levels, 2, cols_dev), f32)
    corners = jax.ShapeDtypeStruct((4, levels * 16 // cols_dev, 8, cols_dev), f32)
    hs, hn, hw, he, cor = pl.pallas_call(
        functools.partial(exchange_kernel, axes, nlat, nlon),
        out_shape=[strip] * 4 + [corners],
        in_specs=[pl.BlockSpec(memory_space=pl.ANY)] * 5,
        out_specs=[vmem] * 5,
        scratch_shapes=[pltpu.VMEM((4,) + temp.shape, f32),
                        pltpu.VMEM(depth_levels.shape, jnp.int32)]
        + [pltpu.VMEM(strip.shape, f32)] * 9
        + [pltpu.VMEM(corners.shape[1:], f32), pltpu.VMEM(corners.shape, f32)]
        + [pltpu.SemaphoreType.DMA((11,)), pltpu.SemaphoreType.DMA((11,)),
           pltpu.SemaphoreType.DMA((13,)), pltpu.SemaphoreType.DMA((2,))],
        compiler_params=pltpu.CompilerParams(collective_id=0, has_side_effects=True),
    )(temp, salt, uvel, vvel, depth_levels)

    total_rows = rows_dev * nlat
    global_rows = (at_lat * rows_dev + jnp.arange(rows_dev, dtype=jnp.int32)).astype(f32)
    coriolis = (0.5 * jnp.sin(math.pi * (global_rows + 0.5) / total_rows - 0.5 * math.pi))[:, None]

    frame = rows_dev + 2 * top
    per_step = 4
    level_block = pl.BlockSpec((per_step, rows_dev, cols_dev), lambda k: (k, 0, 0))
    plane = pl.BlockSpec((rows_dev, cols_dev), lambda k: (0, 0))
    column = pl.BlockSpec((rows_dev, 1), lambda k: (0, 0))
    out = pl.pallas_call(
        functools.partial(step_kernel, nlat),
        grid=(levels // per_step,),
        in_specs=[level_block] * 4 + [plane, column] + [vmem] * 5,
        out_specs=[level_block] * 4,
        out_shape=[jax.ShapeDtypeStruct(temp.shape, f32)] * 4,
        scratch_shapes=[pltpu.VMEM((4, frame, cols_dev), f32)] * 5
        + [pltpu.VMEM((rows_dev, cols_dev), f32)] * 2
        + [pltpu.VMEM((cols_dev, cols_dev), f32), pltpu.VMEM((frame, cols_dev), f32)],
        compiler_params=pltpu.CompilerParams(dimension_semantics=("arbitrary",)),
    )(temp, salt, uvel, vvel, depth_levels, coriolis, hs, hn, hw, he, cor)
    return tuple(out)


def solution(mesh):
    placed = (
        P(None, "lat", "lon"),
        P(None, "lat", "lon"),
        P(None, "lat", "lon"),
        P(None, "lat", "lon"),
        P("lat", "lon"),
    )
    return jax.shard_map(
        functools.partial(shards, tuple(mesh.axis_names)),
        mesh=mesh,
        in_specs=placed,
        out_specs=(
            P(None, "lat", "lon"),
            P(None, "lat", "lon"),
            P(None, "lat", "lon"),
            P(None, "lat", "lon"),
        ),
        check_vma=False,
    )
```
